128 devices in a mesh: seq: 16 (over y_lo, x, core), head: 8 (over z, y_hi).
Axes of the slice: x: 4, y: 4 (y_hi: 2, y_lo: 2; y = y_hi * 2 + y_lo), z: 4, core: 2. Of those that a mesh axis runs over, the one named last changes fastest.
Arguments:
- queries: bfloat16 [3072, 8192], P('seq', 'head'), may hold values from -1024 to 1024
- image_keys: bfloat16 [25616, 1024], P('seq', 'head'), may hold values from -8 to 8
- image_values: bfloat16 [25616, 1024], P('seq', 'head'), may hold values from -6 to 6
- layer_input: bfloat16 [3072, 8192], P('seq', 'head'), may hold values from -6 to 6
- out_weight: bfloat16 [8192, 8192], P('head'), may hold values from -0.09375 to 0.09375
- tile_counts: int32 [8], replicated, may hold values from 1 to 4, as said below
- image_range: int32 [2, 3072], P(None, 'seq'), may hold values from 0 to 8, as said below
- attn_gate: float32 [1], replicated, may hold values from 0.5 to 1.5
Outputs:
- layer_out: bfloat16 [3072, 8192], P('seq', 'head')
The draws below stay inside these ranges and needn't reach their ends.
Inputs may be any that keep to these rules, and one draw needn't show every extreme that they name: `tile_counts`: each image has 1 to 4 tiles and together they have 16; some image has exactly 4. Images are numbered in text order. For every token t, image_range[0, t] <= image_range[1, t]; image_range[1, t] never decreases as t grows; image_range[1, 0] = 0, so tokens before the first image attend to none.
All inputs are finite; a program needn't handle non-finite values.
Results may differ from the reference program's by a relative error of at most 0.0055.
Values may be sent and summed in bfloat16 or wider, within the bound.
No kernel may reach another device: no remote copies, remote signals or barrier semaphores. Data moves between devices by JAX's collectives and lax.ppermute only.
A program may use at most 512 MiB of HBM per device.

```python
import math
import jax
import jax.numpy as jnp
from jax import lax

D = 8192
HD = 128
GROUP = 8
TILE_TOK = 1601
TOK_DEV = 192
KVH = 8
HQ = 64
TEXT = 3072
TILES = 16
IMAGES = 8
IMG_TOK = 25616
N_SEQ = 16


def tile_plan(key):
    biggest = jax.random.randint(jax.random.fold_in(key, 31), (), 0, IMAGES)
    extra = TILES - IMAGES - 3
    slots = jax.random.permutation(jax.random.fold_in(key, 32), (IMAGES - 1) * 3)[:extra]
    others = 1 + jnp.sum((slots[None, :] // 3 == jnp.arange(IMAGES - 1, dtype=jnp.int32)[:, None]).astype(jnp.int32), axis=1)
    index = jnp.arange(IMAGES, dtype=jnp.int32)
    ranked = jnp.clip(index - (index > biggest).astype(jnp.int32), 0, IMAGES - 2)
    picked = jnp.sum(jnp.where(ranked[:, None] == jnp.arange(IMAGES - 1, dtype=jnp.int32)[None, :], others[None, :], 0), axis=1)
    return jnp.where(index == biggest, 4, picked).astype(jnp.int32)


def range_plan(key):
    picks = jax.random.permutation(jax.random.fold_in(key, 11), TEXT - 1)[:IMAGES] + 1
    starts = jnp.sort(picks).astype(jnp.int32)
    position = jnp.arange(TEXT, dtype=jnp.int32)
    high = jnp.sum((starts[None, :] <= position[:, None]).astype(jnp.int32), axis=1)
    spread = jax.random.randint(jax.random.fold_in(key, 12), (TEXT,), 0, 1 << 20)
    reach = jnp.maximum(jnp.minimum(high, 3), 1)
    low = jnp.maximum(high - 1 - spread % reach, 0)
    return jnp.stack([low, high]).astype(jnp.int32)


def drawn_pair(key):
    keys = jnp.clip(jax.random.normal(jax.random.fold_in(key, 21), (IMG_TOK, KVH * HD), jnp.float32), -6.0, 6.0)
    queries = jnp.clip(jax.random.normal(jax.random.fold_in(key, 22), (TEXT, HQ * HD), jnp.float32), -6.0, 6.0)
    return (queries, keys)


def draw_queries(key, part):
    return drawn_pair(key)[0].astype(jnp.bfloat16)


def draw_image_keys(key, part):
    return drawn_pair(key)[1].astype(jnp.bfloat16)


def draw_tile_counts(key, part):
    return tile_plan(key)


def draw_image_range(key, part):
    return range_plan(key)


def strengthened(drawn, key, source, target, blocks, factor):
    def block_of(dim):
        return (jnp.arange(drawn.shape[dim]) // (drawn.shape[dim] // blocks)).reshape((-1,) + (1,) * (drawn.ndim - 1 - dim))

    near = jax.random.permutation(key, blocks)[block_of(target)]
    second = (block_of(target) + blocks // 2) % blocks
    return jnp.where((block_of(source) == near) | (block_of(source) == second), factor * drawn, drawn)


def block_scale(rng, extent, cuts, least, high):
    level, own = 1.0, jax.random.fold_in(rng, 6)
    for axis_at, parts in cuts:
        heights = jnp.exp(jax.random.uniform(jax.random.fold_in(own, axis_at), (parts,), jnp.float32, least / len(cuts), high / len(cuts)))
        level = level * jnp.repeat(heights, extent[axis_at] // parts).reshape([-1 if axis == axis_at else 1 for axis in range(len(extent))])
    return level


def scatter_about(key, extent, deviation, bound, split=(), held_as=jnp.bfloat16):
    drawn = deviation * jax.random.normal(key, extent, jnp.float32)
    if split:
        drawn = drawn * block_scale(key, extent, split, -0.22, 0.18)
    return jnp.clip(drawn, -bound, bound).astype(held_as)


def bell_draw_with(key, dims, scale, limit, shards, heavy, kind=jnp.bfloat16):
    array = scale * jax.random.normal(key, dims, jnp.float32)
    if shards:
        array = array * block_scale(key, dims, shards, -0.22, 0.18)
    return jnp.clip(strengthened(array, jax.random.fold_in(key, 3), *heavy), -limit, limit).astype(kind)


def setup_inputs(seed: int = 0) -> dict:
    arg_keys = jax.random.split(jax.random.key(seed), 9)
    return {
        "queries": draw_queries(jax.random.fold_in(arg_keys[8], 71), 0),
        "image_keys": draw_image_keys(jax.random.fold_in(arg_keys[8], 71), 0),
        "image_values": scatter_about(arg_keys[2], (IMG_TOK, KVH * HD), 1.0, 6.0, ((0, 16), (1, 8))),
        "layer_input": scatter_about(arg_keys[3], (TEXT, D), 1.0, 6.0, ((0, 16), (1, 8))),
        "out_weight": bell_draw_with(arg_keys[4], (HQ * HD, D), (HQ * HD) ** -0.5, 0.09375, ((0, 8),), (0, 1, 8, 2.0)),
        "tile_counts": draw_tile_counts(jax.random.fold_in(arg_keys[8], 71), 0),
        "image_range": draw_image_range(jax.random.fold_in(arg_keys[8], 71), 0),
        "attn_gate": jnp.clip(jax.random.uniform(arg_keys[7], (1,), jnp.float32, 0.5, 1.5), 0.5, 1.5),
    }


def group_attention(item, key_image, low, high):
    q_group, k_group, v_group = item
    blocks = q_group.reshape(N_SEQ, TOK_DEV, GROUP, HD)
    lows = low.reshape(N_SEQ, TOK_DEV)
    highs = high.reshape(N_SEQ, TOK_DEV)

    def one_block(block_item):
        q_block, low_block, high_block = block_item
        scores = jnp.einsum('tgd,kd->tgk', q_block.astype(jnp.float32), k_group.astype(jnp.float32))
        scores = scores * (1.0 / math.sqrt(HD))
        allowed = (low_block[:, None] <= key_image[None, :]) & (key_image[None, :] < high_block[:, None])
        masked = jnp.where(allowed[:, None, :], scores, -jnp.inf)
        live = high_block > low_block
        top = jnp.where(live[:, None], lax.optimization_barrier(jnp.max(masked, axis=2)), 0.0)
        weights = jnp.exp(masked - top[:, :, None])
        total = lax.optimization_barrier(jnp.sum(weights, axis=2))
        numer = jnp.einsum('tgk,kd->tgd', weights.astype(jnp.bfloat16).astype(jnp.float32), v_group.astype(jnp.float32))
        safe_total = jnp.where(live[:, None], total, 1.0)
        result = jnp.where(live[:, None, None], numer / safe_total[:, :, None], 0.0)
        return result.astype(jnp.bfloat16)
    mapped = lax.map(one_block, (blocks, lows, highs))
    return mapped.reshape(TEXT, GROUP, HD)

def reference(queries, image_keys, image_values, layer_input, out_weight, tile_counts, image_range, attn_gate):
    ends = jnp.cumsum(tile_counts).astype(jnp.int32)
    tile = jnp.arange(IMG_TOK, dtype=jnp.int32) // TILE_TOK
    key_image = lax.optimization_barrier(jnp.sum((ends[None, :] <= tile[:, None]).astype(jnp.int32), axis=1))
    low = image_range[0]
    high = image_range[1]
    q_heads = jnp.transpose(queries.reshape(TEXT, KVH, GROUP, HD), (1, 0, 2, 3))
    k_heads = jnp.transpose(image_keys.reshape(IMG_TOK, KVH, HD), (1, 0, 2))
    v_heads = jnp.transpose(image_values.reshape(IMG_TOK, KVH, HD), (1, 0, 2))
    per_group = lax.map(lambda item: group_attention(item, key_image, low, high), (q_heads, k_heads, v_heads))
    attended = jnp.transpose(per_group, (1, 0, 2, 3)).reshape(TEXT, HQ * HD)
    projected = jnp.dot(attended, out_weight, preferred_element_type=jnp.float32)
    gate = jnp.tanh(attn_gate[0])
    return (layer_input.astype(jnp.float32) + gate * projected).astype(jnp.bfloat16)
```

```python
import math

import jax
import jax.numpy as jnp
from jax import lax
from jax.experimental import pallas as pl
from jax.experimental.pallas import tpu as pltpu
from jax.sharding import Mesh
from jax.sharding import PartitionSpec as P

SEQ = ("y", "x", "core")
HEAD = ("z", "yh")
CHUNK = 64
LOWEST = -1e30
BLOCKED = 1e30
BF16 = jnp.bfloat16
F32 = jnp.float32


def shifted(value, axis, steps):
    count = lax.axis_size(axis)
    return lax.ppermute(value, axis, [(s, (s + steps) % count) for s in range(count)])


def head_shifted(value, dz, dy):
    nz, ny = lax.axis_size("z"), lax.axis_size("yh")
    pairs = []
    for z in range(nz):
        for y in range(ny):
            pairs.append((z * ny + y, (z + dz) % nz * ny + (y + dy) % ny))
    return lax.ppermute(value, HEAD, pairs)


def attend_kernel(flags, images, q_ref, bounds_ref, *rest, scale, hd, group):
    kv_refs = rest[:4]
    out_ref, top_ref, acc_ref = rest[4:]
    step = pl.program_id(0)
    tokens = q_ref.shape[0]
    rows = tokens * group
    top_ref[...] = jnp.full(top_ref.shape, LOWEST, F32)
    acc_ref[...] = jnp.zeros(acc_ref.shape, F32)
    factor = scale * math.log2(math.e)
    low = jnp.concatenate([bounds_ref[:, 0:1]] * group, axis=0)
    high = jnp.concatenate([bounds_ref[:, 1:2]] * group, axis=0)
    for j in range(4):

        @pl.when(flags[step * 4 + j] > 0)
        def _():
            keys = kv_refs[j][:, :hd]
            count = keys.shape[0]
            values = jnp.concatenate([kv_refs[j][:, hd:], jnp.ones((count, hd), BF16)], axis=1)
            q = jnp.concatenate([q_ref[:, h * hd : (h + 1) * hd] for h in range(group)], axis=0)
            image = images[j]
            part = rows // 2
            for r in range(0, rows, part):
                at = pl.ds(r, part)
                scores = lax.dot_general(
                    q[r : r + part], keys, (((1,), (1,)), ((), ())), preferred_element_type=F32
                )
                allowed = (low[r : r + part] <= image) & (image < high[r : r + part])
                old = top_ref[at, 0:1]
                best = jnp.max(scores, axis=1, keepdims=True)
                new = jnp.where(allowed, jnp.maximum(old, best), old)
                anchor = jnp.where(allowed, new, BLOCKED)
                weights = jnp.exp2((scores - anchor) * factor).astype(BF16)
                rescale = jnp.exp2((old - new) * factor)
                mixed = jnp.dot(weights, values, preferred_element_type=F32)
                acc_ref[at, :] = acc_ref[at, :] * rescale + mixed
                top_ref[at, :] = jnp.broadcast_to(new, (part, hd))

    total = acc_ref[:, hd : hd + 1]
    seen = total > 0
    safe = jnp.where(seen, total, 1.0)
    mean = (acc_ref[:, :hd] / safe).astype(BF16)
    logsum = jnp.where(seen, top_ref[:, 0:1] * scale + jnp.log(safe), LOWEST)
    lane = lax.broadcasted_iota(jnp.int32, (tokens, hd), 1)
    spread = jnp.zeros((tokens, hd), F32)
    for h in range(group):
        at = slice(h * tokens, (h + 1) * tokens)
        out_ref[:, h * hd : (h + 1) * hd] = mean[at]
        hi = logsum[at].astype(BF16).astype(F32)
        mid = (logsum[at] - hi).astype(BF16).astype(F32)
        lo = logsum[at] - hi - mid
        spread = jnp.where(lane == h, hi, spread)
        spread = jnp.where(lane == h + group, mid, spread)
        spread = jnp.where(lane == h + 2 * group, lo, spread)
    out_ref[:, group * hd :] = spread.astype(BF16)


def attend(payload, bounds, flags, images, tiles, hd):
    tokens, width = bounds.shape[0], payload.shape[1]
    group = width // hd
    steps = tokens // CHUNK
    keys = tiles[0].shape[0]
    whole = pl.BlockSpec(tiles[0].shape, lambda c, *_: (0, 0), pipeline_mode=pl.Buffered(1))
    return pl.pallas_call(
        lambda *refs: attend_kernel(*refs, scale=1.0 / math.sqrt(hd), hd=hd, group=group),
        out_shape=jax.ShapeDtypeStruct((tokens, width + hd), BF16),
        grid_spec=pltpu.PrefetchScalarGridSpec(
            num_scalar_prefetch=2,
            grid=(steps,),
            in_specs=[
                pl.BlockSpec((CHUNK, width), lambda c, *_: (c, 0)),
                pl.BlockSpec((CHUNK, 2), lambda c, *_: (c, 0)),
            ]
            + [whole] * 4,
            out_specs=pl.BlockSpec((CHUNK, width + hd), lambda c, *_: (c, 0)),
            scratch_shapes=[
                pltpu.VMEM((CHUNK * group, hd), F32),
                pltpu.VMEM((CHUNK * group, 2 * hd), F32),
            ],
        ),
        compiler_params=pltpu.CompilerParams(vmem_limit_bytes=48 << 20),
        cost_estimate=pl.CostEstimate(
            flops=2 * tokens * group * keys * 4 * hd,
            bytes_accessed=tokens * width * 4 + keys * hd * 16,
            transcendentals=tokens * group * keys * 2,
        ),
        name="attend",
    )(flags, images, payload, bounds, *tiles)


def combine_kernel(a_ref, b_ref, c_ref, d_ref, out_ref, *, hd, group):
    parts = (a_ref, b_ref, c_ref, d_ref)
    width = group * hd
    sums = []
    for ref in parts:
        pieces = ref[:, width:].astype(F32)
        sums.append(pieces[:, :group] + pieces[:, group : 2 * group] + pieces[:, 2 * group : 3 * group])
    top = jnp.maximum(jnp.maximum(sums[0], sums[1]), jnp.maximum(sums[2], sums[3]))
    shares = [jnp.exp(s - top) for s in sums]
    total = shares[0] + shares[1] + shares[2] + shares[3]
    shares = [s / total for s in shares]
    for h in range(group):
        at = slice(h * hd, (h + 1) * hd)
        mixed = parts[0][:, at].astype(F32) * shares[0][:, h : h + 1]
        for ref, share in zip(parts[1:], shares[1:]):
            mixed = mixed + ref[:, at].astype(F32) * share[:, h : h + 1]
        out_ref[:, at] = mixed.astype(BF16)


def combine(parts, hd):
    tokens, wide = parts[0].shape
    width = wide - hd
    return pl.pallas_call(
        lambda *refs: combine_kernel(*refs, hd=hd, group=width // hd),
        out_shape=jax.ShapeDtypeStruct((tokens, width), BF16),
        cost_estimate=pl.CostEstimate(
            flops=8 * tokens * width, bytes_accessed=10 * tokens * width, transcendentals=tokens * 32
        ),
        compiler_params=pltpu.CompilerParams(vmem_limit_bytes=32 << 20),
        name="combine",
    )(*parts)


def project_kernel(block, a_ref, w_ref, out_ref):
    out_ref[...] = jnp.dot(a_ref[...], w_ref[...], preferred_element_type=F32).astype(BF16)


def project(attended, weight, block, width):
    tokens, depth = attended.shape
    cuts = 4
    step = width // cuts
    return pl.pallas_call(
        project_kernel,
        out_shape=jax.ShapeDtypeStruct((tokens, width), BF16),
        grid_spec=pltpu.PrefetchScalarGridSpec(
            num_scalar_prefetch=1,
            grid=(cuts,),
            in_specs=[
                pl.BlockSpec((tokens, depth), lambda g, b: (0, 0)),
                pl.BlockSpec((depth, step), lambda g, b: (0, b[0] * cuts + g)),
            ],
            out_specs=pl.BlockSpec((tokens, step), lambda g, b: (0, g)),
        ),
        cost_estimate=pl.CostEstimate(
            flops=2 * tokens * depth * width,
            bytes_accessed=2 * (depth * width + tokens * (depth + width)),
            transcendentals=0,
        ),
        compiler_params=pltpu.CompilerParams(vmem_limit_bytes=32 << 20),
        name="project",
    )(block.reshape(1), attended, weight)


def shards(
    queries, image_keys, image_values, layer_input, out_weight, tile_counts, image_range, attn_gate
):
    tokens, width = queries.shape
    hd = image_keys.shape[1]
    y, x, core = (lax.axis_index(n) for n in SEQ)
    z, yh = (lax.axis_index(n) for n in HEAD)
    nx, nc = lax.axis_size("x"), lax.axis_size("core")
    ny = lax.axis_size("y")
    nz, nyh = lax.axis_size("z"), lax.axis_size("yh")

    pair = jnp.concatenate([image_keys, image_values], axis=1)
    edge = jnp.pad(image_range.astype(BF16), ((0, 14), (0, width - tokens)))
    payload = jnp.concatenate([queries, edge], axis=0)
    across = shifted(pair, "y", 1)
    beside = shifted(pair, "core", 1)
    payloads = [payload] + [shifted(payload, "x", s) for s in (1, 2, 3)]
    diagonal = shifted(across, "core", 1)
    tiles = (pair, beside, across, diagonal)

    def number(yy, cc):
        return (yy % ny * nx + x) * nc + cc % nc

    held = jnp.stack([number(y, core), number(y, core + 1), number(y + 1, core), number(y + 1, core + 1)])
    order = jnp.arange(tile_counts.shape[0])
    ends = jnp.sum(jnp.where(order[None, :] <= order[:, None], tile_counts[None, :], 0), axis=1)
    images = jnp.sum((ends[None, :] <= held[:, None]).astype(jnp.int32), axis=1)

    returned = []
    for s in (2, 1, 3, 0):
        got = payloads[s]
        reach = got[tokens : tokens + 2, :tokens].astype(jnp.int32)
        low, high = reach[0], reach[1]
        hit = (low[:, None] <= images[None, :]) & (images[None, :] < high[:, None])
        flags = jnp.any(hit.reshape(tokens // CHUNK, CHUNK, 4), axis=1).astype(jnp.int32).reshape(-1)
        part = attend(got, reach.T, flags, images, tiles, hd)
        returned.append(part if s == 0 else shifted(part, "x", nx - s))
    attended = combine(returned, hd)

    total = None
    for dz, dy in ((2, 1), (1, 1), (3, 1), (2, 0), (0, 1), (1, 0), (3, 0), (0, 0)):
        block = (z + dz) % nz * nyh + (yh + dy) % nyh
        term = project(attended, out_weight, block, layer_input.shape[1])
        if (dz, dy) != (0, 0):
            term = head_shifted(term, dz, dy)
        term = term.astype(F32)
        total = term if total is None else total + term
    gate = jnp.tanh(attn_gate[0])
    return (layer_input.astype(F32) + gate * total).astype(BF16)


def solution(mesh):
    split = Mesh(mesh.devices.reshape(2, 4, 2, 4, 2), ("y", "x", "core", "z", "yh"))
    return jax.shard_map(
        shards,
        mesh=split,
        in_specs=(
            P(SEQ, HEAD),
            P(SEQ, HEAD),
            P(SEQ, HEAD),
            P(SEQ, HEAD),
            P(HEAD, None),
            P(),
            P(None, SEQ),
            P(),
        ),
        out_specs=P(SEQ, HEAD),
        check_vma=False,
    )
```

```python
import math

import jax
import jax.numpy as jnp
from jax import lax
from jax.experimental import pallas as pl
from jax.experimental.pallas import tpu as pltpu
from jax.sharding import Mesh
from jax.sharding import PartitionSpec as P

SEQ = ("y", "x", "core")
HEAD = ("z", "yh")
CHUNK = 32
LOWEST = -1e30
BLOCKED = 1e30
GROUPS = ((2, 1, 3, 0),)
BF16 = jnp.bfloat16
F32 = jnp.float32


def shifted(value, axis, steps):
    count = lax.axis_size(axis)
    return lax.ppermute(value, axis, [(s, (s + steps) % count) for s in range(count)])


def head_shifted(value, dz, dy):
    nz, ny = lax.axis_size("z"), lax.axis_size("yh")
    pairs = []
    for z in range(nz):
        for y in range(ny):
            pairs.append((z * ny + y, (z + dz) % nz * ny + (y + dy) % ny))
    return lax.ppermute(value, HEAD, pairs)


def attend_kernel(items, count, images, *refs, scale, hd, group, blocks, keys, padded):
    q_refs = refs[:blocks]
    bounds_ref = refs[blocks]
    key_refs = refs[blocks + 1 : blocks + 5]
    value_refs = refs[blocks + 5 : blocks + 9]
    out_refs = refs[blocks + 9 : 2 * blocks + 9]
    q_all, key_all, value_all, first_s, second_s, first_b, second_b, top_ref, acc_ref, sems = refs[
        2 * blocks + 9 :
    ]
    tokens = out_refs[0].shape[0]
    rows = CHUNK * group
    factor = scale * math.log2(math.e)
    copies = []
    for j in range(4):
        copies.append(pltpu.make_async_copy(key_refs[j], key_all.at[j], sems.at[2 * j]))
        copies.append(
            pltpu.make_async_copy(value_refs[j], value_all.at[j, :, pl.ds(0, hd)], sems.at[2 * j + 1])
        )
    for i in range(blocks):
        copies.append(
            pltpu.make_async_copy(
                q_refs[i].at[pl.ds(0, tokens)], q_all.at[pl.ds(i * tokens, tokens)], sems.at[8 + i]
            )
        )
    for copy in copies:
        copy.start()
    place = lax.broadcasted_iota(jnp.int32, (padded, hd), 0)
    ones = jnp.where(place < keys, 1.0, 0.0).astype(BF16)
    for j in range(4):
        value_all[j, :, hd:] = ones
    top_ref[...] = jnp.full(top_ref.shape, LOWEST, F32)
    acc_ref[...] = jnp.zeros(acc_ref.shape, F32)
    for copy in copies:
        copy.wait()

    def where_is(i):
        item = items[i]
        return item // 8, item % 4, jnp.where(item % 8 < 4, images[item % 4], -1)

    def score(i, scores_ref, best_ref):
        chunk, j, _ = where_is(i)
        at = pl.ds(pl.multiple_of(chunk * CHUNK, CHUNK), CHUNK)
        q = jnp.concatenate([q_all[at, h * hd : (h + 1) * hd] for h in range(group)], axis=0)
        best = None
        for k in range(0, padded, 128):
            part = jnp.dot(q, key_all[j, :, k : k + 128], preferred_element_type=F32)
            scores_ref[:, k : k + 128] = part
            best = part if best is None else jnp.maximum(best, part)
        best_ref[...] = jnp.broadcast_to(jnp.max(best, axis=1, keepdims=True), best_ref.shape)

    def absorb(i, scores_ref, best_ref):
        chunk, j, image = where_is(i)
        at = pl.ds(pl.multiple_of(chunk * rows, rows), rows)
        near = pl.ds(pl.multiple_of(chunk * CHUNK, CHUNK), CHUNK)
        low = jnp.concatenate([bounds_ref[near, 0:1]] * group, axis=0)
        high = jnp.concatenate([bounds_ref[near, 1:2]] * group, axis=0)
        allowed = (low <= image) & (image < high)
        old = top_ref[at, 0:1]
        new = jnp.where(allowed, jnp.maximum(old, best_ref[:, 0:1]), old)
        anchor = jnp.where(allowed, new, BLOCKED)
        rescale = jnp.exp2((old - new) * factor)
        top_ref[at, :] = jnp.broadcast_to(new, (rows, hd))
        weights = jnp.exp2((scores_ref[...] - anchor) * factor).astype(BF16)
        mixed = jnp.dot(weights, value_all[j], preferred_element_type=F32)
        acc_ref[at, :] = acc_ref[at, :] * rescale + mixed

    def pair(k, carry):
        i = 2 * k
        score(i + 1, second_s, second_b)
        absorb(i, first_s, first_b)
        score(i + 2, first_s, first_b)
        absorb(i + 1, second_s, second_b)
        return carry

    score(0, first_s, first_b)
    lax.fori_loop(0, (count[0] + 1) // 2, pair, 0)

    lane = lax.broadcasted_iota(jnp.int32, (CHUNK, hd), 1)
    for c in range(blocks * tokens // CHUNK):
        at = pl.ds(c * rows, rows)
        out_ref = out_refs[c * CHUNK // tokens]
        near = pl.ds(c * CHUNK % tokens, CHUNK)
        total = acc_ref[at, hd:]
        seen = total > 0
        safe = jnp.where(seen, total, 1.0)
        mean = (acc_ref[at, :hd] / safe).astype(BF16)
        logsum = jnp.where(seen, top_ref[at, :] * scale + jnp.log(safe), LOWEST)
        spread = jnp.zeros((CHUNK, hd), F32)
        for h in range(group):
            mine = slice(h * CHUNK, (h + 1) * CHUNK)
            out_ref[near, h * hd : (h + 1) * hd] = mean[mine]
            hi = logsum[mine].astype(BF16).astype(F32)
            mid = (logsum[mine] - hi).astype(BF16).astype(F32)
            lo = logsum[mine] - hi - mid
            spread = jnp.where(lane == h, hi, spread)
            spread = jnp.where(lane == h + group, mid, spread)
            spread = jnp.where(lane == h + 2 * group, lo, spread)
        out_ref[near, group * hd :] = spread.astype(BF16)


def attend(payloads, bounds, items, count, images, keys_t, values, keys, tokens):
    blocks = len(payloads)
    width = payloads[0].shape[1]
    hd, padded = keys_t[0].shape
    group = width // hd
    rows = CHUNK * group
    apart = pl.BlockSpec(memory_space=pl.ANY)
    here = pl.BlockSpec(memory_space=pltpu.VMEM)
    result = jax.ShapeDtypeStruct((tokens, width + hd), BF16)
    return pl.pallas_call(
        lambda *refs: attend_kernel(
            *refs, scale=1.0 / math.sqrt(hd), hd=hd, group=group, blocks=blocks, keys=keys, padded=padded
        ),
        out_shape=[result] * blocks,
        grid_spec=pltpu.PrefetchScalarGridSpec(
            num_scalar_prefetch=3,
            grid=(),
            in_specs=[apart] * blocks + [here] + [apart] * 8,
            out_specs=[here] * blocks,
            scratch_shapes=[
                pltpu.VMEM((blocks * tokens, width), BF16),
                pltpu.VMEM((4, hd, padded), BF16),
                pltpu.VMEM((4, padded, 2 * hd), BF16),
                pltpu.VMEM((rows, padded), F32),
                pltpu.VMEM((rows, padded), F32),
                pltpu.VMEM((rows, hd), F32),
                pltpu.VMEM((rows, hd), F32),
                pltpu.VMEM((blocks * tokens * group, hd), F32),
                pltpu.VMEM((blocks * tokens * group, 2 * hd), F32),
                pltpu.SemaphoreType.DMA((8 + blocks,)),
            ],
        ),
        compiler_params=pltpu.CompilerParams(vmem_limit_bytes=40 << 20),
        cost_estimate=pl.CostEstimate(
            flops=2 * blocks * tokens * group * padded * 2 * hd,
            bytes_accessed=blocks * tokens * width * 4 + padded * hd * 16,
            transcendentals=blocks * tokens * group * padded * 2,
        ),
        name="attend",
    )(items, count, images, *payloads, bounds, *keys_t, *values)


def work_list(hits, images):
    tokens, tiles = hits.shape
    flags = jnp.any(hits.reshape(tokens // CHUNK, CHUNK, tiles), axis=1).reshape(-1)
    size = flags.shape[0]
    place = jnp.arange(size, dtype=jnp.int32)
    rank = jnp.sum((place[None, :] < place[:, None]) & flags[None, :], axis=1)
    count = jnp.sum(flags.astype(jnp.int32))
    code = place // tiles * 8 + place % tiles + 1
    slot = jnp.arange(size + 3, dtype=jnp.int32)
    chosen = (rank[None, :] == slot[:, None]) & flags[None, :]
    items = jnp.sum(jnp.where(chosen, code[None, :], 0), axis=1)
    items = jnp.where(items > 0, items - 1, 4)
    return items.astype(jnp.int32), count.reshape(1)


def combine_kernel(order_ref, a_ref, b_ref, c_ref, d_ref, out_ref, *, hd, group):
    parts = (a_ref, b_ref, c_ref, d_ref)
    width = group * hd
    sums = []
    for ref in parts:
        pieces = ref[:, width:].astype(F32)
        sums.append(pieces[:, :group] + pieces[:, group : 2 * group] + pieces[:, 2 * group : 3 * group])
    top = jnp.maximum(jnp.maximum(sums[0], sums[1]), jnp.maximum(sums[2], sums[3]))
    shares = [jnp.exp(s - top) for s in sums]
    total = shares[0] + shares[1] + shares[2] + shares[3]
    shares = [s / total for s in shares]
    for h in range(group):
        at = slice(h * hd, (h + 1) * hd)
        mixed = parts[0][:, at].astype(F32) * shares[0][:, h : h + 1]
        for ref, share in zip(parts[1:], shares[1:]):
            mixed = mixed + ref[:, at].astype(F32) * share[:, h : h + 1]
        mixed = lax.dot_general(
            order_ref[...], mixed.astype(BF16), (((0,), (0,)), ((), ())), preferred_element_type=F32
        )
        out_ref[:, at] = mixed.astype(BF16)


def combine(order, parts, hd):
    tokens, wide = parts[0].shape
    width = wide - hd
    return pl.pallas_call(
        lambda *refs: combine_kernel(*refs, hd=hd, group=width // hd),
        out_shape=jax.ShapeDtypeStruct((tokens, width), BF16),
        cost_estimate=pl.CostEstimate(
            flops=8 * tokens * width, bytes_accessed=10 * tokens * width, transcendentals=tokens * 32
        ),
        compiler_params=pltpu.CompilerParams(vmem_limit_bytes=32 << 20),
        name="combine",
    )(order, *parts)


def project_kernel(block, a_ref, w_ref, out_ref):
    out_ref[...] = jnp.dot(a_ref[...], w_ref[...], preferred_element_type=F32).astype(BF16)


def project(attended, weight, block, width):
    tokens, depth = attended.shape
    cuts = 4
    step = width // cuts
    return pl.pallas_call(
        project_kernel,
        out_shape=jax.ShapeDtypeStruct((tokens, width), BF16),
        grid_spec=pltpu.PrefetchScalarGridSpec(
            num_scalar_prefetch=1,
            grid=(cuts,),
            in_specs=[
                pl.BlockSpec((tokens, depth), lambda g, b: (0, 0)),
                pl.BlockSpec((depth, step), lambda g, b: (0, b[0] * cuts + g)),
            ],
            out_specs=pl.BlockSpec((tokens, step), lambda g, b: (0, g)),
        ),
        cost_estimate=pl.CostEstimate(
            flops=2 * tokens * depth * width,
            bytes_accessed=2 * (depth * width + tokens * (depth + width)),
            transcendentals=0,
        ),
        compiler_params=pltpu.CompilerParams(vmem_limit_bytes=56 << 20),
        name="project",
    )(block.reshape(1), attended, weight)


def shards(
    queries, image_keys, image_values, layer_input, out_weight, tile_counts, image_range, attn_gate
):
    tokens, width = queries.shape
    hd = image_keys.shape[1]
    y, x, core = (lax.axis_index(n) for n in SEQ)
    z, yh = (lax.axis_index(n) for n in HEAD)
    nx, nc = lax.axis_size("x"), lax.axis_size("core")
    ny = lax.axis_size("y")
    nz, nyh = lax.axis_size("z"), lax.axis_size("yh")

    keys = image_keys.shape[0]
    padded = -(-keys // 128) * 128
    spare = jnp.broadcast_to(image_keys[:1], (padded - keys, hd))
    key_t = jnp.concatenate([image_keys, spare], axis=0).T
    value = jnp.pad(image_values, ((0, padded - keys), (0, 0)))
    own = (key_t, value)
    across = [shifted(v, "y", 1) for v in own]
    beside = [shifted(v, "core", 1) for v in own]

    low, high = image_range[0], image_range[1]
    grade = jnp.where(low < high, low * 16 + high, 1 << 10)
    place = jnp.arange(tokens, dtype=jnp.int32)
    ahead = (grade[None, :] < grade[:, None]) | (
        (grade[None, :] == grade[:, None]) & (place[None, :] < place[:, None])
    )
    rank = jnp.sum(ahead.astype(jnp.int32), axis=1)
    order = (rank[None, :] == place[:, None]).astype(BF16)
    sorted_q = jnp.dot(order, queries, preferred_element_type=F32).astype(BF16)
    sorted_range = jnp.dot(image_range.astype(BF16), order.T, preferred_element_type=F32).astype(BF16)
    edge = jnp.pad(sorted_range, ((0, 14), (0, width - tokens)))
    payload = jnp.concatenate([sorted_q, edge], axis=0)
    payloads = [payload] + [shifted(payload, "x", s) for s in (1, 2, 3)]
    diagonal = [shifted(v, "core", 1) for v in across]
    tiles = (own, beside, across, diagonal)

    def number(yy, cc):
        return (yy % ny * nx + x) * nc + cc % nc

    held = jnp.stack([number(y, core), number(y, core + 1), number(y + 1, core), number(y + 1, core + 1)])
    image = jnp.arange(tile_counts.shape[0])
    ends = jnp.sum(jnp.where(image[None, :] <= image[:, None], tile_counts[None, :], 0), axis=1)
    images = jnp.sum((ends[None, :] <= held[:, None]).astype(jnp.int32), axis=1)

    returned = []
    for turns in GROUPS:
        got = [payloads[s] for s in turns]
        reach = jnp.concatenate([p[tokens : tokens + 2, :tokens] for p in got], axis=1).astype(jnp.int32)
        hits = (reach[0][:, None] <= images[None, :]) & (images[None, :] < reach[1][:, None])
        items, count = work_list(hits, images)
        parts = attend(
            got, reach.T, items, count, images, [t[0] for t in tiles], [t[1] for t in tiles], keys, tokens
        )
        for s, part in zip(turns, parts):
            returned.append(part if s == 0 else shifted(part, "x", nx - s))
    attended = combine(order, returned, hd)

    total = None
    for dz, dy in ((2, 1), (1, 1), (3, 1), (2, 0), (0, 1), (1, 0), (3, 0), (0, 0)):
        block = (z + dz) % nz * nyh + (yh + dy) % nyh
        term = project(attended, out_weight, block, layer_input.shape[1])
        if (dz, dy) != (0, 0):
            term = head_shifted(term, dz, dy)
        term = term.astype(F32)
        total = term if total is None else total + term
    gate = jnp.tanh(attn_gate[0])
    return (layer_input.astype(F32) + gate * total).astype(BF16)


def solution(mesh):
    split = Mesh(mesh.devices.reshape(2, 4, 2, 4, 2), ("y", "x", "core", "z", "yh"))
    return jax.shard_map(
        shards,
        mesh=split,
        in_specs=(
            P(SEQ, HEAD),
            P(SEQ, HEAD),
            P(SEQ, HEAD),
            P(SEQ, HEAD),
            P(HEAD, None),
            P(),
            P(None, SEQ),
            P(),
        ),
        out_specs=P(SEQ, HEAD),
        check_vma=False,
    )
```

```python
import math

import jax
import jax.numpy as jnp
from jax import lax
from jax.experimental import pallas as pl
from jax.experimental.pallas import tpu as pltpu
from jax.sharding import Mesh
from jax.sharding import PartitionSpec as P

SEQ = ("y", "x", "core")
HEAD = ("z", "yh")
CHUNK = 32
HALVES = 2
LOWEST = -1e30
BLOCKED = 1e30
TURNS = (2, 1, 3, 0)
ROUTES = (((2, 1), (1, 1)), ((3, 1), (0, 1), (2, 0)), ((1, 0), (3, 0), (0, 0)))
BF16 = jnp.bfloat16
F32 = jnp.float32


def shifted(value, axis, steps):
    count = lax.axis_size(axis)
    return lax.ppermute(value, axis, [(s, (s + steps) % count) for s in range(count)])


def head_shifted(value, dz, dy):
    nz, ny = lax.axis_size("z"), lax.axis_size("yh")
    pairs = []
    for z in range(nz):
        for y in range(ny):
            pairs.append((z * ny + y, (z + dz) % nz * ny + (y + dy) % ny))
    return lax.ppermute(value, HEAD, pairs)


def attend_kernel(items, count, images, *refs, scale, hd, group, blocks, keys, padded, start):
    q_refs = refs[:blocks]
    key_refs = refs[blocks : blocks + 4]
    value_refs = refs[blocks + 4 : blocks + 8]
    out_refs = refs[blocks + 8 : 2 * blocks + 8]
    q_all, key_all, value_all, first_s, second_s, first_b, second_b, top_ref, acc_ref, sems = refs[
        2 * blocks + 8 :
    ]
    tokens = out_refs[0].shape[0]
    rows = CHUNK * group
    width = group * hd
    factor = scale * math.log2(math.e)
    copies = []
    for j in range(4):
        copies.append(pltpu.make_async_copy(key_refs[j], key_all.at[j], sems.at[2 * j]))
        copies.append(
            pltpu.make_async_copy(
                value_refs[j], value_all.at[j, :, pl.ds(0, hd)], sems.at[2 * j + 1]
            )
        )
    for i in range(blocks):
        copies.append(
            pltpu.make_async_copy(
                q_refs[i].at[pl.ds(start, tokens)], q_all.at[pl.ds(i * tokens, tokens)], sems.at[8 + i]
            )
        )
    for copy in copies:
        copy.start()
    place = lax.broadcasted_iota(jnp.int32, (padded, hd), 0)
    ones = jnp.where(place < keys, 1.0, 0.0).astype(BF16)
    for j in range(4):
        value_all[j, :, hd:] = ones
    top_ref[...] = jnp.full(top_ref.shape, LOWEST, F32)
    acc_ref[...] = jnp.zeros(acc_ref.shape, F32)
    for copy in copies:
        copy.wait()

    def where_is(i):
        item = items[i]
        return item // 8, item % 4, jnp.where(item % 8 < 4, images[item % 4], -1)

    def score(i, scores_ref, best_ref):
        chunk, j, _ = where_is(i)
        at = pl.ds(pl.multiple_of(chunk * CHUNK, CHUNK), CHUNK)
        q = jnp.concatenate([q_all[at, h * hd : (h + 1) * hd] for h in range(group)], axis=0)
        best = None
        for k in range(0, padded, 128):
            part = jnp.dot(q, key_all[j, :, k : k + 128], preferred_element_type=F32)
            scores_ref[:, k : k + 128] = part
            best = part if best is None else jnp.maximum(best, part)
        best_ref[...] = jnp.broadcast_to(jnp.max(best, axis=1, keepdims=True), best_ref.shape)

    def absorb(i, scores_ref, best_ref):
        chunk, j, image = where_is(i)
        at = pl.ds(pl.multiple_of(chunk * rows, rows), rows)
        near = pl.ds(pl.multiple_of(chunk * CHUNK, CHUNK), CHUNK)
        reach = q_all[near, width : width + hd].astype(F32)
        low = jnp.concatenate([reach[:, 0:1]] * group, axis=0)
        high = jnp.concatenate([reach[:, 1:2]] * group, axis=0)
        number = image.astype(F32)
        allowed = (low <= number) & (number < high)
        old = top_ref[at, 0:1]
        new = jnp.where(allowed, jnp.maximum(old, best_ref[:, 0:1]), old)
        anchor = jnp.where(allowed, new, BLOCKED)
        rescale = jnp.exp2((old - new) * factor)
        top_ref[at, :] = jnp.broadcast_to(new, (rows, hd))
        weights = jnp.exp2((scores_ref[...] - anchor) * factor).astype(BF16)
        mixed = jnp.dot(weights, value_all[j], preferred_element_type=F32)
        acc_ref[at, :] = acc_ref[at, :] * rescale + mixed

    def pair(k, carry):
        i = 2 * k
        score(i + 1, second_s, second_b)
        absorb(i, first_s, first_b)
        score(i + 2, first_s, first_b)
        absorb(i + 1, second_s, second_b)
        return carry

    score(0, first_s, first_b)
    lax.fori_loop(0, (count[0] + 1) // 2, pair, 0)

    lane = lax.broadcasted_iota(jnp.int32, (CHUNK, hd), 1)
    for c in range(blocks * tokens // CHUNK):
        out_ref = out_refs[c * CHUNK // tokens]
        near = pl.ds(c * CHUNK % tokens, CHUNK)
        totals = jnp.zeros((CHUNK, hd), F32)
        tops = jnp.zeros((CHUNK, hd), F32)
        for h in range(group):
            at = pl.ds(c * rows + h * CHUNK, CHUNK)
            total = acc_ref[at, hd:]
            safe = jnp.where(total > 0, total, 1.0)
            out_ref[near, h * hd : (h + 1) * hd] = (acc_ref[at, :hd] / safe).astype(BF16)
            totals = jnp.where(lane % group == h, total, totals)
            tops = jnp.where(lane % group == h, top_ref[at, :], tops)
        seen = totals > 0
        logsum = jnp.where(seen, tops * scale + jnp.log(jnp.where(seen, totals, 1.0)), LOWEST)
        hi = logsum.astype(BF16).astype(F32)
        mid = (logsum - hi).astype(BF16).astype(F32)
        lo = logsum - hi - mid
        pieces = jnp.where(lane < group, hi, jnp.where(lane < 2 * group, mid, lo))
        out_ref[near, width:] = pieces.astype(BF16)


def attend(payloads, items, count, images, keys_t, values, keys, tokens, start):
    blocks = len(payloads)
    wide = payloads[0].shape[1]
    hd, padded = keys_t[0].shape
    width = wide - hd
    group = width // hd
    rows = CHUNK * group
    apart = pl.BlockSpec(memory_space=pl.ANY)
    here = pl.BlockSpec(memory_space=pltpu.VMEM)
    return pl.pallas_call(
        lambda *refs: attend_kernel(
            *refs,
            scale=1.0 / math.sqrt(hd),
            hd=hd,
            group=group,
            blocks=blocks,
            keys=keys,
            padded=padded,
            start=start,
        ),
        out_shape=[jax.ShapeDtypeStruct((tokens, wide), BF16)] * blocks,
        grid_spec=pltpu.PrefetchScalarGridSpec(
            num_scalar_prefetch=3,
            grid=(),
            in_specs=[apart] * (blocks + 8),
            out_specs=[here] * blocks,
            scratch_shapes=[
                pltpu.VMEM((blocks * tokens, wide), BF16),
                pltpu.VMEM((4, hd, padded), BF16),
                pltpu.VMEM((4, padded, 2 * hd), BF16),
                pltpu.VMEM((rows, padded), F32),
                pltpu.VMEM((rows, padded), F32),
                pltpu.VMEM((rows, hd), F32),
                pltpu.VMEM((rows, hd), F32),
                pltpu.VMEM((blocks * tokens * group, hd), F32),
                pltpu.VMEM((blocks * tokens * group, 2 * hd), F32),
                pltpu.SemaphoreType.DMA((8 + blocks,)),
            ],
        ),
        compiler_params=pltpu.CompilerParams(vmem_limit_bytes=48 << 20),
        cost_estimate=pl.CostEstimate(
            flops=2 * blocks * tokens * group * padded * 2 * hd,
            bytes_accessed=blocks * tokens * width * 4 + padded * hd * 16,
            transcendentals=blocks * tokens * group * padded * 2,
        ),
        name="attend",
    )(items, count, images, *payloads, *keys_t, *values)


def work_list(hits):
    tokens, tiles = hits.shape
    flags = jnp.any(hits.reshape(tokens // CHUNK, CHUNK, tiles), axis=1).reshape(-1)
    size = flags.shape[0]
    place = jnp.arange(size, dtype=jnp.int32)
    rank = jnp.sum((place[None, :] < place[:, None]) & flags[None, :], axis=1)
    count = jnp.sum(flags.astype(jnp.int32))
    code = place // tiles * 8 + place % tiles + 1
    slot = jnp.arange(size + 3, dtype=jnp.int32)
    chosen = (rank[None, :] == slot[:, None]) & flags[None, :]
    items = jnp.sum(jnp.where(chosen, code[None, :], 0), axis=1)
    items = jnp.where(items > 0, items - 1, 4)
    return items.astype(jnp.int32), count.reshape(1)


def combined(parts, out_ref, hd, group):
    width = group * hd
    sums = []
    for ref in parts:
        pieces = ref[:, width:].astype(F32)
        sums.append(pieces[:, :group] + pieces[:, group : 2 * group] + pieces[:, 2 * group : 3 * group])
    top = jnp.maximum(jnp.maximum(sums[0], sums[1]), jnp.maximum(sums[2], sums[3]))
    shares = [jnp.exp(s - top) for s in sums]
    total = shares[0] + shares[1] + shares[2] + shares[3]
    shares = [s / total for s in shares]
    for h in range(group):
        at = slice(h * hd, (h + 1) * hd)
        mixed = parts[0][:, at].astype(F32) * shares[0][:, h : h + 1]
        for ref, share in zip(parts[1:], shares[1:]):
            mixed = mixed + ref[:, at].astype(F32) * share[:, h : h + 1]
        out_ref[:, at] = mixed.astype(BF16)


def project_kernel(columns, *refs, hd, group, wanted, merge):
    sources = refs[: 4 if merge else 1]
    w_ref = refs[len(sources)]
    outs = refs[len(sources) + 1 : len(sources) + 1 + wanted]
    held, sems = refs[-2:]
    depth, width = held.shape[1:]
    cuts = 2
    piece = depth // cuts
    copies = []
    for i in range(wanted):
        for c in range(cuts):
            at = pl.ds(c * piece, piece)
            copy = pltpu.make_async_copy(
                w_ref.at[at, pl.ds(pl.multiple_of(columns[i] * width, width), width)],
                held.at[i, at],
                sems.at[i * cuts + c],
            )
            copy.start()
            copies.append(copy)
    if merge:
        attended = refs[len(sources) + 1 + wanted]
        combined(sources, attended, hd, group)
    else:
        attended = sources[0]
    for i in range(wanted):
        for c in range(cuts):
            copies[i * cuts + c].wait()
        outs[i][...] = jnp.dot(attended[...], held[i], preferred_element_type=F32).astype(BF16)


def project(sources, weight, columns, width, hd):
    merge = len(sources) > 1
    tokens = sources[0].shape[0]
    depth = weight.shape[0]
    wanted = columns.shape[0]
    here = pl.BlockSpec(memory_space=pltpu.VMEM)
    results = [jax.ShapeDtypeStruct((tokens, width), BF16)] * wanted
    if merge:
        results.append(jax.ShapeDtypeStruct((tokens, depth), BF16))
    return pl.pallas_call(
        lambda *refs: project_kernel(*refs, hd=hd, group=depth // hd, wanted=wanted, merge=merge),
        out_shape=results,
        grid_spec=pltpu.PrefetchScalarGridSpec(
            num_scalar_prefetch=1,
            grid=(),
            in_specs=[here] * len(sources) + [pl.BlockSpec(memory_space=pl.ANY)],
            out_specs=[here] * len(results),
            scratch_shapes=[
                pltpu.VMEM((wanted, depth, width), BF16),
                pltpu.SemaphoreType.DMA((2 * wanted,)),
            ],
        ),
        cost_estimate=pl.CostEstimate(
            flops=2 * tokens * depth * width * wanted,
            bytes_accessed=2 * wanted * (depth * width + tokens * (depth + width)),
            transcendentals=0,
        ),
        compiler_params=pltpu.CompilerParams(vmem_limit_bytes=52 << 20),
        name="project",
    )(columns, *sources, weight)


def settle_kernel(gate_ref, order_ref, layer_ref, *refs):
    terms, out_ref = refs[:-1], refs[-1]
    each = len(terms) // HALVES
    tokens = order_ref.shape[0] // HALVES
    total = None
    for half in range(HALVES):
        order = order_ref[half * tokens : (half + 1) * tokens]
        for ref in terms[half * each : (half + 1) * each]:
            part = lax.dot_general(
                order, ref[...], (((0,), (0,)), ((), ())), preferred_element_type=F32
            )
            total = part if total is None else total + part
    out_ref[...] = (layer_ref[...].astype(F32) + gate_ref[0] * total).astype(BF16)


def settle(gate, order, layer, terms):
    tokens, width = layer.shape
    cuts = 4
    step = width // cuts
    tall = pl.BlockSpec((tokens, step), lambda g: (0, g))
    part = pl.BlockSpec((tokens // HALVES, step), lambda g: (0, g))
    return pl.pallas_call(
        settle_kernel,
        out_shape=jax.ShapeDtypeStruct((tokens, width), BF16),
        grid=(cuts,),
        in_specs=[
            pl.BlockSpec(memory_space=pltpu.SMEM),
            pl.BlockSpec((tokens, tokens), lambda g: (0, 0)),
            tall,
        ]
        + [part] * len(terms),
        out_specs=tall,
        compiler_params=pltpu.CompilerParams(vmem_limit_bytes=32 << 20),
        name="settle",
    )(gate, order, layer, *terms)


def shards(
    queries, image_keys, image_values, layer_input, out_weight, tile_counts, image_range, attn_gate
):
    tokens, width = queries.shape
    keys, hd = image_keys.shape
    y, x, core = (lax.axis_index(n) for n in SEQ)
    z, yh = (lax.axis_index(n) for n in HEAD)
    ny, nx, nc = (lax.axis_size(n) for n in SEQ)
    nz, nyh = (lax.axis_size(n) for n in HEAD)

    padded = -(-keys // 128) * 128
    spare = jnp.broadcast_to(image_keys[:1], (padded - keys, hd))
    key_t = jnp.concatenate([image_keys, spare], axis=0).T
    own = (key_t, jnp.pad(image_values, ((0, padded - keys), (0, 0))))
    across = [shifted(v, "y", 1) for v in own]
    beside = [shifted(v, "core", 1) for v in own]
    diagonal = [shifted(v, "core", 1) for v in across]
    tiles = (own, beside, across, diagonal)

    bounds, _ = lax.optimization_barrier((image_range, key_t))
    low, high = bounds[0], bounds[1]
    grade = jnp.where(low < high, low * 16 + high, 1 << 10)
    place = jnp.arange(tokens, dtype=jnp.int32)
    ahead = (grade[None, :] < grade[:, None]) | (
        (grade[None, :] == grade[:, None]) & (place[None, :] < place[:, None])
    )
    rank = jnp.sum(ahead.astype(jnp.int32), axis=1)
    order = (rank[None, :] == place[:, None]).astype(BF16)
    extra = jnp.pad(bounds.astype(BF16).T, ((0, 0), (0, hd - 2)))
    payload = jnp.dot(
        order, jnp.concatenate([queries, extra], axis=1), preferred_element_type=F32
    ).astype(BF16)
    payloads = [payload if s == 0 else shifted(payload, "x", s) for s in TURNS]

    def number(yy, cc):
        return (yy % ny * nx + x) * nc + cc % nc

    held = jnp.stack([number(y, core), number(y, core + 1), number(y + 1, core), number(y + 1, core + 1)])
    image = jnp.arange(tile_counts.shape[0])
    ends = jnp.sum(jnp.where(image[None, :] <= image[:, None], tile_counts[None, :], 0), axis=1)
    images = jnp.sum((ends[None, :] <= held[:, None]).astype(jnp.int32), axis=1)

    share = tokens // HALVES
    columns = [
        jnp.stack([(z + dz) % nz * nyh + (yh + dy) % nyh for dz, dy in some]).astype(jnp.int32)
        for some in ROUTES
    ]
    terms = []
    for half in range(HALVES):
        start = half * share
        reach = jnp.concatenate(
            [p[start : start + share, width : width + 2] for p in payloads], axis=0
        ).astype(jnp.int32)
        hits = (reach[:, :1] <= images[None, :]) & (images[None, :] < reach[:, 1:])
        items, count = work_list(hits)
        parts = attend(
            payloads, items, count, images, [t[0] for t in tiles], [t[1] for t in tiles], keys, share, start
        )
        parts = [p if s == 0 else shifted(p, "x", nx - s) for s, p in zip(TURNS, parts)]
        sources = parts
        for some, column in zip(ROUTES, columns):
            got = project(sources, out_weight, column, width, hd)
            if len(sources) > 1:
                sources = [got[-1]]
            for (dz, dy), term in zip(some, got):
                terms.append(term if (dz, dy) == (0, 0) else head_shifted(term, dz, dy))
    return settle(jnp.tanh(attn_gate), order, layer_input, terms)


def solution(mesh):
    split = Mesh(mesh.devices.reshape(2, 4, 2, 4, 2), ("y", "x", "core", "z", "yh"))
    return jax.shard_map(
        shards,
        mesh=split,
        in_specs=(
            P(SEQ, HEAD),
            P(SEQ, HEAD),
            P(SEQ, HEAD),
            P(SEQ, HEAD),
            P(HEAD, None),
            P(),
            P(None, SEQ),
            P(),
        ),
        out_specs=P(SEQ, HEAD),
        check_vma=False,
    )
```

```python
import math

import jax
import jax.numpy as jnp
from jax import lax
from jax.experimental import pallas as pl
from jax.experimental.pallas import tpu as pltpu
from jax.sharding import Mesh
from jax.sharding import PartitionSpec as P

SEQ = ("y", "x", "core")
HEAD = ("z", "yh")
CHUNK = 32
GROUPS = ((2, 1, 3, 0),)
LOWEST = -1e30
BLOCKED = 1e30
ROUTES = (((2, 1), (1, 1)), ((3, 1), (0, 1), (2, 0)), ((1, 0), (3, 0), (0, 0)))
BF16 = jnp.bfloat16
F32 = jnp.float32


def shifted(value, axis, steps):
    count = lax.axis_size(axis)
    return lax.ppermute(value, axis, [(s, (s + steps) % count) for s in range(count)])


def head_shifted(value, dz, dy):
    nz, ny = lax.axis_size("z"), lax.axis_size("yh")
    pairs = []
    for z in range(nz):
        for y in range(ny):
            pairs.append((z * ny + y, (z + dz) % nz * ny + (y + dy) % ny))
    return lax.ppermute(value, HEAD, pairs)


def attend_kernel(items, count, images, *refs, scale, hd, group, blocks, keys, padded):
    q_refs = refs[:blocks]
    key_refs = refs[blocks : blocks + 4]
    value_refs = refs[blocks + 4 : blocks + 8]
    out_refs = refs[blocks + 8 : 2 * blocks + 8]
    q_all, key_all, value_all, first_s, second_s, first_b, second_b, top_ref, acc_ref, sems = refs[
        2 * blocks + 8 :
    ]
    tokens = out_refs[0].shape[0]
    rows = CHUNK * group
    width = group * hd
    factor = scale * math.log2(math.e)
    copies = []
    for j in range(4):
        copies.append(pltpu.make_async_copy(key_refs[j], key_all.at[j], sems.at[2 * j]))
        copies.append(
            pltpu.make_async_copy(
                value_refs[j], value_all.at[j, :, pl.ds(0, hd)], sems.at[2 * j + 1]
            )
        )
    for i in range(blocks):
        copies.append(
            pltpu.make_async_copy(
                q_refs[i], q_all.at[pl.ds(i * tokens, tokens)], sems.at[8 + i]
            )
        )
    for copy in copies:
        copy.start()
    place = lax.broadcasted_iota(jnp.int32, (padded, hd), 0)
    ones = jnp.where(place < keys, 1.0, 0.0).astype(BF16)
    for j in range(4):
        value_all[j, :, hd:] = ones
    top_ref[...] = jnp.full(top_ref.shape, LOWEST, F32)
    acc_ref[...] = jnp.zeros(acc_ref.shape, F32)
    for copy in copies:
        copy.wait()

    def where_is(i):
        item = items[i]
        return item // 8, item % 4, jnp.where(item % 8 < 4, images[item % 4], -1)

    def score(i, scores_ref, best_ref):
        chunk, j, _ = where_is(i)
        at = pl.ds(pl.multiple_of(chunk * CHUNK, CHUNK), CHUNK)
        q = jnp.concatenate([q_all[at, h * hd : (h + 1) * hd] for h in range(group)], axis=0)
        best = None
        for k in range(0, padded, 128):
            part = jnp.dot(q, key_all[j, :, k : k + 128], preferred_element_type=F32)
            scores_ref[:, k : k + 128] = part
            best = part if best is None else jnp.maximum(best, part)
        best_ref[...] = jnp.broadcast_to(jnp.max(best, axis=1, keepdims=True), best_ref.shape)

    def absorb(i, scores_ref, best_ref):
        chunk, j, image = where_is(i)
        at = pl.ds(pl.multiple_of(chunk * rows, rows), rows)
        near = pl.ds(pl.multiple_of(chunk * CHUNK, CHUNK), CHUNK)
        reach = q_all[near, width : width + hd].astype(F32)
        low = jnp.concatenate([reach[:, 0:1]] * group, axis=0)
        high = jnp.concatenate([reach[:, 1:2]] * group, axis=0)
        number = image.astype(F32)
        allowed = (low <= number) & (number < high)
        old = top_ref[at, 0:1]
        new = jnp.where(allowed, jnp.maximum(old, best_ref[:, 0:1]), old)
        anchor = jnp.where(allowed, new, BLOCKED)
        rescale = jnp.exp2((old - new) * factor)
        top_ref[at, :] = jnp.broadcast_to(new, (rows, hd))
        weights = jnp.exp2((scores_ref[...] - anchor) * factor).astype(BF16)
        mixed = jnp.dot(weights, value_all[j], preferred_element_type=F32)
        acc_ref[at, :] = acc_ref[at, :] * rescale + mixed

    def pair(k, carry):
        i = 2 * k
        score(i + 1, second_s, second_b)
        absorb(i, first_s, first_b)
        score(i + 2, first_s, first_b)
        absorb(i + 1, second_s, second_b)
        return carry

    score(0, first_s, first_b)
    lax.fori_loop(0, (count[0] + 1) // 2, pair, 0)

    lane = lax.broadcasted_iota(jnp.int32, (CHUNK, hd), 1)
    for c in range(blocks * tokens // CHUNK):
        out_ref = out_refs[c * CHUNK // tokens]
        near = pl.ds(c * CHUNK % tokens, CHUNK)
        totals = jnp.zeros((CHUNK, hd), F32)
        tops = jnp.zeros((CHUNK, hd), F32)
        for h in range(group):
            at = pl.ds(c * rows + h * CHUNK, CHUNK)
            total = acc_ref[at, hd:]
            safe = jnp.where(total > 0, total, 1.0)
            out_ref[near, h * hd : (h + 1) * hd] = (acc_ref[at, :hd] / safe).astype(BF16)
            totals = jnp.where(lane % group == h, total, totals)
            tops = jnp.where(lane % group == h, top_ref[at, :], tops)
        seen = totals > 0
        logsum = jnp.where(seen, tops * scale + jnp.log(jnp.where(seen, totals, 1.0)), LOWEST)
        hi = logsum.astype(BF16).astype(F32)
        mid = (logsum - hi).astype(BF16).astype(F32)
        lo = logsum - hi - mid
        pieces = jnp.where(lane < group, hi, jnp.where(lane < 2 * group, mid, lo))
        out_ref[near, width:] = pieces.astype(BF16)


def attend(payloads, items, count, images, keys_t, values, keys, tokens):
    blocks = len(payloads)
    wide = payloads[0].shape[1]
    hd, padded = keys_t[0].shape
    width = wide - hd
    group = width // hd
    rows = CHUNK * group
    apart = pl.BlockSpec(memory_space=pl.ANY)
    here = pl.BlockSpec(memory_space=pltpu.VMEM)
    return pl.pallas_call(
        lambda *refs: attend_kernel(
            *refs,
            scale=1.0 / math.sqrt(hd),
            hd=hd,
            group=group,
            blocks=blocks,
            keys=keys,
            padded=padded,
        ),
        out_shape=[jax.ShapeDtypeStruct((tokens, wide), BF16)] * blocks,
        grid_spec=pltpu.PrefetchScalarGridSpec(
            num_scalar_prefetch=3,
            grid=(),
            in_specs=[apart] * (blocks + 8),
            out_specs=[here] * blocks,
            scratch_shapes=[
                pltpu.VMEM((blocks * tokens, wide), BF16),
                pltpu.VMEM((4, hd, padded), BF16),
                pltpu.VMEM((4, padded, 2 * hd), BF16),
                pltpu.VMEM((rows, padded), F32),
                pltpu.VMEM((rows, padded), F32),
                pltpu.VMEM((rows, hd), F32),
                pltpu.VMEM((rows, hd), F32),
                pltpu.VMEM((blocks * tokens * group, hd), F32),
                pltpu.VMEM((blocks * tokens * group, 2 * hd), F32),
                pltpu.SemaphoreType.DMA((8 + blocks,)),
            ],
        ),
        compiler_params=pltpu.CompilerParams(vmem_limit_bytes=32 << 20),
        cost_estimate=pl.CostEstimate(
            flops=2 * blocks * tokens * group * padded * 2 * hd,
            bytes_accessed=blocks * tokens * width * 4 + padded * hd * 16,
            transcendentals=blocks * tokens * group * padded * 2,
        ),
        name="attend",
    )(items, count, images, *payloads, *keys_t, *values)


def work_list(wanted):
    tiles = wanted.shape[-1]
    flags = wanted.reshape(-1) > 0
    size = flags.shape[0]
    place = jnp.arange(size, dtype=jnp.int32)
    rank = jnp.sum((place[None, :] < place[:, None]) & flags[None, :], axis=1)
    count = jnp.sum(flags.astype(jnp.int32))
    code = place // tiles * 8 + place % tiles + 1
    slot = jnp.arange(size + 3, dtype=jnp.int32)
    chosen = (rank[None, :] == slot[:, None]) & flags[None, :]
    items = jnp.sum(jnp.where(chosen, code[None, :], 0), axis=1)
    items = jnp.where(items > 0, items - 1, 4)
    return items.astype(jnp.int32), count.reshape(1)


def combined(parts, out_ref, hd, group):
    width = group * hd
    sums = []
    for ref in parts:
        pieces = ref[:, width:].astype(F32)
        sums.append(pieces[:, :group] + pieces[:, group : 2 * group] + pieces[:, 2 * group : 3 * group])
    top = jnp.maximum(jnp.maximum(sums[0], sums[1]), jnp.maximum(sums[2], sums[3]))
    shares = [jnp.exp(s - top) for s in sums]
    total = shares[0] + shares[1] + shares[2] + shares[3]
    shares = [s / total for s in shares]
    for h in range(group):
        at = slice(h * hd, (h + 1) * hd)
        mixed = parts[0][:, at].astype(F32) * shares[0][:, h : h + 1]
        for ref, share in zip(parts[1:], shares[1:]):
            mixed = mixed + ref[:, at].astype(F32) * share[:, h : h + 1]
        out_ref[:, at] = mixed.astype(BF16)


def project_kernel(columns, *refs, hd, group, wanted, merge):
    sources = refs[: 4 if merge else 1]
    w_ref = refs[len(sources)]
    outs = refs[len(sources) + 1 : len(sources) + 1 + wanted]
    held, sems = refs[-2:]
    depth, width = held.shape[1:]
    cuts = 2
    piece = depth // cuts
    copies = []
    for i in range(wanted):
        for c in range(cuts):
            at = pl.ds(c * piece, piece)
            copy = pltpu.make_async_copy(
                w_ref.at[at, pl.ds(pl.multiple_of(columns[i] * width, width), width)],
                held.at[i, at],
                sems.at[i * cuts + c],
            )
            copy.start()
            copies.append(copy)
    if merge:
        attended = refs[len(sources) + 1 + wanted]
        combined(sources, attended, hd, group)
    else:
        attended = sources[0]
    for i in range(wanted):
        for c in range(cuts):
            copies[i * cuts + c].wait()
        outs[i][...] = jnp.dot(attended[...], held[i], preferred_element_type=F32).astype(BF16)


def project(sources, weight, columns, width, hd):
    merge = len(sources) > 1
    tokens = sources[0].shape[0]
    depth = weight.shape[0]
    wanted = columns.shape[0]
    here = pl.BlockSpec(memory_space=pltpu.VMEM)
    results = [jax.ShapeDtypeStruct((tokens, width), BF16)] * wanted
    if merge:
        results.append(jax.ShapeDtypeStruct((tokens, depth), BF16))
    return pl.pallas_call(
        lambda *refs: project_kernel(*refs, hd=hd, group=depth // hd, wanted=wanted, merge=merge),
        out_shape=results,
        grid_spec=pltpu.PrefetchScalarGridSpec(
            num_scalar_prefetch=1,
            grid=(),
            in_specs=[here] * len(sources) + [pl.BlockSpec(memory_space=pl.ANY)],
            out_specs=[here] * len(results),
            scratch_shapes=[
                pltpu.VMEM((wanted, depth, width), BF16),
                pltpu.SemaphoreType.DMA((2 * wanted,)),
            ],
        ),
        cost_estimate=pl.CostEstimate(
            flops=2 * tokens * depth, bytes_accessed=2 * tokens * depth, transcendentals=0
        ),
        compiler_params=pltpu.CompilerParams(vmem_limit_bytes=50 << 20),
        name="project",
    )(columns, *sources, weight)


def settle_kernel(gate_ref, order_ref, layer_ref, *refs):
    terms, out_ref = refs[:-1], refs[-1]
    total = None
    for ref in terms:
        part = lax.dot_general(
            order_ref[...], ref[...], (((0,), (0,)), ((), ())), preferred_element_type=F32
        )
        total = part if total is None else total + part
    out_ref[...] = (layer_ref[...].astype(F32) + gate_ref[0] * total).astype(BF16)


def settle(gate, order, layer, terms):
    tokens, width = layer.shape
    cuts = 4
    step = width // cuts
    tall = pl.BlockSpec((tokens, step), lambda g: (0, g))
    return pl.pallas_call(
        settle_kernel,
        out_shape=jax.ShapeDtypeStruct((tokens, width), BF16),
        grid=(cuts,),
        in_specs=[
            pl.BlockSpec(memory_space=pltpu.SMEM),
            pl.BlockSpec((tokens, tokens), lambda g: (0, 0)),
            tall,
        ]
        + [tall] * len(terms),
        out_specs=tall,
        compiler_params=pltpu.CompilerParams(vmem_limit_bytes=24 << 20),
        name="settle",
    )(gate, order, layer, *terms)


def shards(
    queries, image_keys, image_values, layer_input, out_weight, tile_counts, image_range, attn_gate
):
    tokens, width = queries.shape
    keys, hd = image_keys.shape
    y, x, core = (lax.axis_index(n) for n in SEQ)
    z, yh = (lax.axis_index(n) for n in HEAD)
    ny, nx, nc = (lax.axis_size(n) for n in SEQ)
    nz, nyh = (lax.axis_size(n) for n in HEAD)

    padded = -(-keys // 128) * 128
    spare = jnp.broadcast_to(image_keys[:1], (padded - keys, hd))
    key_t = jnp.concatenate([image_keys, spare], axis=0).T
    value = jnp.pad(image_values, ((0, padded - keys), (0, 0)))
    own = (key_t, value)
    across = [shifted(v, "y", 1) for v in own]

    bounds, _, _ = lax.optimization_barrier((image_range, key_t, value))
    low, high = bounds[0], bounds[1]
    grade = jnp.where(low < high, low * 16 + high, 1 << 10)
    place = jnp.arange(tokens, dtype=jnp.int32)
    ahead = (grade[None, :] < grade[:, None]) | (
        (grade[None, :] == grade[:, None]) & (place[None, :] < place[:, None])
    )
    rank = jnp.sum(ahead.astype(jnp.int32), axis=1)
    order = (rank[None, :] == place[:, None]).astype(BF16)
    extra = jnp.pad(bounds.astype(BF16).T, ((0, 0), (0, hd - 2)))
    payload = jnp.dot(
        order, jnp.concatenate([queries, extra], axis=1), preferred_element_type=F32
    ).astype(BF16)
    payloads = {s: shifted(payload, "x", s) for s in (2, 1, 3)}
    payloads[0] = payload
    late = lax.optimization_barrier((key_t, value, payloads[1]))[:2]
    beside = [shifted(v, "core", 1) for v in late]
    diagonal = [shifted(v, "core", 1) for v in across]
    tiles = (own, beside, across, diagonal)

    image = jnp.arange(tile_counts.shape[0])
    ends = jnp.sum(jnp.where(image[None, :] <= image[:, None], tile_counts[None, :], 0), axis=1)
    tile = jnp.arange(ny * nx * nc, dtype=jnp.int32)
    owner = jnp.sum((ends[None, :] <= tile[:, None]).astype(jnp.int32), axis=1)
    hits = (low[:, None] <= owner[None, :]) & (owner[None, :] < high[:, None])
    which = jnp.arange(tokens // CHUNK, dtype=jnp.int32)
    member = rank[:, None] // CHUNK == which[None, :]
    live = jnp.any(member[:, :, None] & hits[:, None, :], axis=0).astype(jnp.int32)
    everyone = lax.all_gather(live, "x")

    def number(yy, cc):
        return (yy % ny * nx + x) * nc + cc % nc

    held = jnp.stack([number(y, core), number(y, core + 1), number(y + 1, core), number(y + 1, core + 1)])
    mine = (held[:, None] == tile[None, :]).astype(jnp.int32)
    images = jnp.sum(mine * owner[None, :], axis=1)

    parts = {}
    for turns in GROUPS:
        source = jnp.stack([(x - s) % nx for s in turns])
        from_whom = (source[:, None] == jnp.arange(nx)[None, :]).astype(jnp.int32)
        chosen = from_whom[:, :, None, None, None] * everyone[None, :, :, None, :]
        wanted = jnp.sum(chosen * mine[None, None, None, :, :], axis=(1, 4))
        items, count = work_list(wanted)
        got = attend(
            [payloads[s] for s in turns],
            items,
            count,
            images,
            [t[0] for t in tiles],
            [t[1] for t in tiles],
            keys,
            tokens,
        )
        for s, part in zip(turns, got):
            parts[s] = part if s == 0 else shifted(part, "x", nx - s)

    sources = [parts[s] for s in (2, 1, 3, 0)]
    terms = []
    for some in ROUTES:
        column = jnp.stack([(z + dz) % nz * nyh + (yh + dy) % nyh for dz, dy in some]).astype(jnp.int32)
        got = project(sources, out_weight, column, width, hd)
        if len(sources) > 1:
            sources = [got[-1]]
        for (dz, dy), term in zip(some, got):
            if len(terms) > 4:
                term = lax.optimization_barrier((term, terms[len(terms) - 5]))[0]
            terms.append(term if (dz, dy) == (0, 0) else head_shifted(term, dz, dy))
    return settle(jnp.tanh(attn_gate), order, layer_input, terms)


def solution(mesh):
    split = Mesh(mesh.devices.reshape(2, 4, 2, 4, 2), ("y", "x", "core", "z", "yh"))
    return jax.shard_map(
        shards,
        mesh=split,
        in_specs=(
            P(SEQ, HEAD),
            P(SEQ, HEAD),
            P(SEQ, HEAD),
            P(SEQ, HEAD),
            P(HEAD, None),
            P(),
            P(None, SEQ),
            P(),
        ),
        out_specs=P(SEQ, HEAD),
        check_vma=False,
    )
```

```python
import math

import jax
import jax.numpy as jnp
from jax import lax
from jax.experimental import pallas as pl
from jax.experimental.pallas import tpu as pltpu
from jax.sharding import Mesh
from jax.sharding import PartitionSpec as P

SEQ = ("y", "x", "core")
HEAD = ("z", "yh")
CHUNK = 32
GROUPS = ((2, 1, 3, 0),)
LOWEST = -1e30
BLOCKED = 1e30
BF16 = jnp.bfloat16
F32 = jnp.float32


def shifted(value, axis, steps):
    count = lax.axis_size(axis)
    return lax.ppermute(value, axis, [(s, (s + steps) % count) for s in range(count)])


def head_shifted(value, dz, dy):
    nz, ny = lax.axis_size("z"), lax.axis_size("yh")
    pairs = []
    for z in range(nz):
        for y in range(ny):
            pairs.append((z * ny + y, (z + dz) % nz * ny + (y + dy) % ny))
    return lax.ppermute(value, HEAD, pairs)


def attend_kernel(items, count, images, *refs, scale, hd, group, blocks, keys, padded):
    q_refs = refs[:blocks]
    key_refs = refs[blocks : blocks + 4]
    value_refs = refs[blocks + 4 : blocks + 8]
    out_refs = refs[blocks + 8 : 2 * blocks + 8]
    q_all, key_all, value_all, first_s, second_s, first_b, second_b, top_ref, acc_ref, sems = refs[
        2 * blocks + 8 :
    ]
    tokens = out_refs[0].shape[0]
    rows = CHUNK * group
    width = group * hd
    factor = scale * math.log2(math.e)
    copies = []
    for j in range(4):
        copies.append(pltpu.make_async_copy(key_refs[j], key_all.at[j], sems.at[2 * j]))
        copies.append(
            pltpu.make_async_copy(
                value_refs[j], value_all.at[j, :, pl.ds(0, hd)], sems.at[2 * j + 1]
            )
        )
    for i in range(blocks):
        copies.append(
            pltpu.make_async_copy(
                q_refs[i], q_all.at[pl.ds(i * tokens, tokens)], sems.at[8 + i]
            )
        )
    for copy in copies:
        copy.start()
    place = lax.broadcasted_iota(jnp.int32, (padded, hd), 0)
    ones = jnp.where(place < keys, 1.0, 0.0).astype(BF16)
    for j in range(4):
        value_all[j, :, hd:] = ones
    top_ref[...] = jnp.full(top_ref.shape, LOWEST, F32)
    acc_ref[...] = jnp.zeros(acc_ref.shape, F32)
    for copy in copies:
        copy.wait()

    def where_is(i):
        item = items[i]
        return item // 8, item % 4, jnp.where(item % 8 < 4, images[item % 4], -1)

    def score(i, scores_ref, best_ref):
        chunk, j, _ = where_is(i)
        at = pl.ds(pl.multiple_of(chunk * CHUNK, CHUNK), CHUNK)
        q = jnp.concatenate([q_all[at, h * hd : (h + 1) * hd] for h in range(group)], axis=0)
        best = None
        for k in range(0, padded, 128):
            part = jnp.dot(q, key_all[j, :, k : k + 128], preferred_element_type=F32)
            scores_ref[:, k : k + 128] = part
            best = part if best is None else jnp.maximum(best, part)
        best_ref[...] = jnp.broadcast_to(jnp.max(best, axis=1, keepdims=True), best_ref.shape)

    def absorb(i, scores_ref, best_ref):
        chunk, j, image = where_is(i)
        at = pl.ds(pl.multiple_of(chunk * rows, rows), rows)
        near = pl.ds(pl.multiple_of(chunk * CHUNK, CHUNK), CHUNK)
        reach = q_all[near, width : width + hd].astype(F32)
        low = jnp.concatenate([reach[:, 0:1]] * group, axis=0)
        high = jnp.concatenate([reach[:, 1:2]] * group, axis=0)
        number = image.astype(F32)
        allowed = (low <= number) & (number < high)
        old = top_ref[at, 0:1]
        new = jnp.where(allowed, jnp.maximum(old, best_ref[:, 0:1]), old)
        anchor = jnp.where(allowed, new, BLOCKED)
        rescale = jnp.exp2((old - new) * factor)
        top_ref[at, :] = jnp.broadcast_to(new, (rows, hd))
        weights = jnp.exp2((scores_ref[...] - anchor) * factor).astype(BF16)
        mixed = jnp.dot(weights, value_all[j], preferred_element_type=F32)
        acc_ref[at, :] = acc_ref[at, :] * rescale + mixed

    def pair(k, carry):
        i = 2 * k
        score(i + 1, second_s, second_b)
        absorb(i, first_s, first_b)
        score(i + 2, first_s, first_b)
        absorb(i + 1, second_s, second_b)
        return carry

    score(0, first_s, first_b)
    lax.fori_loop(0, (count[0] + 1) // 2, pair, 0)

    lane = lax.broadcasted_iota(jnp.int32, (CHUNK, hd), 1)
    for c in range(blocks * tokens // CHUNK):
        out_ref = out_refs[c * CHUNK // tokens]
        near = pl.ds(c * CHUNK % tokens, CHUNK)
        totals = jnp.zeros((CHUNK, hd), F32)
        tops = jnp.zeros((CHUNK, hd), F32)
        for h in range(group):
            at = pl.ds(c * rows + h * CHUNK, CHUNK)
            total = acc_ref[at, hd:]
            safe = jnp.where(total > 0, total, 1.0)
            out_ref[near, h * hd : (h + 1) * hd] = (acc_ref[at, :hd] / safe).astype(BF16)
            totals = jnp.where(lane % group == h, total, totals)
            tops = jnp.where(lane % group == h, top_ref[at, :], tops)
        seen = totals > 0
        logsum = jnp.where(seen, tops * scale + jnp.log(jnp.where(seen, totals, 1.0)), LOWEST)
        hi = logsum.astype(BF16).astype(F32)
        mid = (logsum - hi).astype(BF16).astype(F32)
        lo = logsum - hi - mid
        pieces = jnp.where(lane < group, hi, jnp.where(lane < 2 * group, mid, lo))
        out_ref[near, width:] = pieces.astype(BF16)


def attend(payloads, items, count, images, keys_t, values, keys, tokens):
    blocks = len(payloads)
    wide = payloads[0].shape[1]
    hd, padded = keys_t[0].shape
    width = wide - hd
    group = width // hd
    rows = CHUNK * group
    apart = pl.BlockSpec(memory_space=pl.ANY)
    here = pl.BlockSpec(memory_space=pltpu.VMEM)
    return pl.pallas_call(
        lambda *refs: attend_kernel(
            *refs,
            scale=1.0 / math.sqrt(hd),
            hd=hd,
            group=group,
            blocks=blocks,
            keys=keys,
            padded=padded,
        ),
        out_shape=[jax.ShapeDtypeStruct((tokens, wide), BF16)] * blocks,
        grid_spec=pltpu.PrefetchScalarGridSpec(
            num_scalar_prefetch=3,
            grid=(),
            in_specs=[apart] * (blocks + 8),
            out_specs=[here] * blocks,
            scratch_shapes=[
                pltpu.VMEM((blocks * tokens, wide), BF16),
                pltpu.VMEM((4, hd, padded), BF16),
                pltpu.VMEM((4, padded, 2 * hd), BF16),
                pltpu.VMEM((rows, padded), F32),
                pltpu.VMEM((rows, padded), F32),
                pltpu.VMEM((rows, hd), F32),
                pltpu.VMEM((rows, hd), F32),
                pltpu.VMEM((blocks * tokens * group, hd), F32),
                pltpu.VMEM((blocks * tokens * group, 2 * hd), F32),
                pltpu.SemaphoreType.DMA((8 + blocks,)),
            ],
        ),
        compiler_params=pltpu.CompilerParams(vmem_limit_bytes=32 << 20),
        cost_estimate=pl.CostEstimate(
            flops=2 * blocks * tokens * group * padded * 2 * hd,
            bytes_accessed=blocks * tokens * width * 4 + padded * hd * 16,
            transcendentals=blocks * tokens * group * padded * 2,
        ),
        name="attend",
    )(items, count, images, *payloads, *keys_t, *values)


def work_list(wanted):
    tiles = wanted.shape[-1]
    flags = wanted.reshape(-1) > 0
    size = flags.shape[0]
    place = jnp.arange(size, dtype=jnp.int32)
    rank = jnp.sum((place[None, :] < place[:, None]) & flags[None, :], axis=1)
    count = jnp.sum(flags.astype(jnp.int32))
    code = place // tiles * 8 + place % tiles + 1
    slot = jnp.arange(size + 3, dtype=jnp.int32)
    chosen = (rank[None, :] == slot[:, None]) & flags[None, :]
    items = jnp.sum(jnp.where(chosen, code[None, :], 0), axis=1)
    items = jnp.where(items > 0, items - 1, 4)
    return items.astype(jnp.int32), count.reshape(1)


def combined(order_ref, parts, out_ref, hd, group):
    width = group * hd
    sums = []
    for ref in parts:
        pieces = ref[:, width:].astype(F32)
        sums.append(pieces[:, :group] + pieces[:, group : 2 * group] + pieces[:, 2 * group : 3 * group])
    top = jnp.maximum(jnp.maximum(sums[0], sums[1]), jnp.maximum(sums[2], sums[3]))
    shares = [jnp.exp(s - top) for s in sums]
    total = shares[0] + shares[1] + shares[2] + shares[3]
    shares = [s / total for s in shares]
    for h in range(group):
        at = slice(h * hd, (h + 1) * hd)
        mixed = parts[0][:, at].astype(F32) * shares[0][:, h : h + 1]
        for ref, share in zip(parts[1:], shares[1:]):
            mixed = mixed + ref[:, at].astype(F32) * share[:, h : h + 1]
        placed = lax.dot_general(
            order_ref[...], mixed.astype(BF16), (((0,), (0,)), ((), ())), preferred_element_type=F32
        )
        out_ref[:, at] = placed.astype(BF16)


def project_kernel(columns, *refs, hd, group, pieces, merge):
    sources = refs[: 5 if merge else 1]
    w_ref = refs[len(sources)]
    outs = refs[len(sources) + 1 : len(sources) + 1 + len(pieces)]
    held, sems = refs[-2:]
    width = held.shape[2]
    copies = []
    for i in range(sum(pieces)):
        start = pl.multiple_of(columns[i] * width, width)
        copies.append(pltpu.make_async_copy(w_ref.at[:, pl.ds(start, width)], held.at[i], sems.at[i]))
        copies[-1].start()
    if merge:
        attended = refs[len(sources) + 1 + len(pieces)]
        combined(sources[0], sources[1:], attended, hd, group)
    else:
        attended = sources[0]
    i = 0
    for out_ref, count in zip(outs, pieces):
        for c in range(count):
            copies[i].wait()
            term = jnp.dot(attended[...], held[i], preferred_element_type=F32)
            out_ref[:, c * width : (c + 1) * width] = term.astype(BF16)
            i += 1


def project(sources, weight, columns, pieces, width, hd):
    merge = len(sources) > 1
    tokens = sources[-1].shape[0]
    depth = weight.shape[0]
    total = sum(pieces)
    here = pl.BlockSpec(memory_space=pltpu.VMEM)
    results = [jax.ShapeDtypeStruct((tokens, width * count), BF16) for count in pieces]
    if merge:
        results.append(jax.ShapeDtypeStruct((tokens, depth), BF16))
    return pl.pallas_call(
        lambda *refs: project_kernel(*refs, hd=hd, group=depth // hd, pieces=pieces, merge=merge),
        out_shape=results,
        grid_spec=pltpu.PrefetchScalarGridSpec(
            num_scalar_prefetch=1,
            grid=(),
            in_specs=[here] * len(sources) + [pl.BlockSpec(memory_space=pl.ANY)],
            out_specs=[here] * len(results),
            scratch_shapes=[
                pltpu.VMEM((total, depth, width), BF16),
                pltpu.SemaphoreType.DMA((total,)),
            ],
        ),
        cost_estimate=pl.CostEstimate(
            flops=2 * tokens * depth, bytes_accessed=2 * tokens * depth, transcendentals=0
        ),
        compiler_params=pltpu.CompilerParams(vmem_limit_bytes=50 << 20),
        name="project",
    )(jnp.stack(columns).astype(jnp.int32), *sources, weight)


def add_kernel(*refs, count):
    parts, send_ref, keep_ref = refs[:count], refs[-2], refs[-1]
    total = parts[0][...].astype(F32)
    for ref in parts[1:]:
        total = total + ref[...].astype(F32)
    cut = send_ref.shape[1]
    send_ref[...] = total[:, :cut].astype(BF16)
    keep_ref[...] = total[:, cut:]


def add_up(parts, keep):
    tokens, width = parts[0].shape
    return pl.pallas_call(
        lambda *refs: add_kernel(*refs, count=len(parts)),
        out_shape=[
            jax.ShapeDtypeStruct((tokens, width - keep), BF16),
            jax.ShapeDtypeStruct((tokens, keep), F32),
        ],
        compiler_params=pltpu.CompilerParams(vmem_limit_bytes=24 << 20),
        name="add_up",
    )(*parts)


def settle_kernel(gate_ref, layer_ref, *refs):
    parts, out_ref = refs[:-1], refs[-1]
    half = out_ref.shape[1] // 2
    for at, some in ((slice(0, half), parts[:2]), (slice(half, None), parts[2:])):
        total = some[0][...]
        for ref in some[1:]:
            total = total + ref[...].astype(F32)
        out_ref[:, at] = (layer_ref[:, at].astype(F32) + gate_ref[0] * total).astype(BF16)


def settle(gate, layer, parts):
    tokens, width = layer.shape
    cuts = 2
    rows = tokens // cuts
    wide = pl.BlockSpec((rows, width), lambda g: (g, 0))
    part = pl.BlockSpec((rows, width // 2), lambda g: (g, 0))
    return pl.pallas_call(
        settle_kernel,
        out_shape=jax.ShapeDtypeStruct((tokens, width), BF16),
        grid=(cuts,),
        in_specs=[pl.BlockSpec(memory_space=pltpu.SMEM), wide] + [part] * len(parts),
        out_specs=wide,
        compiler_params=pltpu.CompilerParams(vmem_limit_bytes=24 << 20),
        name="settle",
    )(gate, layer, *parts)


def shards(
    queries, image_keys, image_values, layer_input, out_weight, tile_counts, image_range, attn_gate
):
    tokens, width = queries.shape
    keys, hd = image_keys.shape
    y, x, core = (lax.axis_index(n) for n in SEQ)
    z, yh = (lax.axis_index(n) for n in HEAD)
    ny, nx, nc = (lax.axis_size(n) for n in SEQ)
    nz, nyh = (lax.axis_size(n) for n in HEAD)

    padded = -(-keys // 128) * 128
    spare = jnp.broadcast_to(image_keys[:1], (padded - keys, hd))
    key_t = jnp.concatenate([image_keys, spare], axis=0).T
    value = jnp.pad(image_values, ((0, padded - keys), (0, 0)))
    own = (key_t, value)
    across = [shifted(v, "y", 1) for v in own]

    bounds, _, _ = lax.optimization_barrier((image_range, key_t, value))
    low, high = bounds[0], bounds[1]
    grade = jnp.where(low < high, low * 16 + high, 1 << 10)
    place = jnp.arange(tokens, dtype=jnp.int32)
    ahead = (grade[None, :] < grade[:, None]) | (
        (grade[None, :] == grade[:, None]) & (place[None, :] < place[:, None])
    )
    rank = jnp.sum(ahead.astype(jnp.int32), axis=1)
    order = (rank[None, :] == place[:, None]).astype(BF16)
    image = jnp.arange(tile_counts.shape[0])
    ends = jnp.sum(jnp.where(image[None, :] <= image[:, None], tile_counts[None, :], 0), axis=1)
    tile = jnp.arange(ny * nx * nc, dtype=jnp.int32)
    owner = jnp.sum((ends[None, :] <= tile[:, None]).astype(jnp.int32), axis=1)
    hits = (low[:, None] <= owner[None, :]) & (owner[None, :] < high[:, None])
    same = (place[:, None] // CHUNK == rank[None, :] // CHUNK).astype(BF16)
    live = jnp.dot(same, hits.astype(BF16), preferred_element_type=F32) > 0
    flagged = jnp.pad(live.astype(F32), ((0, 0), (width + 16, hd - 16 - tile.shape[0])))
    extra = jnp.pad(bounds.astype(BF16).T, ((0, 0), (0, hd - 2)))
    payload = jnp.dot(
        order, jnp.concatenate([queries, extra], axis=1), preferred_element_type=F32
    )
    payload = (payload + flagged).astype(BF16)
    payloads = {s: shifted(payload, "x", s) for s in (2, 1, 3)}
    payloads[0] = payload
    late = lax.optimization_barrier((key_t, value, across[0]))[:2]
    beside = [shifted(v, "core", 1) for v in late]
    diagonal = [shifted(v, "core", 1) for v in across]
    tiles = (own, beside, across, diagonal)

    def number(yy, cc):
        return (yy % ny * nx + x) * nc + cc % nc

    held = jnp.stack([number(y, core), number(y, core + 1), number(y + 1, core), number(y + 1, core + 1)])
    mine = (held[:, None] == tile[None, :]).astype(jnp.int32)
    images = jnp.sum(mine * owner[None, :], axis=1)

    parts = {}
    for turns in GROUPS:
        flags = jnp.concatenate([payloads[s][::CHUNK, width + 16 : width + 32] for s in turns], axis=0)
        wanted = jnp.sum(flags.astype(jnp.int32)[:, None, :] * mine[None, :, :], axis=2)
        items, count = work_list(wanted)
        got = attend(
            [payloads[s] for s in turns],
            items,
            count,
            images,
            [t[0] for t in tiles],
            [t[1] for t in tiles],
            keys,
            tokens,
        )
        for s, part in zip(turns, got):
            parts[s] = part if s == 0 else shifted(part, "x", nx - s)

    half = width // 2

    def first(dz, dy):
        return ((z + dz) % nz * nyh + (yh + dy) % nyh) * 2

    sources = [order] + [parts[s] for s in (2, 1, 3, 0)]
    over_y, attended = project(
        sources, out_weight, [first(dz, 1) + 1 for dz in (1, 2, 3, 0)], (4,), half, hd
    )
    got_y = shifted(over_y, "yh", 1)
    far = [first(dz, dy) for dz in (2, 1, 3) for dy in (1, 0)]
    over_z = project([attended], out_weight, far, (2, 2, 2), half, hd)
    got_z = [shifted(term, "z", dz) for dz, term in zip((2, 1, 3), over_z)]
    near = [first(0, 1), first(0, 0)] + [first(dz, 0) + 1 for dz in (1, 2, 3, 0)]
    own_z, own_y = project([attended], out_weight, near, (2, 4), half, hd)
    late_z, kept_b = add_up([own_y, got_y], half)
    ends_b = [shifted(late_z[:, i * half : (i + 1) * half], "z", i + 1) for i in (1, 0, 2)]
    late_y, kept_a = add_up([own_z] + got_z, half)
    end_a = shifted(late_y, "yh", 1)
    return settle(jnp.tanh(attn_gate), layer_input, [kept_a, end_a, kept_b] + ends_b)


def solution(mesh):
    split = Mesh(mesh.devices.reshape(2, 4, 2, 4, 2), ("y", "x", "core", "z", "yh"))
    return jax.shard_map(
        shards,
        mesh=split,
        in_specs=(
            P(SEQ, HEAD),
            P(SEQ, HEAD),
            P(SEQ, HEAD),
            P(SEQ, HEAD),
            P(HEAD, None),
            P(),
            P(None, SEQ),
            P(),
        ),
        out_specs=P(SEQ, HEAD),
        check_vma=False,
    )
```

```python
import math

import jax
import jax.numpy as jnp
from jax import lax
from jax.experimental import pallas as pl
from jax.experimental.pallas import tpu as pltpu
from jax.sharding import Mesh
from jax.sharding import PartitionSpec as P

SEQ = ("y", "x", "core")
HEAD = ("z", "yh")
CHUNK = 32
GROUPS = ((2, 1, 3, 0),)
LOWEST = -1e30
BLOCKED = 1e30
BF16 = jnp.bfloat16
F32 = jnp.float32


def shifted(value, axis, steps):
    count = lax.axis_size(axis)
    return lax.ppermute(value, axis, [(s, (s + steps) % count) for s in range(count)])


def head_shifted(value, dz, dy):
    nz, ny = lax.axis_size("z"), lax.axis_size("yh")
    pairs = []
    for z in range(nz):
        for y in range(ny):
            pairs.append((z * ny + y, (z + dz) % nz * ny + (y + dy) % ny))
    return lax.ppermute(value, HEAD, pairs)


def attend_kernel(items, count, images, *refs, scale, hd, group, blocks, keys, padded):
    q_refs = refs[:blocks]
    tile_refs = refs[blocks : blocks + 4]
    out_refs = refs[blocks + 4 : 2 * blocks + 4]
    q_all, key_all, value_in, value_all, first_s, second_s, first_b, second_b, top_ref, acc_ref, sems = refs[
        2 * blocks + 4 :
    ]
    tokens = out_refs[0].shape[0]
    rows = CHUNK * group
    width = group * hd
    factor = scale * math.log2(math.e)
    copies = []
    for j in range(4):
        copies.append(
            pltpu.make_async_copy(tile_refs[j].at[pl.ds(0, hd)], key_all.at[j], sems.at[2 * j])
        )
        copies.append(
            pltpu.make_async_copy(tile_refs[j].at[pl.ds(hd, hd)], value_in.at[j], sems.at[2 * j + 1])
        )
    for i in range(blocks):
        copies.append(
            pltpu.make_async_copy(
                q_refs[i], q_all.at[pl.ds(i * tokens, tokens)], sems.at[8 + i]
            )
        )
    for copy in copies:
        copy.start()
    place = lax.broadcasted_iota(jnp.int32, (padded, hd), 0)
    ones = jnp.where(place < keys, 1.0, 0.0).astype(BF16)
    for j in range(4):
        value_all[j, :, hd:] = ones
    top_ref[...] = jnp.full(top_ref.shape, LOWEST, F32)
    acc_ref[...] = jnp.zeros(acc_ref.shape, F32)
    for copy in copies:
        copy.wait()
    for j in range(4):
        for k in range(0, padded, hd):
            value_all[j, k : k + hd, :hd] = value_in[j, :, k : k + hd]

    def where_is(i):
        item = items[i]
        return item // 8, item % 4, jnp.where(item % 8 < 4, images[item % 4], -1)

    def score(i, scores_ref, best_ref):
        chunk, j, _ = where_is(i)
        at = pl.ds(pl.multiple_of(chunk * CHUNK, CHUNK), CHUNK)
        q = jnp.concatenate([q_all[at, h * hd : (h + 1) * hd] for h in range(group)], axis=0)
        best = None
        for k in range(0, padded, 128):
            part = jnp.dot(q, key_all[j, :, k : k + 128], preferred_element_type=F32)
            scores_ref[:, k : k + 128] = part
            best = part if best is None else jnp.maximum(best, part)
        best_ref[...] = jnp.broadcast_to(jnp.max(best, axis=1, keepdims=True), best_ref.shape)

    def absorb(i, scores_ref, best_ref):
        chunk, j, image = where_is(i)
        at = pl.ds(pl.multiple_of(chunk * rows, rows), rows)
        near = pl.ds(pl.multiple_of(chunk * CHUNK, CHUNK), CHUNK)
        reach = q_all[near, width : width + hd].astype(F32)
        low = jnp.concatenate([reach[:, 0:1]] * group, axis=0)
        high = jnp.concatenate([reach[:, 1:2]] * group, axis=0)
        number = image.astype(F32)
        allowed = (low <= number) & (number < high)
        old = top_ref[at, 0:1]
        new = jnp.where(allowed, jnp.maximum(old, best_ref[:, 0:1]), old)
        anchor = jnp.where(allowed, new, BLOCKED)
        rescale = jnp.exp2((old - new) * factor)
        top_ref[at, :] = jnp.broadcast_to(new, (rows, hd))
        weights = jnp.exp2((scores_ref[...] - anchor) * factor).astype(BF16)
        mixed = jnp.dot(weights, value_all[j], preferred_element_type=F32)
        acc_ref[at, :] = acc_ref[at, :] * rescale + mixed

    def pair(k, carry):
        i = 2 * k
        score(i + 1, second_s, second_b)
        absorb(i, first_s, first_b)
        score(i + 2, first_s, first_b)
        absorb(i + 1, second_s, second_b)
        return carry

    score(0, first_s, first_b)
    lax.fori_loop(0, (count[0] + 1) // 2, pair, 0)

    lane = lax.broadcasted_iota(jnp.int32, (CHUNK, hd), 1)
    for c in range(blocks * tokens // CHUNK):
        out_ref = out_refs[c * CHUNK // tokens]
        near = pl.ds(c * CHUNK % tokens, CHUNK)
        totals = jnp.zeros((CHUNK, hd), F32)
        tops = jnp.zeros((CHUNK, hd), F32)
        for h in range(group):
            at = pl.ds(c * rows + h * CHUNK, CHUNK)
            total = acc_ref[at, hd:]
            safe = jnp.where(total > 0, total, 1.0)
            out_ref[near, h * hd : (h + 1) * hd] = (acc_ref[at, :hd] / safe).astype(BF16)
            totals = jnp.where(lane % group == h, total, totals)
            tops = jnp.where(lane % group == h, top_ref[at, :], tops)
        seen = totals > 0
        logsum = jnp.where(seen, tops * scale + jnp.log(jnp.where(seen, totals, 1.0)), LOWEST)
        hi = logsum.astype(BF16).astype(F32)
        mid = (logsum - hi).astype(BF16).astype(F32)
        lo = logsum - hi - mid
        pieces = jnp.where(lane < group, hi, jnp.where(lane < 2 * group, mid, lo))
        out_ref[near, width:] = pieces.astype(BF16)


def attend(payloads, items, count, images, tiles, keys, tokens, hd):
    blocks = len(payloads)
    wide = payloads[0].shape[1]
    padded = tiles[0].shape[1]
    width = wide - hd
    group = width // hd
    rows = CHUNK * group
    apart = pl.BlockSpec(memory_space=pl.ANY)
    here = pl.BlockSpec(memory_space=pltpu.VMEM)
    return pl.pallas_call(
        lambda *refs: attend_kernel(
            *refs,
            scale=1.0 / math.sqrt(hd),
            hd=hd,
            group=group,
            blocks=blocks,
            keys=keys,
            padded=padded,
        ),
        out_shape=[jax.ShapeDtypeStruct((tokens, wide), BF16)] * blocks,
        grid_spec=pltpu.PrefetchScalarGridSpec(
            num_scalar_prefetch=3,
            grid=(),
            in_specs=[apart] * (blocks + 4),
            out_specs=[here] * blocks,
            scratch_shapes=[
                pltpu.VMEM((blocks * tokens, wide), BF16),
                pltpu.VMEM((4, hd, padded), BF16),
                pltpu.VMEM((4, hd, padded), BF16),
                pltpu.VMEM((4, padded, 2 * hd), BF16),
                pltpu.VMEM((rows, padded), F32),
                pltpu.VMEM((rows, padded), F32),
                pltpu.VMEM((rows, hd), F32),
                pltpu.VMEM((rows, hd), F32),
                pltpu.VMEM((blocks * tokens * group, hd), F32),
                pltpu.VMEM((blocks * tokens * group, 2 * hd), F32),
                pltpu.SemaphoreType.DMA((8 + blocks,)),
            ],
        ),
        compiler_params=pltpu.CompilerParams(vmem_limit_bytes=32 << 20),
        cost_estimate=pl.CostEstimate(
            flops=2 * blocks * tokens * group * padded * 2 * hd,
            bytes_accessed=blocks * tokens * width * 4 + padded * hd * 16,
            transcendentals=blocks * tokens * group * padded * 2,
        ),
        name="attend",
    )(items, count, images, *payloads, *tiles)


def prepare_kernel(key_ref, value_ref, q_ref, order_ref, extra_ref, tile_ref, payload_ref):
    keys, hd = key_ref.shape
    padded = tile_ref.shape[1]
    width = q_ref.shape[1]
    whole = keys // hd * hd
    mid = keys // 16 * 16
    for k in range(0, whole, hd):
        block = key_ref[k : k + hd].astype(F32)
        tile_ref[:hd, k : k + hd] = block.T.astype(BF16)
        tile_ref[hd:, k : k + hd] = value_ref[k : k + hd]
    first = lax.broadcasted_iota(jnp.int32, (padded - mid, hd), 0) == 0
    last_key = jnp.where(first, key_ref[mid:keys].astype(F32), key_ref[0:1].astype(F32))
    last_value = jnp.where(first, value_ref[mid:keys].astype(F32), 0.0)
    block = jnp.concatenate([key_ref[whole:mid].astype(F32), last_key], axis=0)
    tile_ref[:hd, whole:] = block.T.astype(BF16)
    block = jnp.concatenate([value_ref[whole:mid].astype(F32), last_value], axis=0)
    tile_ref[hd:, whole:] = block.astype(BF16)
    order = order_ref[...]
    step = 2 * hd
    for k in range(0, width, step):
        part = jnp.dot(order, q_ref[:, k : k + step], preferred_element_type=F32)
        payload_ref[:, k : k + step] = part.astype(BF16)
    payload_ref[:, width:] = extra_ref[...].astype(BF16)


def prepare(keys, values, queries, order, extra, padded):
    hd = keys.shape[1]
    tokens, width = queries.shape
    here = pl.BlockSpec(memory_space=pltpu.VMEM)
    return pl.pallas_call(
        prepare_kernel,
        out_shape=[
            jax.ShapeDtypeStruct((2 * hd, padded), BF16),
            jax.ShapeDtypeStruct((tokens, width + hd), BF16),
        ],
        in_specs=[here] * 5,
        out_specs=[here] * 2,
        compiler_params=pltpu.CompilerParams(vmem_limit_bytes=24 << 20),
        name="prepare",
    )(keys, values, queries, order, extra)


def work_list(wanted):
    tiles = wanted.shape[-1]
    flags = wanted.reshape(-1) > 0
    size = flags.shape[0]
    place = jnp.arange(size, dtype=jnp.int32)
    rank = jnp.sum((place[None, :] < place[:, None]) & flags[None, :], axis=1)
    count = jnp.sum(flags.astype(jnp.int32))
    code = place // tiles * 8 + place % tiles + 1
    slot = jnp.arange(size + 3, dtype=jnp.int32)
    chosen = (rank[None, :] == slot[:, None]) & flags[None, :]
    items = jnp.sum(jnp.where(chosen, code[None, :], 0), axis=1)
    items = jnp.where(items > 0, items - 1, 4)
    return items.astype(jnp.int32), count.reshape(1)


def combined(order_ref, parts, out_ref, hd, group):
    width = group * hd
    sums = []
    for ref in parts:
        pieces = ref[:, width:].astype(F32)
        sums.append(pieces[:, :group] + pieces[:, group : 2 * group] + pieces[:, 2 * group : 3 * group])
    top = jnp.maximum(jnp.maximum(sums[0], sums[1]), jnp.maximum(sums[2], sums[3]))
    shares = [jnp.exp(s - top) for s in sums]
    total = shares[0] + shares[1] + shares[2] + shares[3]
    shares = [s / total for s in shares]
    for h in range(group):
        at = slice(h * hd, (h + 1) * hd)
        mixed = parts[0][:, at].astype(F32) * shares[0][:, h : h + 1]
        for ref, share in zip(parts[1:], shares[1:]):
            mixed = mixed + ref[:, at].astype(F32) * share[:, h : h + 1]
        placed = lax.dot_general(
            order_ref[...], mixed.astype(BF16), (((0,), (0,)), ((), ())), preferred_element_type=F32
        )
        out_ref[:, at] = placed.astype(BF16)


def project_kernel(columns, *refs, hd, group, pieces, merge):
    sources = refs[: 5 if merge else 1]
    w_ref = refs[len(sources)]
    outs = refs[len(sources) + 1 : len(sources) + 1 + len(pieces)]
    held, sems = refs[-2:]
    width = held.shape[2]
    copies = []
    for i in range(sum(pieces)):
        start = pl.multiple_of(columns[i] * width, width)
        copies.append(pltpu.make_async_copy(w_ref.at[:, pl.ds(start, width)], held.at[i], sems.at[i]))
        copies[-1].start()
    if merge:
        attended = refs[len(sources) + 1 + len(pieces)]
        combined(sources[0], sources[1:], attended, hd, group)
    else:
        attended = sources[0]
    i = 0
    for out_ref, count in zip(outs, pieces):
        for c in range(count):
            copies[i].wait()
            term = jnp.dot(attended[...], held[i], preferred_element_type=F32)
            out_ref[:, c * width : (c + 1) * width] = term.astype(BF16)
            i += 1


def project(sources, weight, columns, pieces, width, hd):
    merge = len(sources) > 1
    tokens = sources[-1].shape[0]
    depth = weight.shape[0]
    total = sum(pieces)
    here = pl.BlockSpec(memory_space=pltpu.VMEM)
    results = [jax.ShapeDtypeStruct((tokens, width * count), BF16) for count in pieces]
    if merge:
        results.append(jax.ShapeDtypeStruct((tokens, depth), BF16))
    return pl.pallas_call(
        lambda *refs: project_kernel(*refs, hd=hd, group=depth // hd, pieces=pieces, merge=merge),
        out_shape=results,
        grid_spec=pltpu.PrefetchScalarGridSpec(
            num_scalar_prefetch=1,
            grid=(),
            in_specs=[here] * len(sources) + [pl.BlockSpec(memory_space=pl.ANY)],
            out_specs=[here] * len(results),
            scratch_shapes=[
                pltpu.VMEM((total, depth, width), BF16),
                pltpu.SemaphoreType.DMA((total,)),
            ],
        ),
        cost_estimate=pl.CostEstimate(
            flops=2 * tokens * depth, bytes_accessed=2 * tokens * depth, transcendentals=0
        ),
        compiler_params=pltpu.CompilerParams(vmem_limit_bytes=50 << 20),
        name="project",
    )(jnp.stack(columns).astype(jnp.int32), *sources, weight)


def add_kernel(*refs, count):
    parts, send_ref, keep_ref = refs[:count], refs[-2], refs[-1]
    total = parts[0][...].astype(F32)
    for ref in parts[1:]:
        total = total + ref[...].astype(F32)
    cut = send_ref.shape[1]
    send_ref[...] = total[:, :cut].astype(BF16)
    keep_ref[...] = total[:, cut:]


def add_up(parts, keep):
    tokens, width = parts[0].shape
    return pl.pallas_call(
        lambda *refs: add_kernel(*refs, count=len(parts)),
        out_shape=[
            jax.ShapeDtypeStruct((tokens, width - keep), BF16),
            jax.ShapeDtypeStruct((tokens, keep), F32),
        ],
        compiler_params=pltpu.CompilerParams(vmem_limit_bytes=24 << 20),
        name="add_up",
    )(*parts)


def settle_kernel(gate_ref, layer_ref, *refs):
    parts, out_ref = refs[:-1], refs[-1]
    half = out_ref.shape[1] // 2
    for at, some in ((slice(0, half), parts[:2]), (slice(half, None), parts[2:])):
        total = some[0][...]
        for ref in some[1:]:
            total = total + ref[...].astype(F32)
        out_ref[:, at] = (layer_ref[:, at].astype(F32) + gate_ref[0] * total).astype(BF16)


def settle(gate, layer, parts):
    tokens, width = layer.shape
    cuts = 2
    rows = tokens // cuts
    wide = pl.BlockSpec((rows, width), lambda g: (g, 0))
    part = pl.BlockSpec((rows, width // 2), lambda g: (g, 0))
    return pl.pallas_call(
        settle_kernel,
        out_shape=jax.ShapeDtypeStruct((tokens, width), BF16),
        grid=(cuts,),
        in_specs=[pl.BlockSpec(memory_space=pltpu.SMEM), wide] + [part] * len(parts),
        out_specs=wide,
        compiler_params=pltpu.CompilerParams(vmem_limit_bytes=24 << 20),
        name="settle",
    )(gate, layer, *parts)


def shards(
    queries, image_keys, image_values, layer_input, out_weight, tile_counts, image_range, attn_gate
):
    tokens, width = queries.shape
    keys, hd = image_keys.shape
    y, x, core = (lax.axis_index(n) for n in SEQ)
    z, yh = (lax.axis_index(n) for n in HEAD)
    ny, nx, nc = (lax.axis_size(n) for n in SEQ)
    nz, nyh = (lax.axis_size(n) for n in HEAD)

    padded = -(-keys // 128) * 128
    low, high = image_range[0], image_range[1]
    grade = jnp.where(low < high, low * 16 + high, 1 << 10)
    place = jnp.arange(tokens, dtype=jnp.int32)
    ahead = (grade[None, :] < grade[:, None]) | (
        (grade[None, :] == grade[:, None]) & (place[None, :] < place[:, None])
    )
    rank = jnp.sum(ahead.astype(jnp.int32), axis=1)
    order = (rank[None, :] == place[:, None]).astype(BF16)
    image = jnp.arange(tile_counts.shape[0])
    ends = jnp.sum(jnp.where(image[None, :] <= image[:, None], tile_counts[None, :], 0), axis=1)
    tile = jnp.arange(ny * nx * nc, dtype=jnp.int32)
    owner = jnp.sum((ends[None, :] <= tile[:, None]).astype(jnp.int32), axis=1)
    hits = (low[:, None] <= owner[None, :]) & (owner[None, :] < high[:, None])
    same = (place[:, None] // CHUNK == rank[None, :] // CHUNK).astype(BF16)
    live = jnp.dot(same, hits.astype(BF16), preferred_element_type=F32) > 0
    span = jnp.dot(order, image_range.astype(BF16).T, preferred_element_type=F32)
    extra = jnp.concatenate(
        [
            jnp.pad(span, ((0, 0), (0, 14))),
            jnp.pad(live.astype(F32), ((0, 0), (0, hd - 16 - tile.shape[0]))),
        ],
        axis=1,
    )
    own, payload = prepare(image_keys, image_values, queries, order, extra, padded)
    across = shifted(own, "y", 1)
    payloads = {s: shifted(payload, "x", s) for s in (2, 1, 3)}
    payloads[0] = payload
    beside = shifted(own, "core", 1)
    diagonal = shifted(across, "core", 1)
    tiles = (own, beside, across, diagonal)

    def number(yy, cc):
        return (yy % ny * nx + x) * nc + cc % nc

    held = jnp.stack([number(y, core), number(y, core + 1), number(y + 1, core), number(y + 1, core + 1)])
    mine = (held[:, None] == tile[None, :]).astype(jnp.int32)
    images = jnp.sum(mine * owner[None, :], axis=1)

    parts = {}
    for turns in GROUPS:
        flags = jnp.concatenate([payloads[s][::CHUNK, width + 16 : width + 32] for s in turns], axis=0)
        wanted = jnp.sum(flags.astype(jnp.int32)[:, None, :] * mine[None, :, :], axis=2)
        items, count = work_list(wanted)
        got = attend(
            [payloads[s] for s in turns],
            items,
            count,
            images,
            tiles,
            keys,
            tokens,
            hd,
        )
        for s, part in zip(turns, got):
            parts[s] = part if s == 0 else shifted(part, "x", nx - s)

    half = width // 2

    def first(dz, dy):
        return ((z + dz) % nz * nyh + (yh + dy) % nyh) * 2

    sources = [order] + [parts[s] for s in (2, 1, 3, 0)]
    far = [first(dz, dy) for dz in (2, 1) for dy in (1, 0)]
    *over_z, attended = project(sources, out_weight, far, (2, 2), half, hd)
    got_z = [shifted(term, "z", dz) for dz, term in zip((2, 1), over_z)]
    mixed = [first(3, 1), first(3, 0)] + [first(dz, 1) + 1 for dz in (1, 2, 3, 0)]
    last_z, over_y = project([attended], out_weight, mixed, (2, 4), half, hd)
    got_y = shifted(over_y, "yh", 1)
    got_z.append(shifted(last_z, "z", 3))
    near = [first(0, 1), first(0, 0)] + [first(dz, 0) + 1 for dz in (1, 2, 3, 0)]
    own_z, own_y = project([attended], out_weight, near, (2, 4), half, hd)
    late_z, kept_b = add_up([own_y, got_y], half)
    ends_b = [shifted(late_z[:, i * half : (i + 1) * half], "z", i + 1) for i in (1, 0, 2)]
    late_y, kept_a = add_up([own_z] + got_z[::-1], half)
    end_a = shifted(late_y, "yh", 1)
    return settle(jnp.tanh(attn_gate), layer_input, [kept_a, end_a, kept_b] + ends_b)


def solution(mesh):
    split = Mesh(mesh.devices.reshape(2, 4, 2, 4, 2), ("y", "x", "core", "z", "yh"))
    return jax.shard_map(
        shards,
        mesh=split,
        in_specs=(
            P(SEQ, HEAD),
            P(SEQ, HEAD),
            P(SEQ, HEAD),
            P(SEQ, HEAD),
            P(HEAD, None),
            P(),
            P(None, SEQ),
            P(),
        ),
        out_specs=P(SEQ, HEAD),
        check_vma=False,
    )
```

```python
import math

import jax
import jax.numpy as jnp
from jax import lax
from jax.experimental import pallas as pl
from jax.experimental.pallas import tpu as pltpu
from jax.sharding import Mesh
from jax.sharding import PartitionSpec as P

SEQ = ("y", "x", "core")
HEAD = ("z", "yh")
CHUNK = 32
GROUPS = ((2, 1, 3), (0,))
LOWEST = -1e30
BLOCKED = 1e30
BF16 = jnp.bfloat16
F32 = jnp.float32


def shifted(value, axis, steps):
    count = lax.axis_size(axis)
    return lax.ppermute(value, axis, [(s, (s + steps) % count) for s in range(count)])


def head_shifted(value, dz, dy):
    nz, ny = lax.axis_size("z"), lax.axis_size("yh")
    pairs = []
    for z in range(nz):
        for y in range(ny):
            pairs.append((z * ny + y, (z + dz) % nz * ny + (y + dy) % ny))
    return lax.ppermute(value, HEAD, pairs)


def attend_kernel(items, count, images, *refs, scale, hd, group, blocks, keys, padded):
    q_refs = refs[:blocks]
    tile_refs = refs[blocks : blocks + 4]
    out_refs = refs[blocks + 4 : 2 * blocks + 4]
    q_all, key_all, value_in, value_all, first_s, second_s, first_b, second_b, top_ref, acc_ref, sems = refs[
        2 * blocks + 4 :
    ]
    tokens = out_refs[0].shape[0]
    rows = CHUNK * group
    width = group * hd
    factor = scale * math.log2(math.e)
    copies = []
    for j in range(4):
        copies.append(
            pltpu.make_async_copy(tile_refs[j].at[pl.ds(0, hd)], key_all.at[j], sems.at[2 * j])
        )
        copies.append(
            pltpu.make_async_copy(tile_refs[j].at[pl.ds(hd, hd)], value_in.at[j], sems.at[2 * j + 1])
        )
    for i in range(blocks):
        copies.append(
            pltpu.make_async_copy(
                q_refs[i], q_all.at[pl.ds(i * tokens, tokens)], sems.at[8 + i]
            )
        )
    for copy in copies:
        copy.start()
    place = lax.broadcasted_iota(jnp.int32, (padded, hd), 0)
    ones = jnp.where(place < keys, 1.0, 0.0).astype(BF16)
    for j in range(4):
        value_all[j, :, hd:] = ones
    top_ref[...] = jnp.full(top_ref.shape, LOWEST, F32)
    acc_ref[...] = jnp.zeros(acc_ref.shape, F32)
    for copy in copies:
        copy.wait()
    for j in range(4):
        for k in range(0, padded, hd):
            value_all[j, k : k + hd, :hd] = value_in[j, :, k : k + hd]

    def where_is(i):
        item = items[i]
        return item // 8, item % 4, jnp.where(item % 8 < 4, images[item % 4], -1)

    def score(i, scores_ref, best_ref):
        chunk, j, _ = where_is(i)
        at = pl.ds(pl.multiple_of(chunk * CHUNK, CHUNK), CHUNK)
        q = jnp.concatenate([q_all[at, h * hd : (h + 1) * hd] for h in range(group)], axis=0)
        best = None
        for k in range(0, padded, 128):
            part = jnp.dot(q, key_all[j, :, k : k + 128], preferred_element_type=F32)
            scores_ref[:, k : k + 128] = part
            best = part if best is None else jnp.maximum(best, part)
        best_ref[...] = jnp.broadcast_to(jnp.max(best, axis=1, keepdims=True), best_ref.shape)

    def absorb(i, scores_ref, best_ref):
        chunk, j, image = where_is(i)
        at = pl.ds(pl.multiple_of(chunk * rows, rows), rows)
        near = pl.ds(pl.multiple_of(chunk * CHUNK, CHUNK), CHUNK)
        reach = q_all[near, width : width + hd].astype(F32)
        low = jnp.concatenate([reach[:, 0:1]] * group, axis=0)
        high = jnp.concatenate([reach[:, 1:2]] * group, axis=0)
        number = image.astype(F32)
        allowed = (low <= number) & (number < high)
        old = top_ref[at, 0:1]
        new = jnp.where(allowed, jnp.maximum(old, best_ref[:, 0:1]), old)
        anchor = jnp.where(allowed, new, BLOCKED)
        rescale = jnp.exp2((old - new) * factor)
        top_ref[at, :] = jnp.broadcast_to(new, (rows, hd))
        weights = jnp.exp2((scores_ref[...] - anchor) * factor).astype(BF16)
        mixed = jnp.dot(weights, value_all[j], preferred_element_type=F32)
        acc_ref[at, :] = acc_ref[at, :] * rescale + mixed

    def pair(k, carry):
        i = 2 * k
        score(i + 1, second_s, second_b)
        absorb(i, first_s, first_b)
        score(i + 2, first_s, first_b)
        absorb(i + 1, second_s, second_b)
        return carry

    score(0, first_s, first_b)
    lax.fori_loop(0, (count[0] + 1) // 2, pair, 0)

    lane = lax.broadcasted_iota(jnp.int32, (CHUNK, hd), 1)
    for c in range(blocks * tokens // CHUNK):
        out_ref = out_refs[c * CHUNK // tokens]
        near = pl.ds(c * CHUNK % tokens, CHUNK)
        totals = jnp.zeros((CHUNK, hd), F32)
        tops = jnp.zeros((CHUNK, hd), F32)
        for h in range(group):
            at = pl.ds(c * rows + h * CHUNK, CHUNK)
            total = acc_ref[at, hd:]
            safe = jnp.where(total > 0, total, 1.0)
            out_ref[near, h * hd : (h + 1) * hd] = (acc_ref[at, :hd] / safe).astype(BF16)
            totals = jnp.where(lane % group == h, total, totals)
            tops = jnp.where(lane % group == h, top_ref[at, :], tops)
        seen = totals > 0
        logsum = jnp.where(seen, tops * scale + jnp.log(jnp.where(seen, totals, 1.0)), LOWEST)
        hi = logsum.astype(BF16).astype(F32)
        mid = (logsum - hi).astype(BF16).astype(F32)
        lo = logsum - hi - mid
        pieces = jnp.where(lane < group, hi, jnp.where(lane < 2 * group, mid, lo))
        out_ref[near, width:] = pieces.astype(BF16)


def attend(payloads, items, count, images, tiles, keys, tokens, hd):
    blocks = len(payloads)
    wide = payloads[0].shape[1]
    padded = tiles[0].shape[1]
    width = wide - hd
    group = width // hd
    rows = CHUNK * group
    apart = pl.BlockSpec(memory_space=pl.ANY)
    here = pl.BlockSpec(memory_space=pltpu.VMEM)
    return pl.pallas_call(
        lambda *refs: attend_kernel(
            *refs,
            scale=1.0 / math.sqrt(hd),
            hd=hd,
            group=group,
            blocks=blocks,
            keys=keys,
            padded=padded,
        ),
        out_shape=[jax.ShapeDtypeStruct((tokens, wide), BF16)] * blocks,
        grid_spec=pltpu.PrefetchScalarGridSpec(
            num_scalar_prefetch=3,
            grid=(),
            in_specs=[apart] * (blocks + 4),
            out_specs=[here] * blocks,
            scratch_shapes=[
                pltpu.VMEM((blocks * tokens, wide), BF16),
                pltpu.VMEM((4, hd, padded), BF16),
                pltpu.VMEM((4, hd, padded), BF16),
                pltpu.VMEM((4, padded, 2 * hd), BF16),
                pltpu.VMEM((rows, padded), F32),
                pltpu.VMEM((rows, padded), F32),
                pltpu.VMEM((rows, hd), F32),
                pltpu.VMEM((rows, hd), F32),
                pltpu.VMEM((blocks * tokens * group, hd), F32),
                pltpu.VMEM((blocks * tokens * group, 2 * hd), F32),
                pltpu.SemaphoreType.DMA((8 + blocks,)),
            ],
        ),
        compiler_params=pltpu.CompilerParams(vmem_limit_bytes=32 << 20),
        cost_estimate=pl.CostEstimate(
            flops=2 * blocks * tokens * group * padded * 2 * hd,
            bytes_accessed=blocks * tokens * width * 4 + padded * hd * 16,
            transcendentals=blocks * tokens * group * padded * 2,
        ),
        name="attend",
    )(items, count, images, *payloads, *tiles)


def pack_kernel(key_hbm, value_hbm, tile_ref, key_ref, value_ref, sems):
    copies = [
        pltpu.make_async_copy(key_hbm, key_ref, sems.at[0]),
        pltpu.make_async_copy(value_hbm, value_ref, sems.at[1]),
    ]
    for copy in copies:
        copy.start()
    for copy in copies:
        copy.wait()
    keys, hd = key_ref.shape
    whole = keys // hd * hd
    mid = keys // 16 * 16
    padded = tile_ref.shape[1]
    for k in range(0, whole, hd):
        block = key_ref[k : k + hd].astype(F32)
        tile_ref[:hd, k : k + hd] = block.T.astype(BF16)
        tile_ref[hd:, k : k + hd] = value_ref[k : k + hd]
    first = lax.broadcasted_iota(jnp.int32, (padded - mid, hd), 0) == 0
    last_key = jnp.where(first, key_ref[mid:keys].astype(F32), key_ref[0:1].astype(F32))
    last_value = jnp.where(first, value_ref[mid:keys].astype(F32), 0.0)
    block = jnp.concatenate([key_ref[whole:mid].astype(F32), last_key], axis=0)
    tile_ref[:hd, whole:] = block.T.astype(BF16)
    block = jnp.concatenate([value_ref[whole:mid].astype(F32), last_value], axis=0)
    tile_ref[hd:, whole:] = block.astype(BF16)


def pack(keys, values, padded):
    hd = keys.shape[1]
    apart = pl.BlockSpec(memory_space=pl.ANY)
    return pl.pallas_call(
        pack_kernel,
        out_shape=jax.ShapeDtypeStruct((2 * hd, padded), BF16),
        in_specs=[apart] * 2,
        out_specs=pl.BlockSpec(memory_space=pltpu.VMEM),
        scratch_shapes=[
            pltpu.VMEM(keys.shape, BF16),
            pltpu.VMEM(values.shape, BF16),
            pltpu.SemaphoreType.DMA((2,)),
        ],
        compiler_params=pltpu.CompilerParams(vmem_limit_bytes=60 << 20),
        name="pack",
    )(keys, values)


def sort_kernel(q_ref, order_ref, extra_ref, payload_ref):
    width = q_ref.shape[1]
    order = order_ref[...]
    step = 256
    for k in range(0, width, step):
        part = jnp.dot(order, q_ref[:, k : k + step], preferred_element_type=F32)
        payload_ref[:, k : k + step] = part.astype(BF16)
    payload_ref[:, width:] = extra_ref[...].astype(BF16)


def sort_tokens(queries, order, extra):
    tokens, width = queries.shape
    here = pl.BlockSpec(memory_space=pltpu.VMEM)
    return pl.pallas_call(
        sort_kernel,
        out_shape=jax.ShapeDtypeStruct((tokens, width + extra.shape[1]), BF16),
        in_specs=[here] * 3,
        out_specs=here,
        compiler_params=pltpu.CompilerParams(vmem_limit_bytes=24 << 20),
        name="sort_tokens",
    )(queries, order, extra)


def work_list(wanted):
    tiles = wanted.shape[-1]
    flags = wanted.reshape(-1) > 0
    size = flags.shape[0]
    place = jnp.arange(size, dtype=jnp.int32)
    rank = jnp.sum((place[None, :] < place[:, None]) & flags[None, :], axis=1)
    count = jnp.sum(flags.astype(jnp.int32))
    code = place // tiles * 8 + place % tiles + 1
    slot = jnp.arange(size + 3, dtype=jnp.int32)
    chosen = (rank[None, :] == slot[:, None]) & flags[None, :]
    items = jnp.sum(jnp.where(chosen, code[None, :], 0), axis=1)
    items = jnp.where(items > 0, items - 1, 4)
    return items.astype(jnp.int32), count.reshape(1)


def combined(order_ref, parts, out_ref, hd, group):
    width = group * hd
    sums = []
    for ref in parts:
        pieces = ref[:, width:].astype(F32)
        sums.append(pieces[:, :group] + pieces[:, group : 2 * group] + pieces[:, 2 * group : 3 * group])
    top = jnp.maximum(jnp.maximum(sums[0], sums[1]), jnp.maximum(sums[2], sums[3]))
    shares = [jnp.exp(s - top) for s in sums]
    total = shares[0] + shares[1] + shares[2] + shares[3]
    shares = [s / total for s in shares]
    for h in range(group):
        at = slice(h * hd, (h + 1) * hd)
        mixed = parts[0][:, at].astype(F32) * shares[0][:, h : h + 1]
        for ref, share in zip(parts[1:], shares[1:]):
            mixed = mixed + ref[:, at].astype(F32) * share[:, h : h + 1]
        placed = lax.dot_general(
            order_ref[...], mixed.astype(BF16), (((0,), (0,)), ((), ())), preferred_element_type=F32
        )
        out_ref[:, at] = placed.astype(BF16)


def project_kernel(columns, *refs, hd, group, pieces, merge):
    sources = refs[: 5 if merge else 1]
    w_ref = refs[len(sources)]
    outs = refs[len(sources) + 1 : len(sources) + 1 + len(pieces)]
    held, sems = refs[-2:]
    width = held.shape[2]
    copies = []
    for i in range(sum(pieces)):
        start = pl.multiple_of(columns[i] * width, width)
        copies.append(pltpu.make_async_copy(w_ref.at[:, pl.ds(start, width)], held.at[i], sems.at[i]))
        copies[-1].start()
    if merge:
        attended = refs[len(sources) + 1 + len(pieces)]
        combined(sources[0], sources[1:], attended, hd, group)
    else:
        attended = sources[0]
    i = 0
    for out_ref, count in zip(outs, pieces):
        for c in range(count):
            copies[i].wait()
            term = jnp.dot(attended[...], held[i], preferred_element_type=F32)
            out_ref[:, c * width : (c + 1) * width] = term.astype(BF16)
            i += 1


def project(sources, weight, columns, pieces, width, hd):
    merge = len(sources) > 1
    tokens = sources[-1].shape[0]
    depth = weight.shape[0]
    total = sum(pieces)
    here = pl.BlockSpec(memory_space=pltpu.VMEM)
    results = [jax.ShapeDtypeStruct((tokens, width * count), BF16) for count in pieces]
    if merge:
        results.append(jax.ShapeDtypeStruct((tokens, depth), BF16))
    return pl.pallas_call(
        lambda *refs: project_kernel(*refs, hd=hd, group=depth // hd, pieces=pieces, merge=merge),
        out_shape=results,
        grid_spec=pltpu.PrefetchScalarGridSpec(
            num_scalar_prefetch=1,
            grid=(),
            in_specs=[here] * len(sources) + [pl.BlockSpec(memory_space=pl.ANY)],
            out_specs=[here] * len(results),
            scratch_shapes=[
                pltpu.VMEM((total, depth, width), BF16),
                pltpu.SemaphoreType.DMA((total,)),
            ],
        ),
        cost_estimate=pl.CostEstimate(
            flops=2 * tokens * depth * width * total, bytes_accessed=4 * depth * width * total, transcendentals=0
        ),
        compiler_params=pltpu.CompilerParams(vmem_limit_bytes=50 << 20),
        name="project",
    )(jnp.stack(columns).astype(jnp.int32), *sources, weight)


def add_kernel(*refs, count):
    parts, send_ref, keep_ref = refs[:count], refs[-2], refs[-1]
    total = parts[0][...].astype(F32)
    for ref in parts[1:]:
        total = total + ref[...].astype(F32)
    cut = send_ref.shape[1]
    send_ref[...] = total[:, :cut].astype(BF16)
    keep_ref[...] = total[:, cut:]


def add_up(parts, keep):
    tokens, width = parts[0].shape
    return pl.pallas_call(
        lambda *refs: add_kernel(*refs, count=len(parts)),
        out_shape=[
            jax.ShapeDtypeStruct((tokens, width - keep), BF16),
            jax.ShapeDtypeStruct((tokens, keep), F32),
        ],
        compiler_params=pltpu.CompilerParams(vmem_limit_bytes=24 << 20),
        name="add_up",
    )(*parts)


def settle_kernel(gate_ref, layer_ref, *refs):
    parts, out_ref = refs[:-1], refs[-1]
    half = out_ref.shape[1] // 2
    for at, some in ((slice(0, half), parts[:2]), (slice(half, None), parts[2:])):
        total = some[0][...]
        for ref in some[1:]:
            total = total + ref[...].astype(F32)
        out_ref[:, at] = (layer_ref[:, at].astype(F32) + gate_ref[0] * total).astype(BF16)


def settle(gate, layer, parts):
    tokens, width = layer.shape
    cuts = 2
    rows = tokens // cuts
    wide = pl.BlockSpec((rows, width), lambda g: (g, 0))
    part = pl.BlockSpec((rows, width // 2), lambda g: (g, 0))
    return pl.pallas_call(
        settle_kernel,
        out_shape=jax.ShapeDtypeStruct((tokens, width), BF16),
        grid=(cuts,),
        in_specs=[pl.BlockSpec(memory_space=pltpu.SMEM), wide] + [part] * len(parts),
        out_specs=wide,
        compiler_params=pltpu.CompilerParams(vmem_limit_bytes=24 << 20),
        name="settle",
    )(gate, layer, *parts)


def shards(
    queries, image_keys, image_values, layer_input, out_weight, tile_counts, image_range, attn_gate
):
    tokens, width = queries.shape
    keys, hd = image_keys.shape
    y, x, core = (lax.axis_index(n) for n in SEQ)
    z, yh = (lax.axis_index(n) for n in HEAD)
    ny, nx, nc = (lax.axis_size(n) for n in SEQ)
    nz, nyh = (lax.axis_size(n) for n in HEAD)

    padded = -(-keys // 128) * 128
    own = pack(image_keys, image_values, padded)
    across = shifted(own, "y", 1)
    beside = shifted(own, "core", 1)
    low, high = image_range[0], image_range[1]
    grade = jnp.where(low < high, low * 16 + high, 1 << 10)
    place = jnp.arange(tokens, dtype=jnp.int32)
    ahead = (grade[None, :] < grade[:, None]) | (
        (grade[None, :] == grade[:, None]) & (place[None, :] < place[:, None])
    )
    rank = jnp.sum(ahead.astype(jnp.int32), axis=1)
    order = (rank[None, :] == place[:, None]).astype(BF16)
    image = jnp.arange(tile_counts.shape[0])
    ends = jnp.sum(jnp.where(image[None, :] <= image[:, None], tile_counts[None, :], 0), axis=1)
    tile = jnp.arange(ny * nx * nc, dtype=jnp.int32)
    owner = jnp.sum((ends[None, :] <= tile[:, None]).astype(jnp.int32), axis=1)
    hits = (low[:, None] <= owner[None, :]) & (owner[None, :] < high[:, None])
    same = (place[:, None] // CHUNK == rank[None, :] // CHUNK).astype(BF16)
    live = jnp.dot(same, hits.astype(BF16), preferred_element_type=F32) > 0
    span = jnp.dot(order, image_range.astype(BF16).T, preferred_element_type=F32)
    extra = jnp.concatenate(
        [
            jnp.pad(span, ((0, 0), (0, 14))),
            jnp.pad(live.astype(F32), ((0, 0), (0, hd - 16 - tile.shape[0]))),
        ],
        axis=1,
    )
    payload = sort_tokens(queries, order, extra)
    payload, beside = lax.optimization_barrier((payload, beside))
    payloads = {s: shifted(payload, "x", s) for s in (2, 1, 3)}
    payloads[0] = payload
    diagonal = shifted(across, "core", 1)
    tiles = (own, beside, across, diagonal)

    def number(yy, cc):
        return (yy % ny * nx + x) * nc + cc % nc

    held = jnp.stack([number(y, core), number(y, core + 1), number(y + 1, core), number(y + 1, core + 1)])
    mine = (held[:, None] == tile[None, :]).astype(jnp.int32)
    images = jnp.sum(mine * owner[None, :], axis=1)

    parts = {}
    for turns in GROUPS:
        if parts:
            images = lax.optimization_barrier((images, *parts.values()))[0]
        flags = jnp.concatenate([payloads[s][::CHUNK, width + 16 : width + 32] for s in turns], axis=0)
        wanted = jnp.sum(flags.astype(jnp.int32)[:, None, :] * mine[None, :, :], axis=2)
        items, count = work_list(wanted)
        got = attend(
            [payloads[s] for s in turns],
            items,
            count,
            images,
            tiles,
            keys,
            tokens,
            hd,
        )
        parts.update(zip(turns, got))
    parts = {s: part if s == 0 else shifted(part, "x", nx - s) for s, part in parts.items()}

    half = width // 2

    def first(dz, dy):
        return ((z + dz) % nz * nyh + (yh + dy) % nyh) * 2

    sources = [order] + [parts[s] for s in (2, 1, 3, 0)]
    over_y, attended = project(
        sources, out_weight, [first(dz, 1) + 1 for dz in (1, 2, 3, 0)], (4,), half, hd
    )
    got_y = shifted(over_y, "yh", 1)
    far = [first(dz, dy) for dz in (2, 1) for dy in (1, 0)]
    over_z = project([attended], out_weight, far, (2, 2), half, hd)
    got_z = [shifted(term, "z", dz) for dz, term in zip((2, 1), over_z)]
    (last_z,) = project([attended], out_weight, [first(3, 1), first(3, 0)], (2,), half, hd)
    got_z.append(shifted(last_z, "z", 3))
    near = [first(0, 1), first(0, 0)] + [first(dz, 0) + 1 for dz in (1, 2, 3, 0)]
    own_z, own_y = project([attended], out_weight, near, (2, 4), half, hd)
    late_z, kept_b = add_up([own_y, got_y], half)
    ends_b = [shifted(late_z[:, i * half : (i + 1) * half], "z", i + 1) for i in (1, 0, 2)]
    late_y, kept_a = add_up([own_z] + got_z[::-1], half)
    end_a = shifted(late_y, "yh", 1)
    return settle(jnp.tanh(attn_gate), layer_input, [kept_a, end_a, kept_b] + ends_b)


def solution(mesh):
    split = Mesh(mesh.devices.reshape(2, 4, 2, 4, 2), ("y", "x", "core", "z", "yh"))
    return jax.shard_map(
        shards,
        mesh=split,
        in_specs=(
            P(SEQ, HEAD),
            P(SEQ, HEAD),
            P(SEQ, HEAD),
            P(SEQ, HEAD),
            P(HEAD, None),
            P(),
            P(None, SEQ),
            P(),
        ),
        out_specs=P(SEQ, HEAD),
        check_vma=False,
    )
```

```python
import math

import jax
import jax.numpy as jnp
from jax import lax
from jax.experimental import pallas as pl
from jax.experimental.pallas import tpu as pltpu
from jax.sharding import Mesh
from jax.sharding import PartitionSpec as P

SEQ = ("y", "x", "core")
HEAD = ("z", "yh")
CHUNK = 32
GROUPS = ((2, 1, 3), (0,))
LOWEST = -1e30
BLOCKED = 1e30
BF16 = jnp.bfloat16
F32 = jnp.float32


def shifted(value, axis, steps):
    count = lax.axis_size(axis)
    return lax.ppermute(value, axis, [(s, (s + steps) % count) for s in range(count)])


def head_shifted(value, dz, dy):
    nz, ny = lax.axis_size("z"), lax.axis_size("yh")
    pairs = []
    for z in range(nz):
        for y in range(ny):
            pairs.append((z * ny + y, (z + dz) % nz * ny + (y + dy) % ny))
    return lax.ppermute(value, HEAD, pairs)


def attend_kernel(items, count, images, *refs, scale, hd, group, blocks, keys, padded):
    q_refs = refs[:blocks]
    tile_refs = refs[blocks : blocks + 4]
    out_refs = refs[blocks + 4 : 2 * blocks + 4]
    q_all, key_all, value_in, value_all, first_s, second_s, first_b, second_b, top_ref, acc_ref, sems = refs[
        2 * blocks + 4 :
    ]
    tokens = out_refs[0].shape[0]
    rows = CHUNK * group
    width = group * hd
    factor = scale * math.log2(math.e)
    copies = []
    for j in range(4):
        copies.append(
            pltpu.make_async_copy(tile_refs[j].at[pl.ds(0, hd)], key_all.at[j], sems.at[2 * j])
        )
        copies.append(
            pltpu.make_async_copy(tile_refs[j].at[pl.ds(hd, hd)], value_in.at[j], sems.at[2 * j + 1])
        )
    for i in range(blocks):
        copies.append(
            pltpu.make_async_copy(
                q_refs[i], q_all.at[pl.ds(i * tokens, tokens)], sems.at[8 + i]
            )
        )
    for copy in copies:
        copy.start()
    place = lax.broadcasted_iota(jnp.int32, (padded, hd), 0)
    ones = jnp.where(place < keys, 1.0, 0.0).astype(BF16)
    for j in range(4):
        value_all[j, :, hd:] = ones
    top_ref[...] = jnp.full(top_ref.shape, LOWEST, F32)
    acc_ref[...] = jnp.zeros(acc_ref.shape, F32)
    for copy in copies:
        copy.wait()
    for j in range(4):
        for k in range(0, padded, hd):
            value_all[j, k : k + hd, :hd] = value_in[j, :, k : k + hd]

    def where_is(i):
        item = items[i]
        return item // 8, item % 4, jnp.where(item % 8 < 4, images[item % 4], -1)

    def score(i, scores_ref, best_ref):
        chunk, j, _ = where_is(i)
        at = pl.ds(pl.multiple_of(chunk * CHUNK, CHUNK), CHUNK)
        q = jnp.concatenate([q_all[at, h * hd : (h + 1) * hd] for h in range(group)], axis=0)
        best = None
        for k in range(0, padded, 128):
            part = jnp.dot(q, key_all[j, :, k : k + 128], preferred_element_type=F32)
            scores_ref[:, k : k + 128] = part
            best = part if best is None else jnp.maximum(best, part)
        best_ref[...] = jnp.broadcast_to(jnp.max(best, axis=1, keepdims=True), best_ref.shape)

    def absorb(i, scores_ref, best_ref):
        chunk, j, image = where_is(i)
        at = pl.ds(pl.multiple_of(chunk * rows, rows), rows)
        near = pl.ds(pl.multiple_of(chunk * CHUNK, CHUNK), CHUNK)
        reach = q_all[near, width : width + hd].astype(F32)
        low = jnp.concatenate([reach[:, 0:1]] * group, axis=0)
        high = jnp.concatenate([reach[:, 1:2]] * group, axis=0)
        number = image.astype(F32)
        allowed = (low <= number) & (number < high)
        old = top_ref[at, 0:1]
        new = jnp.where(allowed, jnp.maximum(old, best_ref[:, 0:1]), old)
        anchor = jnp.where(allowed, new, BLOCKED)
        rescale = jnp.exp2((old - new) * factor)
        top_ref[at, :] = jnp.broadcast_to(new, (rows, hd))
        weights = jnp.exp2((scores_ref[...] - anchor) * factor).astype(BF16)
        mixed = jnp.dot(weights, value_all[j], preferred_element_type=F32)
        acc_ref[at, :] = acc_ref[at, :] * rescale + mixed

    def pair(k, carry):
        i = 2 * k
        score(i + 1, second_s, second_b)
        absorb(i, first_s, first_b)
        score(i + 2, first_s, first_b)
        absorb(i + 1, second_s, second_b)
        return carry

    score(0, first_s, first_b)
    lax.fori_loop(0, (count[0] + 1) // 2, pair, 0)

    lane = lax.broadcasted_iota(jnp.int32, (CHUNK, hd), 1)
    for c in range(blocks * tokens // CHUNK):
        out_ref = out_refs[c * CHUNK // tokens]
        near = pl.ds(c * CHUNK % tokens, CHUNK)
        totals = jnp.zeros((CHUNK, hd), F32)
        tops = jnp.zeros((CHUNK, hd), F32)
        for h in range(group):
            at = pl.ds(c * rows + h * CHUNK, CHUNK)
            total = acc_ref[at, hd:]
            safe = jnp.where(total > 0, total, 1.0)
            out_ref[near, h * hd : (h + 1) * hd] = (acc_ref[at, :hd] / safe).astype(BF16)
            totals = jnp.where(lane % group == h, total, totals)
            tops = jnp.where(lane % group == h, top_ref[at, :], tops)
        seen = totals > 0
        logsum = jnp.where(seen, tops * scale + jnp.log(jnp.where(seen, totals, 1.0)), LOWEST)
        hi = logsum.astype(BF16).astype(F32)
        mid = (logsum - hi).astype(BF16).astype(F32)
        lo = logsum - hi - mid
        pieces = jnp.where(lane < group, hi, jnp.where(lane < 2 * group, mid, lo))
        out_ref[near, width:] = pieces.astype(BF16)


def attend(payloads, items, count, images, tiles, keys, tokens, hd):
    blocks = len(payloads)
    wide = payloads[0].shape[1]
    padded = tiles[0].shape[1]
    width = wide - hd
    group = width // hd
    rows = CHUNK * group
    apart = pl.BlockSpec(memory_space=pl.ANY)
    here = pl.BlockSpec(memory_space=pltpu.VMEM)
    return pl.pallas_call(
        lambda *refs: attend_kernel(
            *refs,
            scale=1.0 / math.sqrt(hd),
            hd=hd,
            group=group,
            blocks=blocks,
            keys=keys,
            padded=padded,
        ),
        out_shape=[jax.ShapeDtypeStruct((tokens, wide), BF16)] * blocks,
        grid_spec=pltpu.PrefetchScalarGridSpec(
            num_scalar_prefetch=3,
            grid=(),
            in_specs=[apart] * (blocks + 4),
            out_specs=[here] * blocks,
            scratch_shapes=[
                pltpu.VMEM((blocks * tokens, wide), BF16),
                pltpu.VMEM((4, hd, padded), BF16),
                pltpu.VMEM((4, hd, padded), BF16),
                pltpu.VMEM((4, padded, 2 * hd), BF16),
                pltpu.VMEM((rows, padded), F32),
                pltpu.VMEM((rows, padded), F32),
                pltpu.VMEM((rows, hd), F32),
                pltpu.VMEM((rows, hd), F32),
                pltpu.VMEM((blocks * tokens * group, hd), F32),
                pltpu.VMEM((blocks * tokens * group, 2 * hd), F32),
                pltpu.SemaphoreType.DMA((8 + blocks,)),
            ],
        ),
        compiler_params=pltpu.CompilerParams(vmem_limit_bytes=32 << 20),
        cost_estimate=pl.CostEstimate(
            flops=2 * blocks * tokens * group * padded * 2 * hd,
            bytes_accessed=blocks * tokens * width * 4 + padded * hd * 16,
            transcendentals=blocks * tokens * group * padded * 2,
        ),
        name="attend",
    )(items, count, images, *payloads, *tiles)


def prepare_kernel(
    counts, range_ref, key_hbm, value_hbm, q_hbm, tile_ref, payload_ref, back_ref, key_ref, value_ref, q_ref, sems
):
    copies = [
        pltpu.make_async_copy(key_hbm, key_ref, sems.at[0]),
        pltpu.make_async_copy(value_hbm, value_ref, sems.at[1]),
        pltpu.make_async_copy(q_hbm, q_ref, sems.at[2]),
    ]
    for copy in copies:
        copy.start()
    tokens, width = q_ref.shape
    keys, hd = key_ref.shape
    square = (tokens, tokens)
    down = lax.broadcasted_iota(jnp.int32, square, 0)
    along = lax.broadcasted_iota(jnp.int32, square, 1)
    rows = range_ref[...].astype(F32)
    low_row = jnp.broadcast_to(rows[0:1], square)
    high_row = jnp.broadcast_to(rows[1:2], square)
    same = down == along
    low = jnp.sum(jnp.where(same, low_row, 0.0), axis=1, keepdims=True)
    high = jnp.sum(jnp.where(same, high_row, 0.0), axis=1, keepdims=True)
    grade_row = jnp.where(low_row < high_row, low_row * 16 + high_row, 1024.0)
    grade = jnp.where(low < high, low * 16 + high, 1024.0)
    equal = grade == grade_row
    before = (grade < grade_row) | (equal & (down < along))
    after = (grade_row < grade) | (equal & (along < down))
    rank_row = jnp.sum(jnp.where(before, 1.0, 0.0), axis=0, keepdims=True)
    rank = jnp.sum(jnp.where(after, 1.0, 0.0), axis=1, keepdims=True)
    order = jnp.where(rank_row == down.astype(F32), 1.0, 0.0).astype(BF16)
    back_ref[...] = jnp.where(rank == along.astype(F32), 1.0, 0.0).astype(BF16)
    lane = lax.broadcasted_iota(jnp.int32, (tokens, hd), 1)
    owner = jnp.zeros((tokens, hd), F32)
    end = 0
    for i in range(counts.shape[0]):
        end = end + counts[i]
        owner = owner + jnp.where(lane - 16 >= end, 1.0, 0.0)
    hits = (low <= owner) & (owner < high) & (lane >= 16) & (lane < 32)
    extra = jnp.where(lane == 0, low, jnp.where(lane == 1, high, jnp.where(hits, 1.0, 0.0)))
    placed = jnp.dot(order, extra.astype(BF16), preferred_element_type=F32)
    group = jnp.where(down // CHUNK == along // CHUNK, 1.0, 0.0).astype(BF16)
    crowd = jnp.dot(group, placed.astype(BF16), preferred_element_type=F32)
    live = jnp.where(crowd > 0, 1.0, 0.0)
    payload_ref[:, width:] = jnp.where(lane < 2, placed, live).astype(BF16)
    for copy in copies:
        copy.wait()
    step = 2 * hd
    for k in range(0, width, step):
        part = jnp.dot(order, q_ref[:, k : k + step], preferred_element_type=F32)
        payload_ref[:, k : k + step] = part.astype(BF16)
    whole = keys // hd * hd
    mid = keys // 16 * 16
    padded = tile_ref.shape[1]
    for k in range(0, whole, hd):
        block = key_ref[k : k + hd].astype(F32)
        tile_ref[:hd, k : k + hd] = block.T.astype(BF16)
        tile_ref[hd:, k : k + hd] = value_ref[k : k + hd]
    first = lax.broadcasted_iota(jnp.int32, (padded - mid, hd), 0) == 0
    last_key = jnp.where(first, key_ref[mid:keys].astype(F32), key_ref[0:1].astype(F32))
    last_value = jnp.where(first, value_ref[mid:keys].astype(F32), 0.0)
    block = jnp.concatenate([key_ref[whole:mid].astype(F32), last_key], axis=0)
    tile_ref[:hd, whole:] = block.T.astype(BF16)
    block = jnp.concatenate([value_ref[whole:mid].astype(F32), last_value], axis=0)
    tile_ref[hd:, whole:] = block.astype(BF16)


def prepare(counts, image_range, keys, values, queries, padded):
    hd = keys.shape[1]
    tokens, width = queries.shape
    apart = pl.BlockSpec(memory_space=pl.ANY)
    here = pl.BlockSpec(memory_space=pltpu.VMEM)
    return pl.pallas_call(
        prepare_kernel,
        out_shape=[
            jax.ShapeDtypeStruct((2 * hd, padded), BF16),
            jax.ShapeDtypeStruct((tokens, width + hd), BF16),
            jax.ShapeDtypeStruct((tokens, tokens), BF16),
        ],
        in_specs=[pl.BlockSpec(memory_space=pltpu.SMEM), here] + [apart] * 3,
        out_specs=[here] * 3,
        scratch_shapes=[
            pltpu.VMEM(keys.shape, BF16),
            pltpu.VMEM(values.shape, BF16),
            pltpu.VMEM(queries.shape, BF16),
            pltpu.SemaphoreType.DMA((3,)),
        ],
        compiler_params=pltpu.CompilerParams(vmem_limit_bytes=60 << 20),
        name="prepare",
    )(counts, image_range, keys, values, queries)


def work_list(wanted):
    tiles = wanted.shape[-1]
    flags = wanted.reshape(-1) > 0
    size = flags.shape[0]
    place = jnp.arange(size, dtype=jnp.int32)
    rank = jnp.sum((place[None, :] < place[:, None]) & flags[None, :], axis=1)
    count = jnp.sum(flags.astype(jnp.int32))
    code = place // tiles * 8 + place % tiles + 1
    slot = jnp.arange(size + 3, dtype=jnp.int32)
    chosen = (rank[None, :] == slot[:, None]) & flags[None, :]
    items = jnp.sum(jnp.where(chosen, code[None, :], 0), axis=1)
    items = jnp.where(items > 0, items - 1, 4)
    return items.astype(jnp.int32), count.reshape(1)


def combined(back_ref, parts, out_ref, hd, group):
    width = group * hd
    sums = []
    for ref in parts:
        pieces = ref[:, width:].astype(F32)
        sums.append(pieces[:, :group] + pieces[:, group : 2 * group] + pieces[:, 2 * group : 3 * group])
    top = jnp.maximum(jnp.maximum(sums[0], sums[1]), jnp.maximum(sums[2], sums[3]))
    shares = [jnp.exp(s - top) for s in sums]
    total = shares[0] + shares[1] + shares[2] + shares[3]
    shares = [s / total for s in shares]
    for h in range(group):
        at = slice(h * hd, (h + 1) * hd)
        mixed = parts[0][:, at].astype(F32) * shares[0][:, h : h + 1]
        for ref, share in zip(parts[1:], shares[1:]):
            mixed = mixed + ref[:, at].astype(F32) * share[:, h : h + 1]
        out_ref[:, at] = mixed.astype(BF16)
    placed = jnp.dot(back_ref[...], out_ref[...], preferred_element_type=F32)
    out_ref[...] = placed.astype(BF16)


def project_kernel(columns, *refs, hd, group, pieces, merge):
    sources = refs[: 5 if merge else 1]
    w_ref = refs[len(sources)]
    outs = refs[len(sources) + 1 : len(sources) + 1 + len(pieces)]
    held, sems = refs[-2:]
    width = held.shape[2]
    copies = []
    for i in range(sum(pieces)):
        start = pl.multiple_of(columns[i] * width, width)
        copies.append(pltpu.make_async_copy(w_ref.at[:, pl.ds(start, width)], held.at[i], sems.at[i]))
        copies[-1].start()
    if merge:
        attended = refs[len(sources) + 1 + len(pieces)]
        combined(sources[0], sources[1:], attended, hd, group)
    else:
        attended = sources[0]
    i = 0
    for out_ref, count in zip(outs, pieces):
        for c in range(count):
            copies[i].wait()
            term = jnp.dot(attended[...], held[i], preferred_element_type=F32)
            out_ref[:, c * width : (c + 1) * width] = term.astype(BF16)
            i += 1


def project(sources, weight, columns, pieces, width, hd):
    merge = len(sources) > 1
    tokens = sources[-1].shape[0]
    depth = weight.shape[0]
    total = sum(pieces)
    here = pl.BlockSpec(memory_space=pltpu.VMEM)
    results = [jax.ShapeDtypeStruct((tokens, width * count), BF16) for count in pieces]
    if merge:
        results.append(jax.ShapeDtypeStruct((tokens, depth), BF16))
    return pl.pallas_call(
        lambda *refs: project_kernel(*refs, hd=hd, group=depth // hd, pieces=pieces, merge=merge),
        out_shape=results,
        grid_spec=pltpu.PrefetchScalarGridSpec(
            num_scalar_prefetch=1,
            grid=(),
            in_specs=[here] * len(sources) + [pl.BlockSpec(memory_space=pl.ANY)],
            out_specs=[here] * len(results),
            scratch_shapes=[
                pltpu.VMEM((total, depth, width), BF16),
                pltpu.SemaphoreType.DMA((total,)),
            ],
        ),
        cost_estimate=pl.CostEstimate(
            flops=2 * tokens * depth * width * total, bytes_accessed=4 * depth * width * total, transcendentals=0
        ),
        compiler_params=pltpu.CompilerParams(vmem_limit_bytes=50 << 20),
        name="project",
    )(jnp.stack(columns).astype(jnp.int32), *sources, weight)


def add_kernel(*refs, count):
    parts, send_ref, keep_ref = refs[:count], refs[-2], refs[-1]
    total = parts[0][...].astype(F32)
    for ref in parts[1:]:
        total = total + ref[...].astype(F32)
    cut = send_ref.shape[1]
    send_ref[...] = total[:, :cut].astype(BF16)
    keep_ref[...] = total[:, cut:]


def add_up(parts, keep):
    tokens, width = parts[0].shape
    return pl.pallas_call(
        lambda *refs: add_kernel(*refs, count=len(parts)),
        out_shape=[
            jax.ShapeDtypeStruct((tokens, width - keep), BF16),
            jax.ShapeDtypeStruct((tokens, keep), F32),
        ],
        compiler_params=pltpu.CompilerParams(vmem_limit_bytes=24 << 20),
        name="add_up",
    )(*parts)


def settle_kernel(gate_ref, layer_ref, *refs):
    parts, out_ref = refs[:-1], refs[-1]
    half = out_ref.shape[1] // 2
    for at, some in ((slice(0, half), parts[:2]), (slice(half, None), parts[2:])):
        total = some[0][...]
        for ref in some[1:]:
            total = total + ref[...].astype(F32)
        out_ref[:, at] = (layer_ref[:, at].astype(F32) + gate_ref[0] * total).astype(BF16)


def settle(gate, layer, parts):
    tokens, width = layer.shape
    cuts = 2
    rows = tokens // cuts
    wide = pl.BlockSpec((rows, width), lambda g: (g, 0))
    part = pl.BlockSpec((rows, width // 2), lambda g: (g, 0))
    return pl.pallas_call(
        settle_kernel,
        out_shape=jax.ShapeDtypeStruct((tokens, width), BF16),
        grid=(cuts,),
        in_specs=[pl.BlockSpec(memory_space=pltpu.SMEM), wide] + [part] * len(parts),
        out_specs=wide,
        compiler_params=pltpu.CompilerParams(vmem_limit_bytes=24 << 20),
        name="settle",
    )(gate, layer, *parts)


def shards(
    queries, image_keys, image_values, layer_input, out_weight, tile_counts, image_range, attn_gate
):
    tokens, width = queries.shape
    keys, hd = image_keys.shape
    y, x, core = (lax.axis_index(n) for n in SEQ)
    z, yh = (lax.axis_index(n) for n in HEAD)
    ny, nx, nc = (lax.axis_size(n) for n in SEQ)
    nz, nyh = (lax.axis_size(n) for n in HEAD)

    padded = -(-keys // 128) * 128
    own, payload, back = prepare(
        tile_counts, image_range, image_keys, image_values, queries, padded
    )
    across = shifted(own, "y", 1)
    image = jnp.arange(tile_counts.shape[0])
    ends = jnp.sum(jnp.where(image[None, :] <= image[:, None], tile_counts[None, :], 0), axis=1)
    tile = jnp.arange(ny * nx * nc, dtype=jnp.int32)
    owner = jnp.sum((ends[None, :] <= tile[:, None]).astype(jnp.int32), axis=1)
    payloads = {s: shifted(payload, "x", s) for s in (2, 1, 3)}
    payloads[0] = payload
    beside = shifted(own, "core", 1)
    diagonal = shifted(across, "core", 1)
    tiles = (own, beside, across, diagonal)

    def number(yy, cc):
        return (yy % ny * nx + x) * nc + cc % nc

    held = jnp.stack([number(y, core), number(y, core + 1), number(y + 1, core), number(y + 1, core + 1)])
    mine = (held[:, None] == tile[None, :]).astype(jnp.int32)
    images = jnp.sum(mine * owner[None, :], axis=1)

    parts = {}
    for turns in GROUPS:
        if parts:
            images = lax.optimization_barrier((images, *parts.values()))[0]
        flags = jnp.concatenate([payloads[s][::CHUNK, width + 16 : width + 32] for s in turns], axis=0)
        wanted = jnp.sum(flags.astype(jnp.int32)[:, None, :] * mine[None, :, :], axis=2)
        items, count = work_list(wanted)
        got = attend(
            [payloads[s] for s in turns],
            items,
            count,
            images,
            tiles,
            keys,
            tokens,
            hd,
        )
        parts.update(zip(turns, got))
    parts = {s: part if s == 0 else shifted(part, "x", nx - s) for s, part in parts.items()}

    half = width // 2

    def first(dz, dy):
        return ((z + dz) % nz * nyh + (yh + dy) % nyh) * 2

    sources = [back] + [parts[s] for s in (2, 1, 3, 0)]
    over_y, attended = project(
        sources, out_weight, [first(dz, 1) + 1 for dz in (1, 2, 3, 0)], (4,), half, hd
    )
    got_y = shifted(over_y, "yh", 1)
    far = [first(dz, dy) for dz in (2, 1) for dy in (1, 0)]
    over_z = project([attended], out_weight, far, (2, 2), half, hd)
    got_z = [shifted(term, "z", dz) for dz, term in zip((2, 1), over_z)]
    (last_z,) = project([attended], out_weight, [first(3, 1), first(3, 0)], (2,), half, hd)
    got_z.append(shifted(last_z, "z", 3))
    near = [first(0, 1), first(0, 0)] + [first(dz, 0) + 1 for dz in (1, 2, 3, 0)]
    own_z, own_y = project([attended], out_weight, near, (2, 4), half, hd)
    late_z, kept_b = add_up([own_y, got_y], half)
    ends_b = [shifted(late_z[:, i * half : (i + 1) * half], "z", i + 1) for i in (1, 0, 2)]
    late_y, kept_a = add_up([own_z] + got_z[::-1], half)
    end_a = shifted(late_y, "yh", 1)
    return settle(jnp.tanh(attn_gate), layer_input, [kept_a, end_a, kept_b] + ends_b)


def solution(mesh):
    split = Mesh(mesh.devices.reshape(2, 4, 2, 4, 2), ("y", "x", "core", "z", "yh"))
    return jax.shard_map(
        shards,
        mesh=split,
        in_specs=(
            P(SEQ, HEAD),
            P(SEQ, HEAD),
            P(SEQ, HEAD),
            P(SEQ, HEAD),
            P(HEAD, None),
            P(),
            P(None, SEQ),
            P(),
        ),
        out_specs=P(SEQ, HEAD),
        check_vma=False,
    )
```

```python
import math

import jax
import jax.numpy as jnp
from jax import lax
from jax.experimental import pallas as pl
from jax.experimental.pallas import tpu as pltpu
from jax.sharding import Mesh
from jax.sharding import PartitionSpec as P

SEQ = ("y", "x", "core")
HEAD = ("z", "yh")
CHUNK = 32
GROUPS = ((2,), (1, 3), (0,))
LOWEST = -1e30
BLOCKED = 1e30
BF16 = jnp.bfloat16
F32 = jnp.float32


def shifted(value, axis, steps):
    count = lax.axis_size(axis)
    return lax.ppermute(value, axis, [(s, (s + steps) % count) for s in range(count)])


def head_shifted(value, dz, dy):
    nz, ny = lax.axis_size("z"), lax.axis_size("yh")
    pairs = []
    for z in range(nz):
        for y in range(ny):
            pairs.append((z * ny + y, (z + dz) % nz * ny + (y + dy) % ny))
    return lax.ppermute(value, HEAD, pairs)


def attend_kernel(items, count, images, *refs, scale, hd, group, blocks, keys, padded):
    q_refs = refs[:blocks]
    tile_refs = refs[blocks : blocks + 4]
    out_refs = refs[blocks + 4 : 2 * blocks + 4]
    q_all, key_all, value_in, value_all, first_s, second_s, first_b, second_b, top_ref, acc_ref, sems = refs[
        2 * blocks + 4 :
    ]
    tokens = out_refs[0].shape[0]
    rows = CHUNK * group
    width = group * hd
    factor = scale * math.log2(math.e)
    copies = []
    for j in range(4):
        copies.append(
            pltpu.make_async_copy(tile_refs[j].at[pl.ds(0, hd)], key_all.at[j], sems.at[2 * j])
        )
        copies.append(
            pltpu.make_async_copy(tile_refs[j].at[pl.ds(hd, hd)], value_in.at[j], sems.at[2 * j + 1])
        )
    for i in range(blocks):
        copies.append(
            pltpu.make_async_copy(
                q_refs[i], q_all.at[pl.ds(i * tokens, tokens)], sems.at[8 + i]
            )
        )
    for copy in copies:
        copy.start()
    place = lax.broadcasted_iota(jnp.int32, (padded, hd), 0)
    ones = jnp.where(place < keys, 1.0, 0.0).astype(BF16)
    for j in range(4):
        value_all[j, :, hd:] = ones
    top_ref[...] = jnp.full(top_ref.shape, LOWEST, F32)
    acc_ref[...] = jnp.zeros(acc_ref.shape, F32)
    for copy in copies:
        copy.wait()
    for j in range(4):
        for k in range(0, padded, hd):
            value_all[j, k : k + hd, :hd] = value_in[j, :, k : k + hd]

    def where_is(i):
        item = items[i]
        return item // 8, item % 4, jnp.where(item % 8 < 4, images[item % 4], -1)

    def score(i, scores_ref, best_ref):
        chunk, j, _ = where_is(i)
        at = pl.ds(pl.multiple_of(chunk * CHUNK, CHUNK), CHUNK)
        q = jnp.concatenate([q_all[at, h * hd : (h + 1) * hd] for h in range(group)], axis=0)
        best = None
        for k in range(0, padded, 128):
            part = jnp.dot(q, key_all[j, :, k : k + 128], preferred_element_type=F32)
            scores_ref[:, k : k + 128] = part
            best = part if best is None else jnp.maximum(best, part)
        best_ref[...] = jnp.broadcast_to(jnp.max(best, axis=1, keepdims=True), best_ref.shape)

    def absorb(i, scores_ref, best_ref):
        chunk, j, image = where_is(i)
        at = pl.ds(pl.multiple_of(chunk * rows, rows), rows)
        near = pl.ds(pl.multiple_of(chunk * CHUNK, CHUNK), CHUNK)
        reach = q_all[near, width : width + hd].astype(F32)
        low = jnp.concatenate([reach[:, 0:1]] * group, axis=0)
        high = jnp.concatenate([reach[:, 1:2]] * group, axis=0)
        number = image.astype(F32)
        allowed = (low <= number) & (number < high)
        old = top_ref[at, 0:1]
        new = jnp.where(allowed, jnp.maximum(old, best_ref[:, 0:1]), old)
        anchor = jnp.where(allowed, new, BLOCKED)
        rescale = jnp.exp2((old - new) * factor)
        top_ref[at, :] = jnp.broadcast_to(new, (rows, hd))
        weights = jnp.exp2((scores_ref[...] - anchor) * factor).astype(BF16)
        mixed = jnp.dot(weights, value_all[j], preferred_element_type=F32)
        acc_ref[at, :] = acc_ref[at, :] * rescale + mixed

    def pair(k, carry):
        i = 2 * k
        score(i + 1, second_s, second_b)
        absorb(i, first_s, first_b)
        score(i + 2, first_s, first_b)
        absorb(i + 1, second_s, second_b)
        return carry

    score(0, first_s, first_b)
    lax.fori_loop(0, (count[0] + 1) // 2, pair, 0)

    lane = lax.broadcasted_iota(jnp.int32, (CHUNK, hd), 1)
    for c in range(blocks * tokens // CHUNK):
        out_ref = out_refs[c * CHUNK // tokens]
        near = pl.ds(c * CHUNK % tokens, CHUNK)
        totals = jnp.zeros((CHUNK, hd), F32)
        tops = jnp.zeros((CHUNK, hd), F32)
        for h in range(group):
            at = pl.ds(c * rows + h * CHUNK, CHUNK)
            total = acc_ref[at, hd:]
            safe = jnp.where(total > 0, total, 1.0)
            out_ref[near, h * hd : (h + 1) * hd] = (acc_ref[at, :hd] / safe).astype(BF16)
            totals = jnp.where(lane % group == h, total, totals)
            tops = jnp.where(lane % group == h, top_ref[at, :], tops)
        seen = totals > 0
        logsum = jnp.where(seen, tops * scale + jnp.log(jnp.where(seen, totals, 1.0)), LOWEST)
        hi = logsum.astype(BF16).astype(F32)
        mid = (logsum - hi).astype(BF16).astype(F32)
        lo = logsum - hi - mid
        pieces = jnp.where(lane < group, hi, jnp.where(lane < 2 * group, mid, lo))
        out_ref[near, width:] = pieces.astype(BF16)


def attend(payloads, items, count, images, tiles, keys, tokens, hd):
    blocks = len(payloads)
    wide = payloads[0].shape[1]
    padded = tiles[0].shape[1]
    width = wide - hd
    group = width // hd
    rows = CHUNK * group
    apart = pl.BlockSpec(memory_space=pl.ANY)
    here = pl.BlockSpec(memory_space=pltpu.VMEM)
    return pl.pallas_call(
        lambda *refs: attend_kernel(
            *refs,
            scale=1.0 / math.sqrt(hd),
            hd=hd,
            group=group,
            blocks=blocks,
            keys=keys,
            padded=padded,
        ),
        out_shape=[jax.ShapeDtypeStruct((tokens, wide), BF16)] * blocks,
        grid_spec=pltpu.PrefetchScalarGridSpec(
            num_scalar_prefetch=3,
            grid=(),
            in_specs=[apart] * (blocks + 4),
            out_specs=[here] * blocks,
            scratch_shapes=[
                pltpu.VMEM((blocks * tokens, wide), BF16),
                pltpu.VMEM((4, hd, padded), BF16),
                pltpu.VMEM((4, hd, padded), BF16),
                pltpu.VMEM((4, padded, 2 * hd), BF16),
                pltpu.VMEM((rows, padded), F32),
                pltpu.VMEM((rows, padded), F32),
                pltpu.VMEM((rows, hd), F32),
                pltpu.VMEM((rows, hd), F32),
                pltpu.VMEM((blocks * tokens * group, hd), F32),
                pltpu.VMEM((blocks * tokens * group, 2 * hd), F32),
                pltpu.SemaphoreType.DMA((8 + blocks,)),
            ],
        ),
        compiler_params=pltpu.CompilerParams(vmem_limit_bytes=32 << 20),
        cost_estimate=pl.CostEstimate(
            flops=2 * blocks * tokens * group * padded * 2 * hd,
            bytes_accessed=blocks * tokens * width * 4 + padded * hd * 16,
            transcendentals=blocks * tokens * group * padded * 2,
        ),
        name="attend",
    )(items, count, images, *payloads, *tiles)


def prepare_kernel(
    counts, range_ref, key_hbm, value_hbm, q_hbm, tile_ref, payload_ref, back_ref, key_ref, value_ref, q_ref, sems
):
    copies = [
        pltpu.make_async_copy(key_hbm, key_ref, sems.at[0]),
        pltpu.make_async_copy(value_hbm, value_ref, sems.at[1]),
        pltpu.make_async_copy(q_hbm, q_ref, sems.at[2]),
    ]
    for copy in copies:
        copy.start()
    tokens, width = q_ref.shape
    keys, hd = key_ref.shape
    square = (tokens, tokens)
    down = lax.broadcasted_iota(jnp.int32, square, 0)
    along = lax.broadcasted_iota(jnp.int32, square, 1)
    rows = range_ref[...].astype(F32)
    low_row = jnp.broadcast_to(rows[0:1], square)
    high_row = jnp.broadcast_to(rows[1:2], square)
    same = down == along
    low = jnp.sum(jnp.where(same, low_row, 0.0), axis=1, keepdims=True)
    high = jnp.sum(jnp.where(same, high_row, 0.0), axis=1, keepdims=True)
    grade_row = jnp.where(low_row < high_row, low_row * 16 + high_row, 1024.0)
    grade = jnp.where(low < high, low * 16 + high, 1024.0)
    equal = grade == grade_row
    before = (grade < grade_row) | (equal & (down < along))
    after = (grade_row < grade) | (equal & (along < down))
    rank_row = jnp.sum(jnp.where(before, 1.0, 0.0), axis=0, keepdims=True)
    rank = jnp.sum(jnp.where(after, 1.0, 0.0), axis=1, keepdims=True)
    order = jnp.where(rank_row == down.astype(F32), 1.0, 0.0).astype(BF16)
    back_ref[...] = jnp.where(rank == along.astype(F32), 1.0, 0.0).astype(BF16)
    lane = lax.broadcasted_iota(jnp.int32, (tokens, hd), 1)
    owner = jnp.zeros((tokens, hd), F32)
    end = 0
    for i in range(counts.shape[0]):
        end = end + counts[i]
        owner = owner + jnp.where(lane - 16 >= end, 1.0, 0.0)
    hits = (low <= owner) & (owner < high) & (lane >= 16) & (lane < 32)
    extra = jnp.where(lane == 0, low, jnp.where(lane == 1, high, jnp.where(hits, 1.0, 0.0)))
    placed = jnp.dot(order, extra.astype(BF16), preferred_element_type=F32)
    group = jnp.where(down // CHUNK == along // CHUNK, 1.0, 0.0).astype(BF16)
    crowd = jnp.dot(group, placed.astype(BF16), preferred_element_type=F32)
    live = jnp.where(crowd > 0, 1.0, 0.0)
    payload_ref[:, width:] = jnp.where(lane < 2, placed, live).astype(BF16)
    for copy in copies:
        copy.wait()
    step = 2 * hd
    for k in range(0, width, step):
        part = jnp.dot(order, q_ref[:, k : k + step], preferred_element_type=F32)
        payload_ref[:, k : k + step] = part.astype(BF16)
    whole = keys // hd * hd
    mid = keys // 16 * 16
    padded = tile_ref.shape[1]
    for k in range(0, whole, hd):
        block = key_ref[k : k + hd].astype(F32)
        tile_ref[:hd, k : k + hd] = block.T.astype(BF16)
        tile_ref[hd:, k : k + hd] = value_ref[k : k + hd]
    first = lax.broadcasted_iota(jnp.int32, (padded - mid, hd), 0) == 0
    last_key = jnp.where(first, key_ref[mid:keys].astype(F32), key_ref[0:1].astype(F32))
    last_value = jnp.where(first, value_ref[mid:keys].astype(F32), 0.0)
    block = jnp.concatenate([key_ref[whole:mid].astype(F32), last_key], axis=0)
    tile_ref[:hd, whole:] = block.T.astype(BF16)
    block = jnp.concatenate([value_ref[whole:mid].astype(F32), last_value], axis=0)
    tile_ref[hd:, whole:] = block.astype(BF16)


def prepare(counts, image_range, keys, values, queries, padded):
    hd = keys.shape[1]
    tokens, width = queries.shape
    apart = pl.BlockSpec(memory_space=pl.ANY)
    here = pl.BlockSpec(memory_space=pltpu.VMEM)
    return pl.pallas_call(
        prepare_kernel,
        out_shape=[
            jax.ShapeDtypeStruct((2 * hd, padded), BF16),
            jax.ShapeDtypeStruct((tokens, width + hd), BF16),
            jax.ShapeDtypeStruct((tokens, tokens), BF16),
        ],
        in_specs=[pl.BlockSpec(memory_space=pltpu.SMEM), here] + [apart] * 3,
        out_specs=[here] * 3,
        scratch_shapes=[
            pltpu.VMEM(keys.shape, BF16),
            pltpu.VMEM(values.shape, BF16),
            pltpu.VMEM(queries.shape, BF16),
            pltpu.SemaphoreType.DMA((3,)),
        ],
        compiler_params=pltpu.CompilerParams(vmem_limit_bytes=60 << 20),
        name="prepare",
    )(counts, image_range, keys, values, queries)


def work_list(wanted):
    tiles = wanted.shape[-1]
    flags = wanted.reshape(-1) > 0
    size = flags.shape[0]
    place = jnp.arange(size, dtype=jnp.int32)
    rank = jnp.sum((place[None, :] < place[:, None]) & flags[None, :], axis=1)
    count = jnp.sum(flags.astype(jnp.int32))
    code = place // tiles * 8 + place % tiles + 1
    slot = jnp.arange(size + 3, dtype=jnp.int32)
    chosen = (rank[None, :] == slot[:, None]) & flags[None, :]
    items = jnp.sum(jnp.where(chosen, code[None, :], 0), axis=1)
    items = jnp.where(items > 0, items - 1, 4)
    return items.astype(jnp.int32), count.reshape(1)


def combined(back_ref, parts, out_ref, hd, group):
    width = group * hd
    sums = []
    for ref in parts:
        pieces = ref[:, width:].astype(F32)
        sums.append(pieces[:, :group] + pieces[:, group : 2 * group] + pieces[:, 2 * group : 3 * group])
    top = jnp.maximum(jnp.maximum(sums[0], sums[1]), jnp.maximum(sums[2], sums[3]))
    shares = [jnp.exp(s - top) for s in sums]
    total = shares[0] + shares[1] + shares[2] + shares[3]
    shares = [s / total for s in shares]
    for h in range(group):
        at = slice(h * hd, (h + 1) * hd)
        mixed = parts[0][:, at].astype(F32) * shares[0][:, h : h + 1]
        for ref, share in zip(parts[1:], shares[1:]):
            mixed = mixed + ref[:, at].astype(F32) * share[:, h : h + 1]
        out_ref[:, at] = mixed.astype(BF16)
    placed = jnp.dot(back_ref[...], out_ref[...], preferred_element_type=F32)
    out_ref[...] = placed.astype(BF16)


def project_kernel(columns, *refs, hd, group, pieces, merge):
    sources = refs[: 5 if merge else 1]
    w_ref = refs[len(sources)]
    outs = refs[len(sources) + 1 : len(sources) + 1 + len(pieces)]
    held, sems = refs[-2:]
    width = held.shape[2]
    copies = []
    for i in range(sum(pieces)):
        start = pl.multiple_of(columns[i] * width, width)
        copies.append(pltpu.make_async_copy(w_ref.at[:, pl.ds(start, width)], held.at[i], sems.at[i]))
        copies[-1].start()
    if merge:
        attended = refs[len(sources) + 1 + len(pieces)]
        combined(sources[0], sources[1:], attended, hd, group)
    else:
        attended = sources[0]
    i = 0
    for out_ref, count in zip(outs, pieces):
        for c in range(count):
            copies[i].wait()
            term = jnp.dot(attended[...], held[i], preferred_element_type=F32)
            out_ref[:, c * width : (c + 1) * width] = term.astype(BF16)
            i += 1


def project(sources, weight, columns, pieces, width, hd):
    merge = len(sources) > 1
    tokens = sources[-1].shape[0]
    depth = weight.shape[0]
    total = sum(pieces)
    here = pl.BlockSpec(memory_space=pltpu.VMEM)
    results = [jax.ShapeDtypeStruct((tokens, width * count), BF16) for count in pieces]
    if merge:
        results.append(jax.ShapeDtypeStruct((tokens, depth), BF16))
    return pl.pallas_call(
        lambda *refs: project_kernel(*refs, hd=hd, group=depth // hd, pieces=pieces, merge=merge),
        out_shape=results,
        grid_spec=pltpu.PrefetchScalarGridSpec(
            num_scalar_prefetch=1,
            grid=(),
            in_specs=[here] * len(sources) + [pl.BlockSpec(memory_space=pl.ANY)],
            out_specs=[here] * len(results),
            scratch_shapes=[
                pltpu.VMEM((total, depth, width), BF16),
                pltpu.SemaphoreType.DMA((total,)),
            ],
        ),
        cost_estimate=pl.CostEstimate(
            flops=2 * tokens * depth * width * total, bytes_accessed=4 * depth * width * total, transcendentals=0
        ),
        compiler_params=pltpu.CompilerParams(vmem_limit_bytes=50 << 20),
        name="project",
    )(jnp.stack(columns).astype(jnp.int32), *sources, weight)


def add_kernel(*refs, count):
    parts, send_ref, keep_ref = refs[:count], refs[-2], refs[-1]
    total = parts[0][...].astype(F32)
    for ref in parts[1:]:
        total = total + ref[...].astype(F32)
    cut = send_ref.shape[1]
    send_ref[...] = total[:, :cut].astype(BF16)
    keep_ref[...] = total[:, cut:]


def add_up(parts, keep):
    tokens, width = parts[0].shape
    return pl.pallas_call(
        lambda *refs: add_kernel(*refs, count=len(parts)),
        out_shape=[
            jax.ShapeDtypeStruct((tokens, width - keep), BF16),
            jax.ShapeDtypeStruct((tokens, keep), F32),
        ],
        compiler_params=pltpu.CompilerParams(vmem_limit_bytes=24 << 20),
        name="add_up",
    )(*parts)


def settle_kernel(gate_ref, layer_ref, *refs):
    parts, out_ref = refs[:-1], refs[-1]
    half = out_ref.shape[1] // 2
    for at, some in ((slice(0, half), parts[:2]), (slice(half, None), parts[2:])):
        total = some[0][...]
        for ref in some[1:]:
            total = total + ref[...].astype(F32)
        out_ref[:, at] = (layer_ref[:, at].astype(F32) + gate_ref[0] * total).astype(BF16)


def settle(gate, layer, parts):
    tokens, width = layer.shape
    cuts = 2
    rows = tokens // cuts
    wide = pl.BlockSpec((rows, width), lambda g: (g, 0))
    part = pl.BlockSpec((rows, width // 2), lambda g: (g, 0))
    return pl.pallas_call(
        settle_kernel,
        out_shape=jax.ShapeDtypeStruct((tokens, width), BF16),
        grid=(cuts,),
        in_specs=[pl.BlockSpec(memory_space=pltpu.SMEM), wide] + [part] * len(parts),
        out_specs=wide,
        compiler_params=pltpu.CompilerParams(vmem_limit_bytes=24 << 20),
        name="settle",
    )(gate, layer, *parts)


def shards(
    queries, image_keys, image_values, layer_input, out_weight, tile_counts, image_range, attn_gate
):
    tokens, width = queries.shape
    keys, hd = image_keys.shape
    y, x, core = (lax.axis_index(n) for n in SEQ)
    z, yh = (lax.axis_index(n) for n in HEAD)
    ny, nx, nc = (lax.axis_size(n) for n in SEQ)
    nz, nyh = (lax.axis_size(n) for n in HEAD)

    padded = -(-keys // 128) * 128
    own, payload, back = prepare(
        tile_counts, image_range, image_keys, image_values, queries, padded
    )
    across = shifted(own, "y", 1)
    image = jnp.arange(tile_counts.shape[0])
    ends = jnp.sum(jnp.where(image[None, :] <= image[:, None], tile_counts[None, :], 0), axis=1)
    tile = jnp.arange(ny * nx * nc, dtype=jnp.int32)
    owner = jnp.sum((ends[None, :] <= tile[:, None]).astype(jnp.int32), axis=1)
    payloads = {s: shifted(payload, "x", s) for s in (2, 1, 3)}
    payloads[0] = payload
    beside = shifted(own, "core", 1)
    diagonal = shifted(across, "core", 1)
    tiles = (own, beside, across, diagonal)

    def number(yy, cc):
        return (yy % ny * nx + x) * nc + cc % nc

    held = jnp.stack([number(y, core), number(y, core + 1), number(y + 1, core), number(y + 1, core + 1)])
    mine = (held[:, None] == tile[None, :]).astype(jnp.int32)
    images = jnp.sum(mine * owner[None, :], axis=1)

    parts = {}
    for turns in GROUPS:
        if parts:
            images = lax.optimization_barrier((images, *parts.values()))[0]
        flags = jnp.concatenate([payloads[s][::CHUNK, width + 16 : width + 32] for s in turns], axis=0)
        wanted = jnp.sum(flags.astype(jnp.int32)[:, None, :] * mine[None, :, :], axis=2)
        items, count = work_list(wanted)
        got = attend(
            [payloads[s] for s in turns],
            items,
            count,
            images,
            tiles,
            keys,
            tokens,
            hd,
        )
        parts.update(zip(turns, got))
    parts = {s: part if s == 0 else shifted(part, "x", nx - s) for s, part in parts.items()}

    half = width // 2

    def first(dz, dy):
        return ((z + dz) % nz * nyh + (yh + dy) % nyh) * 2

    sources = [back] + [parts[s] for s in (2, 1, 3, 0)]
    over_y, attended = project(
        sources, out_weight, [first(dz, 1) + 1 for dz in (1, 2, 3, 0)], (4,), half, hd
    )
    got_y = shifted(over_y, "yh", 1)
    far = [first(dz, dy) for dz in (2, 1, 3) for dy in (1, 0)]
    over_z = project([attended], out_weight, far, (2, 2, 2), half, hd)
    got_z = [shifted(term, "z", dz) for dz, term in zip((2, 1, 3), over_z)]
    near = [first(0, 1), first(0, 0)] + [first(dz, 0) + 1 for dz in (1, 2, 3, 0)]
    own_z, own_y = project([attended], out_weight, near, (2, 4), half, hd)
    late_z, kept_b = add_up([own_y, got_y], half)
    ends_b = [shifted(late_z[:, i * half : (i + 1) * half], "z", i + 1) for i in (1, 0, 2)]
    late_y, kept_a = add_up([own_z] + got_z[::-1], half)
    end_a = shifted(late_y, "yh", 1)
    return settle(jnp.tanh(attn_gate), layer_input, [kept_a, end_a, kept_b] + ends_b)


def solution(mesh):
    split = Mesh(mesh.devices.reshape(2, 4, 2, 4, 2), ("y", "x", "core", "z", "yh"))
    return jax.shard_map(
        shards,
        mesh=split,
        in_specs=(
            P(SEQ, HEAD),
            P(SEQ, HEAD),
            P(SEQ, HEAD),
            P(SEQ, HEAD),
            P(HEAD, None),
            P(),
            P(None, SEQ),
            P(),
        ),
        out_specs=P(SEQ, HEAD),
        check_vma=False,
    )
```

```python
import math

import jax
import jax.numpy as jnp
from jax import lax
from jax.experimental import pallas as pl
from jax.experimental.pallas import tpu as pltpu
from jax.sharding import Mesh
from jax.sharding import PartitionSpec as P

SEQ = ("y", "x", "core")
HEAD = ("z", "yh")
CHUNK = 32
GROUPS = ((2,), (1, 3), (0,))
LOWEST = -1e30
BLOCKED = 1e30
BF16 = jnp.bfloat16
F32 = jnp.float32


def shifted(value, axis, steps):
    count = lax.axis_size(axis)
    return lax.ppermute(value, axis, [(s, (s + steps) % count) for s in range(count)])


def head_shifted(value, dz, dy):
    nz, ny = lax.axis_size("z"), lax.axis_size("yh")
    pairs = []
    for z in range(nz):
        for y in range(ny):
            pairs.append((z * ny + y, (z + dz) % nz * ny + (y + dy) % ny))
    return lax.ppermute(value, HEAD, pairs)


def attend_kernel(items, count, images, *refs, scale, hd, group, blocks, keys, padded):
    q_refs = refs[:blocks]
    tile_refs = refs[blocks : blocks + 4]
    out_refs = refs[blocks + 4 : 2 * blocks + 4]
    q_all, key_all, value_in, value_all, first_s, second_s, first_b, second_b, top_ref, acc_ref, sems = refs[
        2 * blocks + 4 :
    ]
    tokens = out_refs[0].shape[0]
    rows = CHUNK * group
    width = group * hd
    factor = scale * math.log2(math.e)
    copies = []
    for j in range(4):
        copies.append(
            pltpu.make_async_copy(tile_refs[j].at[pl.ds(0, hd)], key_all.at[j], sems.at[2 * j])
        )
    for j in range(4):
        copies.append(
            pltpu.make_async_copy(tile_refs[j].at[pl.ds(hd, hd)], value_in.at[j], sems.at[2 * j + 1])
        )
    for i in range(blocks):
        copies.append(
            pltpu.make_async_copy(
                q_refs[i], q_all.at[pl.ds(i * tokens, tokens)], sems.at[8 + i]
            )
        )
    for copy in copies:
        copy.start()
    place = lax.broadcasted_iota(jnp.int32, (padded, hd), 0)
    ones = jnp.where(place < keys, 1.0, 0.0).astype(BF16)
    for j in range(4):
        value_all[j, :, hd:] = ones
    top_ref[...] = jnp.full(top_ref.shape, LOWEST, F32)
    acc_ref[...] = jnp.zeros(acc_ref.shape, F32)
    for copy in copies[:4] + copies[8:]:
        copy.wait()

    def where_is(i):
        item = items[i]
        return item // 8, item % 4, jnp.where(item % 8 < 4, images[item % 4], -1)

    def score(i, scores_ref, best_ref):
        chunk, j, _ = where_is(i)
        at = pl.ds(pl.multiple_of(chunk * CHUNK, CHUNK), CHUNK)
        q = jnp.concatenate([q_all[at, h * hd : (h + 1) * hd] for h in range(group)], axis=0)
        best = None
        for k in range(0, padded, 128):
            part = jnp.dot(q, key_all[j, :, k : k + 128], preferred_element_type=F32)
            scores_ref[:, k : k + 128] = part
            best = part if best is None else jnp.maximum(best, part)
        best_ref[...] = jnp.broadcast_to(jnp.max(best, axis=1, keepdims=True), best_ref.shape)

    def absorb(i, scores_ref, best_ref):
        chunk, j, image = where_is(i)
        at = pl.ds(pl.multiple_of(chunk * rows, rows), rows)
        near = pl.ds(pl.multiple_of(chunk * CHUNK, CHUNK), CHUNK)
        reach = q_all[near, width : width + hd].astype(F32)
        low = jnp.concatenate([reach[:, 0:1]] * group, axis=0)
        high = jnp.concatenate([reach[:, 1:2]] * group, axis=0)
        number = image.astype(F32)
        allowed = (low <= number) & (number < high)
        old = top_ref[at, 0:1]
        new = jnp.where(allowed, jnp.maximum(old, best_ref[:, 0:1]), old)
        anchor = jnp.where(allowed, new, BLOCKED)
        rescale = jnp.exp2((old - new) * factor)
        top_ref[at, :] = jnp.broadcast_to(new, (rows, hd))
        weights = jnp.exp2((scores_ref[...] - anchor) * factor).astype(BF16)
        mixed = jnp.dot(weights, value_all[j], preferred_element_type=F32)
        acc_ref[at, :] = acc_ref[at, :] * rescale + mixed

    def pair(k, carry):
        i = 2 * k
        score(i + 1, second_s, second_b)
        absorb(i, first_s, first_b)
        score(i + 2, first_s, first_b)
        absorb(i + 1, second_s, second_b)
        return carry

    score(0, first_s, first_b)
    for copy in copies[4:8]:
        copy.wait()
    for j in range(4):
        for k in range(0, padded, hd):
            value_all[j, k : k + hd, :hd] = value_in[j, :, k : k + hd]
    lax.fori_loop(0, (count[0] + 1) // 2, pair, 0)

    lane = lax.broadcasted_iota(jnp.int32, (CHUNK, hd), 1)
    for c in range(blocks * tokens // CHUNK):
        out_ref = out_refs[c * CHUNK // tokens]
        near = pl.ds(c * CHUNK % tokens, CHUNK)
        totals = jnp.zeros((CHUNK, hd), F32)
        tops = jnp.zeros((CHUNK, hd), F32)
        for h in range(group):
            at = pl.ds(c * rows + h * CHUNK, CHUNK)
            total = acc_ref[at, hd:]
            safe = jnp.where(total > 0, total, 1.0)
            out_ref[near, h * hd : (h + 1) * hd] = (acc_ref[at, :hd] / safe).astype(BF16)
            totals = jnp.where(lane % group == h, total, totals)
            tops = jnp.where(lane % group == h, top_ref[at, :], tops)
        seen = totals > 0
        logsum = jnp.where(seen, tops * scale + jnp.log(jnp.where(seen, totals, 1.0)), LOWEST)
        hi = logsum.astype(BF16).astype(F32)
        mid = (logsum - hi).astype(BF16).astype(F32)
        lo = logsum - hi - mid
        pieces = jnp.where(lane < group, hi, jnp.where(lane < 2 * group, mid, lo))
        out_ref[near, width:] = pieces.astype(BF16)


def attend(payloads, items, count, images, tiles, keys, tokens, hd):
    blocks = len(payloads)
    wide = payloads[0].shape[1]
    padded = tiles[0].shape[1]
    width = wide - hd
    group = width // hd
    rows = CHUNK * group
    apart = pl.BlockSpec(memory_space=pl.ANY)
    here = pl.BlockSpec(memory_space=pltpu.VMEM)
    return pl.pallas_call(
        lambda *refs: attend_kernel(
            *refs,
            scale=1.0 / math.sqrt(hd),
            hd=hd,
            group=group,
            blocks=blocks,
            keys=keys,
            padded=padded,
        ),
        out_shape=[jax.ShapeDtypeStruct((tokens, wide), BF16)] * blocks,
        grid_spec=pltpu.PrefetchScalarGridSpec(
            num_scalar_prefetch=3,
            grid=(),
            in_specs=[apart] * (blocks + 4),
            out_specs=[here] * blocks,
            scratch_shapes=[
                pltpu.VMEM((blocks * tokens, wide), BF16),
                pltpu.VMEM((4, hd, padded), BF16),
                pltpu.VMEM((4, hd, padded), BF16),
                pltpu.VMEM((4, padded, 2 * hd), BF16),
                pltpu.VMEM((rows, padded), F32),
                pltpu.VMEM((rows, padded), F32),
                pltpu.VMEM((rows, hd), F32),
                pltpu.VMEM((rows, hd), F32),
                pltpu.VMEM((blocks * tokens * group, hd), F32),
                pltpu.VMEM((blocks * tokens * group, 2 * hd), F32),
                pltpu.SemaphoreType.DMA((8 + blocks,)),
            ],
        ),
        compiler_params=pltpu.CompilerParams(vmem_limit_bytes=32 << 20),
        cost_estimate=pl.CostEstimate(
            flops=2 * blocks * tokens * group * padded * 2 * hd,
            bytes_accessed=blocks * tokens * width * 4 + padded * hd * 16,
            transcendentals=blocks * tokens * group * padded * 2,
        ),
        name="attend",
    )(items, count, images, *payloads, *tiles)


def prepare_kernel(
    counts, range_ref, key_hbm, value_hbm, q_hbm, tile_ref, payload_ref, back_ref, key_ref, value_ref, q_ref, sems
):
    copies = [
        pltpu.make_async_copy(key_hbm, key_ref, sems.at[0]),
        pltpu.make_async_copy(value_hbm, value_ref, sems.at[1]),
        pltpu.make_async_copy(q_hbm, q_ref, sems.at[2]),
    ]
    for copy in copies:
        copy.start()
    tokens, width = q_ref.shape
    keys, hd = key_ref.shape
    square = (tokens, tokens)
    down = lax.broadcasted_iota(jnp.int32, square, 0)
    along = lax.broadcasted_iota(jnp.int32, square, 1)
    rows = range_ref[...].astype(F32)
    low_row = jnp.broadcast_to(rows[0:1], square)
    high_row = jnp.broadcast_to(rows[1:2], square)
    same = down == along
    low = jnp.sum(jnp.where(same, low_row, 0.0), axis=1, keepdims=True)
    high = jnp.sum(jnp.where(same, high_row, 0.0), axis=1, keepdims=True)
    grade_row = jnp.where(low_row < high_row, low_row * 16 + high_row, 1024.0)
    grade = jnp.where(low < high, low * 16 + high, 1024.0)
    equal = grade == grade_row
    before = (grade < grade_row) | (equal & (down < along))
    after = (grade_row < grade) | (equal & (along < down))
    rank_row = jnp.sum(jnp.where(before, 1.0, 0.0), axis=0, keepdims=True)
    rank = jnp.sum(jnp.where(after, 1.0, 0.0), axis=1, keepdims=True)
    order = jnp.where(rank_row == down.astype(F32), 1.0, 0.0).astype(BF16)
    back_ref[...] = jnp.where(rank == along.astype(F32), 1.0, 0.0).astype(BF16)
    lane = lax.broadcasted_iota(jnp.int32, (tokens, hd), 1)
    owner = jnp.zeros((tokens, hd), F32)
    end = 0
    for i in range(counts.shape[0]):
        end = end + counts[i]
        owner = owner + jnp.where(lane - 16 >= end, 1.0, 0.0)
    hits = (low <= owner) & (owner < high) & (lane >= 16) & (lane < 32)
    extra = jnp.where(lane == 0, low, jnp.where(lane == 1, high, jnp.where(hits, 1.0, 0.0)))
    placed = jnp.dot(order, extra.astype(BF16), preferred_element_type=F32)
    group = jnp.where(down // CHUNK == along // CHUNK, 1.0, 0.0).astype(BF16)
    crowd = jnp.dot(group, placed.astype(BF16), preferred_element_type=F32)
    live = jnp.where(crowd > 0, 1.0, 0.0)
    payload_ref[:, width:] = jnp.where(lane < 2, placed, live).astype(BF16)
    for copy in copies:
        copy.wait()
    step = 2 * hd
    for k in range(0, width, step):
        part = jnp.dot(order, q_ref[:, k : k + step], preferred_element_type=F32)
        payload_ref[:, k : k + step] = part.astype(BF16)
    whole = keys // hd * hd
    mid = keys // 16 * 16
    padded = tile_ref.shape[1]
    for k in range(0, whole, hd):
        block = key_ref[k : k + hd].astype(F32)
        tile_ref[:hd, k : k + hd] = block.T.astype(BF16)
        tile_ref[hd:, k : k + hd] = value_ref[k : k + hd]
    first = lax.broadcasted_iota(jnp.int32, (padded - mid, hd), 0) == 0
    last_key = jnp.where(first, key_ref[mid:keys].astype(F32), key_ref[0:1].astype(F32))
    last_value = jnp.where(first, value_ref[mid:keys].astype(F32), 0.0)
    block = jnp.concatenate([key_ref[whole:mid].astype(F32), last_key], axis=0)
    tile_ref[:hd, whole:] = block.T.astype(BF16)
    block = jnp.concatenate([value_ref[whole:mid].astype(F32), last_value], axis=0)
    tile_ref[hd:, whole:] = block.astype(BF16)


def prepare(counts, image_range, keys, values, queries, padded):
    hd = keys.shape[1]
    tokens, width = queries.shape
    apart = pl.BlockSpec(memory_space=pl.ANY)
    here = pl.BlockSpec(memory_space=pltpu.VMEM)
    return pl.pallas_call(
        prepare_kernel,
        out_shape=[
            jax.ShapeDtypeStruct((2 * hd, padded), BF16),
            jax.ShapeDtypeStruct((tokens, width + hd), BF16),
            jax.ShapeDtypeStruct((tokens, tokens), BF16),
        ],
        in_specs=[pl.BlockSpec(memory_space=pltpu.SMEM), here] + [apart] * 3,
        out_specs=[here] * 3,
        scratch_shapes=[
            pltpu.VMEM(keys.shape, BF16),
            pltpu.VMEM(values.shape, BF16),
            pltpu.VMEM(queries.shape, BF16),
            pltpu.SemaphoreType.DMA((3,)),
        ],
        compiler_params=pltpu.CompilerParams(vmem_limit_bytes=60 << 20),
        name="prepare",
    )(counts, image_range, keys, values, queries)


def work_list(wanted):
    tiles = wanted.shape[-1]
    flags = wanted.reshape(-1) > 0
    size = flags.shape[0]
    place = jnp.arange(size, dtype=jnp.int32)
    rank = jnp.sum((place[None, :] < place[:, None]) & flags[None, :], axis=1)
    count = jnp.sum(flags.astype(jnp.int32))
    code = place // tiles * 8 + place % tiles + 1
    slot = jnp.arange(size + 3, dtype=jnp.int32)
    chosen = (rank[None, :] == slot[:, None]) & flags[None, :]
    items = jnp.sum(jnp.where(chosen, code[None, :], 0), axis=1)
    items = jnp.where(items > 0, items - 1, 4)
    return items.astype(jnp.int32), count.reshape(1)


def combined(back_ref, parts, out_ref, hd, group):
    width = group * hd
    sums = []
    for ref in parts:
        pieces = ref[:, width:].astype(F32)
        sums.append(pieces[:, :group] + pieces[:, group : 2 * group] + pieces[:, 2 * group : 3 * group])
    top = jnp.maximum(jnp.maximum(sums[0], sums[1]), jnp.maximum(sums[2], sums[3]))
    shares = [jnp.exp(s - top) for s in sums]
    total = shares[0] + shares[1] + shares[2] + shares[3]
    shares = [s / total for s in shares]
    for h in range(group):
        at = slice(h * hd, (h + 1) * hd)
        mixed = parts[0][:, at].astype(F32) * shares[0][:, h : h + 1]
        for ref, share in zip(parts[1:], shares[1:]):
            mixed = mixed + ref[:, at].astype(F32) * share[:, h : h + 1]
        out_ref[:, at] = mixed.astype(BF16)
    placed = jnp.dot(back_ref[...], out_ref[...], preferred_element_type=F32)
    out_ref[...] = placed.astype(BF16)


def project_kernel(columns, *refs, hd, group, pieces, merge):
    sources = refs[: 5 if merge else 1]
    w_ref = refs[len(sources)]
    outs = refs[len(sources) + 1 : len(sources) + 1 + len(pieces)]
    held, sems = refs[-2:]
    copies = []
    for count, width in pieces:
        for _ in range(count):
            i = len(copies)
            start = pl.multiple_of(columns[i] * hd, hd)
            copies.append(
                pltpu.make_async_copy(
                    w_ref.at[:, pl.ds(start, width)], held.at[i, :, pl.ds(0, width)], sems.at[i]
                )
            )
            copies[-1].start()
    if merge:
        attended = refs[len(sources) + 1 + len(pieces)]
        combined(sources[0], sources[1:], attended, hd, group)
    else:
        attended = sources[0]
    i = 0
    for out_ref, (count, width) in zip(outs, pieces):
        for c in range(count):
            copies[i].wait()
            term = jnp.dot(attended[...], held[i, :, :width], preferred_element_type=F32)
            out_ref[:, c * width : (c + 1) * width] = term.astype(BF16)
            i += 1


def project(sources, weight, columns, pieces, hd):
    merge = len(sources) > 1
    tokens = sources[-1].shape[0]
    depth = weight.shape[0]
    total = sum(count for count, _ in pieces)
    widest = max(width for _, width in pieces)
    area = sum(count * width for count, width in pieces)
    here = pl.BlockSpec(memory_space=pltpu.VMEM)
    results = [jax.ShapeDtypeStruct((tokens, width * count), BF16) for count, width in pieces]
    if merge:
        results.append(jax.ShapeDtypeStruct((tokens, depth), BF16))
    return pl.pallas_call(
        lambda *refs: project_kernel(*refs, hd=hd, group=depth // hd, pieces=pieces, merge=merge),
        out_shape=results,
        grid_spec=pltpu.PrefetchScalarGridSpec(
            num_scalar_prefetch=1,
            grid=(),
            in_specs=[here] * len(sources) + [pl.BlockSpec(memory_space=pl.ANY)],
            out_specs=[here] * len(results),
            scratch_shapes=[
                pltpu.VMEM((total, depth, widest), BF16),
                pltpu.SemaphoreType.DMA((total,)),
            ],
        ),
        cost_estimate=pl.CostEstimate(
            flops=2 * tokens * depth * area, bytes_accessed=4 * depth * area, transcendentals=0
        ),
        compiler_params=pltpu.CompilerParams(vmem_limit_bytes=50 << 20),
        name="project",
    )(jnp.stack(columns).astype(jnp.int32), *sources, weight)


def add_kernel(*refs, count):
    parts, send_ref, keep_ref = refs[:count], refs[-2], refs[-1]
    total = parts[0][...].astype(F32)
    for ref in parts[1:]:
        total = total + ref[...].astype(F32)
    cut = send_ref.shape[1]
    send_ref[...] = total[:, :cut].astype(BF16)
    keep_ref[...] = total[:, cut:]


def add_up(parts, keep):
    tokens, width = parts[0].shape
    return pl.pallas_call(
        lambda *refs: add_kernel(*refs, count=len(parts)),
        out_shape=[
            jax.ShapeDtypeStruct((tokens, width - keep), BF16),
            jax.ShapeDtypeStruct((tokens, keep), F32),
        ],
        compiler_params=pltpu.CompilerParams(vmem_limit_bytes=24 << 20),
        name="add_up",
    )(*parts)


def settle_kernel(gate_ref, layer_ref, *refs):
    parts, out_ref = refs[:-1], refs[-1]
    cut = parts[0].shape[1]
    for at, some in ((slice(0, cut), parts[:2]), (slice(cut, None), parts[2:])):
        total = some[0][...]
        for ref in some[1:]:
            total = total + ref[...].astype(F32)
        out_ref[:, at] = (layer_ref[:, at].astype(F32) + gate_ref[0] * total).astype(BF16)


def settle(gate, layer, parts):
    tokens, width = layer.shape
    cuts = 2
    rows = tokens // cuts
    wide = pl.BlockSpec((rows, width), lambda g: (g, 0))
    each = [pl.BlockSpec((rows, part.shape[1]), lambda g: (g, 0)) for part in parts]
    return pl.pallas_call(
        settle_kernel,
        out_shape=jax.ShapeDtypeStruct((tokens, width), BF16),
        grid=(cuts,),
        in_specs=[pl.BlockSpec(memory_space=pltpu.SMEM), wide] + each,
        out_specs=wide,
        compiler_params=pltpu.CompilerParams(vmem_limit_bytes=24 << 20),
        name="settle",
    )(gate, layer, *parts)


def shards(
    queries, image_keys, image_values, layer_input, out_weight, tile_counts, image_range, attn_gate
):
    tokens, width = queries.shape
    keys, hd = image_keys.shape
    y, x, core = (lax.axis_index(n) for n in SEQ)
    z, yh = (lax.axis_index(n) for n in HEAD)
    ny, nx, nc = (lax.axis_size(n) for n in SEQ)
    nz, nyh = (lax.axis_size(n) for n in HEAD)

    padded = -(-keys // 128) * 128
    own, payload, back = prepare(
        tile_counts, image_range, image_keys, image_values, queries, padded
    )
    across = shifted(own, "y", 1)
    image = jnp.arange(tile_counts.shape[0])
    ends = jnp.sum(jnp.where(image[None, :] <= image[:, None], tile_counts[None, :], 0), axis=1)
    tile = jnp.arange(ny * nx * nc, dtype=jnp.int32)
    owner = jnp.sum((ends[None, :] <= tile[:, None]).astype(jnp.int32), axis=1)
    payloads = {s: shifted(payload, "x", s) for s in (2, 1, 3)}
    payloads[0] = payload
    beside = shifted(own, "core", 1)
    diagonal = shifted(across, "core", 1)
    tiles = (own, beside, across, diagonal)

    def number(yy, cc):
        return (yy % ny * nx + x) * nc + cc % nc

    held = jnp.stack([number(y, core), number(y, core + 1), number(y + 1, core), number(y + 1, core + 1)])
    mine = (held[:, None] == tile[None, :]).astype(jnp.int32)
    images = jnp.sum(mine * owner[None, :], axis=1)

    parts = {}
    for turns in GROUPS:
        if parts:
            images = lax.optimization_barrier((images, *parts.values()))[0]
        flags = jnp.concatenate([payloads[s][::CHUNK, width + 16 : width + 32] for s in turns], axis=0)
        wanted = jnp.sum(flags.astype(jnp.int32)[:, None, :] * mine[None, :, :], axis=2)
        items, count = work_list(wanted)
        got = attend(
            [payloads[s] for s in turns],
            items,
            count,
            images,
            tiles,
            keys,
            tokens,
            hd,
        )
        parts.update(zip(turns, got))
    parts = {s: part if s == 0 else shifted(part, "x", nx - s) for s, part in parts.items()}

    some, rest = width * 3 // 8, width * 5 // 8

    def first(dz, dy):
        return ((z + dz) % nz * nyh + (yh + dy) % nyh) * (width // hd)

    def second(dz, dy):
        return first(dz, dy) + some // hd

    sources = [back] + [parts[s] for s in (2, 1, 3, 0)]
    over_y, attended = project(
        sources, out_weight, [second(dz, 1) for dz in (1, 2, 3, 0)], ((4, rest),), hd
    )
    got_y = shifted(over_y, "yh", 1)
    far = [first(dz, dy) for dz in (2, 1, 3) for dy in (1, 0)]
    over_z = project([attended], out_weight, far, ((2, some),) * 3, hd)
    got_z = [shifted(term, "z", dz) for dz, term in zip((2, 1, 3), over_z)]
    near = [first(0, 1), first(0, 0)] + [second(dz, 0) for dz in (1, 2, 3, 0)]
    own_z, own_y = project([attended], out_weight, near, ((2, some), (4, rest)), hd)
    late_z, kept_b = add_up([own_y, got_y], rest)
    ends_b = [shifted(late_z[:, i * rest : (i + 1) * rest], "z", i + 1) for i in (1, 0, 2)]
    late_y, kept_a = add_up([own_z] + got_z[::-1], some)
    end_a = shifted(late_y, "yh", 1)
    return settle(jnp.tanh(attn_gate), layer_input, [kept_a, end_a, kept_b] + ends_b)


def solution(mesh):
    split = Mesh(mesh.devices.reshape(2, 4, 2, 4, 2), ("y", "x", "core", "z", "yh"))
    return jax.shard_map(
        shards,
        mesh=split,
        in_specs=(
            P(SEQ, HEAD),
            P(SEQ, HEAD),
            P(SEQ, HEAD),
            P(SEQ, HEAD),
            P(HEAD, None),
            P(),
            P(None, SEQ),
            P(),
        ),
        out_specs=P(SEQ, HEAD),
        check_vma=False,
    )
```

```python
import math

import jax
import jax.numpy as jnp
from jax import lax
from jax.experimental import pallas as pl
from jax.experimental.pallas import tpu as pltpu
from jax.sharding import Mesh
from jax.sharding import PartitionSpec as P

SEQ = ("y", "x", "core")
HEAD = ("z", "yh")
CHUNK = 32
GROUPS = ((2,), (1, 3), (0,))
LOWEST = -1e30
BLOCKED = 1e30
BF16 = jnp.bfloat16
F32 = jnp.float32


def shifted(value, axis, steps):
    count = lax.axis_size(axis)
    return lax.ppermute(value, axis, [(s, (s + steps) % count) for s in range(count)])


def head_shifted(value, dz, dy):
    nz, ny = lax.axis_size("z"), lax.axis_size("yh")
    pairs = []
    for z in range(nz):
        for y in range(ny):
            pairs.append((z * ny + y, (z + dz) % nz * ny + (y + dy) % ny))
    return lax.ppermute(value, HEAD, pairs)


def attend_kernel(items, count, images, *refs, scale, hd, group, blocks, keys, padded):
    q_refs = refs[:blocks]
    tile_refs = refs[blocks : blocks + 4]
    out_refs = refs[blocks + 4 : 2 * blocks + 4]
    q_all, key_all, value_in, value_all, first_s, second_s, first_b, second_b, top_ref, acc_ref, sems = refs[
        2 * blocks + 4 :
    ]
    tokens = out_refs[0].shape[0]
    rows = CHUNK * group
    width = group * hd
    factor = scale * math.log2(math.e)
    copies = []
    for j in range(4):
        copies.append(
            pltpu.make_async_copy(tile_refs[j].at[pl.ds(0, hd)], key_all.at[j], sems.at[2 * j])
        )
    for j in range(4):
        copies.append(
            pltpu.make_async_copy(tile_refs[j].at[pl.ds(hd, hd)], value_in.at[j], sems.at[2 * j + 1])
        )
    for i in range(blocks):
        copies.append(
            pltpu.make_async_copy(
                q_refs[i], q_all.at[pl.ds(i * tokens, tokens)], sems.at[8 + i]
            )
        )
    for copy in copies:
        copy.start()
    place = lax.broadcasted_iota(jnp.int32, (padded, hd), 0)
    ones = jnp.where(place < keys, 1.0, 0.0).astype(BF16)
    for j in range(4):
        value_all[j, :, hd:] = ones
    top_ref[...] = jnp.full(top_ref.shape, LOWEST, F32)
    acc_ref[...] = jnp.zeros(acc_ref.shape, F32)
    for copy in copies[:4] + copies[8:]:
        copy.wait()

    def where_is(i):
        item = items[i]
        return item // 8, item % 4, jnp.where(item % 8 < 4, images[item % 4], -1)

    def score(i, scores_ref, best_ref):
        chunk, j, _ = where_is(i)
        at = pl.ds(pl.multiple_of(chunk * CHUNK, CHUNK), CHUNK)
        q = jnp.concatenate([q_all[at, h * hd : (h + 1) * hd] for h in range(group)], axis=0)
        best = None
        for k in range(0, padded, 128):
            part = jnp.dot(q, key_all[j, :, k : k + 128], preferred_element_type=F32)
            scores_ref[:, k : k + 128] = part
            best = part if best is None else jnp.maximum(best, part)
        best_ref[...] = jnp.broadcast_to(jnp.max(best, axis=1, keepdims=True), best_ref.shape)

    def absorb(i, scores_ref, best_ref):
        chunk, j, image = where_is(i)
        at = pl.ds(pl.multiple_of(chunk * rows, rows), rows)
        near = pl.ds(pl.multiple_of(chunk * CHUNK, CHUNK), CHUNK)
        reach = q_all[near, width : width + hd].astype(F32)
        low = jnp.concatenate([reach[:, 0:1]] * group, axis=0)
        high = jnp.concatenate([reach[:, 1:2]] * group, axis=0)
        number = image.astype(F32)
        allowed = (low <= number) & (number < high)
        old = top_ref[at, 0:1]
        new = jnp.where(allowed, jnp.maximum(old, best_ref[:, 0:1]), old)
        anchor = jnp.where(allowed, new, BLOCKED)
        rescale = jnp.exp2((old - new) * factor)
        top_ref[at, :] = jnp.broadcast_to(new, (rows, hd))
        weights = jnp.exp2((scores_ref[...] - anchor) * factor).astype(BF16)
        mixed = jnp.dot(weights, value_all[j], preferred_element_type=F32)
        acc_ref[at, :] = acc_ref[at, :] * rescale + mixed

    def pair(k, carry):
        i = 2 * k
        score(i + 1, second_s, second_b)
        absorb(i, first_s, first_b)
        score(i + 2, first_s, first_b)
        absorb(i + 1, second_s, second_b)
        return carry

    score(0, first_s, first_b)
    for copy in copies[4:8]:
        copy.wait()
    for j in range(4):
        for k in range(0, padded, hd):
            value_all[j, k : k + hd, :hd] = value_in[j, :, k : k + hd]
    lax.fori_loop(0, (count[0] + 1) // 2, pair, 0)

    lane = lax.broadcasted_iota(jnp.int32, (CHUNK, hd), 1)
    for c in range(blocks * tokens // CHUNK):
        out_ref = out_refs[c * CHUNK // tokens]
        near = pl.ds(c * CHUNK % tokens, CHUNK)
        totals = jnp.zeros((CHUNK, hd), F32)
        tops = jnp.zeros((CHUNK, hd), F32)
        for h in range(group):
            at = pl.ds(c * rows + h * CHUNK, CHUNK)
            total = acc_ref[at, hd:]
            safe = jnp.where(total > 0, total, 1.0)
            out_ref[near, h * hd : (h + 1) * hd] = (acc_ref[at, :hd] / safe).astype(BF16)
            totals = jnp.where(lane % group == h, total, totals)
            tops = jnp.where(lane % group == h, top_ref[at, :], tops)
        seen = totals > 0
        logsum = jnp.where(seen, tops * scale + jnp.log(jnp.where(seen, totals, 1.0)), LOWEST)
        hi = logsum.astype(BF16).astype(F32)
        mid = (logsum - hi).astype(BF16).astype(F32)
        lo = logsum - hi - mid
        pieces = jnp.where(lane < group, hi, jnp.where(lane < 2 * group, mid, lo))
        out_ref[near, width:] = pieces.astype(BF16)


def attend(payloads, items, count, images, tiles, keys, tokens, hd):
    blocks = len(payloads)
    wide = payloads[0].shape[1]
    padded = tiles[0].shape[1]
    width = wide - hd
    group = width // hd
    rows = CHUNK * group
    apart = pl.BlockSpec(memory_space=pl.ANY)
    here = pl.BlockSpec(memory_space=pltpu.VMEM)
    return pl.pallas_call(
        lambda *refs: attend_kernel(
            *refs,
            scale=1.0 / math.sqrt(hd),
            hd=hd,
            group=group,
            blocks=blocks,
            keys=keys,
            padded=padded,
        ),
        out_shape=[jax.ShapeDtypeStruct((tokens, wide), BF16)] * blocks,
        grid_spec=pltpu.PrefetchScalarGridSpec(
            num_scalar_prefetch=3,
            grid=(),
            in_specs=[apart] * (blocks + 4),
            out_specs=[here] * blocks,
            scratch_shapes=[
                pltpu.VMEM((blocks * tokens, wide), BF16),
                pltpu.VMEM((4, hd, padded), BF16),
                pltpu.VMEM((4, hd, padded), BF16),
                pltpu.VMEM((4, padded, 2 * hd), BF16),
                pltpu.VMEM((rows, padded), F32),
                pltpu.VMEM((rows, padded), F32),
                pltpu.VMEM((rows, hd), F32),
                pltpu.VMEM((rows, hd), F32),
                pltpu.VMEM((blocks * tokens * group, hd), F32),
                pltpu.VMEM((blocks * tokens * group, 2 * hd), F32),
                pltpu.SemaphoreType.DMA((8 + blocks,)),
            ],
        ),
        compiler_params=pltpu.CompilerParams(vmem_limit_bytes=32 << 20),
        cost_estimate=pl.CostEstimate(
            flops=2 * blocks * tokens * group * padded * 2 * hd,
            bytes_accessed=blocks * tokens * width * 4 + padded * hd * 16,
            transcendentals=blocks * tokens * group * padded * 2,
        ),
        name="attend",
    )(items, count, images, *payloads, *tiles)


def prepare_kernel(
    counts, range_ref, key_hbm, value_hbm, q_hbm, tile_ref, payload_ref, back_ref, key_ref, value_ref, q_ref, sems
):
    copies = [
        pltpu.make_async_copy(key_hbm, key_ref, sems.at[0]),
        pltpu.make_async_copy(value_hbm, value_ref, sems.at[1]),
        pltpu.make_async_copy(q_hbm, q_ref, sems.at[2]),
    ]
    for copy in copies:
        copy.start()
    tokens, width = q_ref.shape
    keys, hd = key_ref.shape
    square = (tokens, tokens)
    down = lax.broadcasted_iota(jnp.int32, square, 0)
    along = lax.broadcasted_iota(jnp.int32, square, 1)
    rows = range_ref[...].astype(F32)
    low_row = jnp.broadcast_to(rows[0:1], square)
    high_row = jnp.broadcast_to(rows[1:2], square)
    same = down == along
    low = jnp.sum(jnp.where(same, low_row, 0.0), axis=1, keepdims=True)
    high = jnp.sum(jnp.where(same, high_row, 0.0), axis=1, keepdims=True)
    grade_row = jnp.where(low_row < high_row, low_row * 16 + high_row, 1024.0)
    grade = jnp.where(low < high, low * 16 + high, 1024.0)
    equal = grade == grade_row
    before = (grade < grade_row) | (equal & (down < along))
    after = (grade_row < grade) | (equal & (along < down))
    rank_row = jnp.sum(jnp.where(before, 1.0, 0.0), axis=0, keepdims=True)
    rank = jnp.sum(jnp.where(after, 1.0, 0.0), axis=1, keepdims=True)
    order = jnp.where(rank_row == down.astype(F32), 1.0, 0.0).astype(BF16)
    back_ref[...] = jnp.where(rank == along.astype(F32), 1.0, 0.0).astype(BF16)
    lane = lax.broadcasted_iota(jnp.int32, (tokens, hd), 1)
    owner = jnp.zeros((tokens, hd), F32)
    end = 0
    for i in range(counts.shape[0]):
        end = end + counts[i]
        owner = owner + jnp.where(lane - 16 >= end, 1.0, 0.0)
    hits = (low <= owner) & (owner < high) & (lane >= 16) & (lane < 32)
    extra = jnp.where(lane == 0, low, jnp.where(lane == 1, high, jnp.where(hits, 1.0, 0.0)))
    placed = jnp.dot(order, extra.astype(BF16), preferred_element_type=F32)
    group = jnp.where(down // CHUNK == along // CHUNK, 1.0, 0.0).astype(BF16)
    crowd = jnp.dot(group, placed.astype(BF16), preferred_element_type=F32)
    live = jnp.where(crowd > 0, 1.0, 0.0)
    payload_ref[:, width:] = jnp.where(lane < 2, placed, live).astype(BF16)
    for copy in copies:
        copy.wait()
    step = 2 * hd
    for k in range(0, width, step):
        part = jnp.dot(order, q_ref[:, k : k + step], preferred_element_type=F32)
        payload_ref[:, k : k + step] = part.astype(BF16)
    whole = keys // hd * hd
    mid = keys // 16 * 16
    padded = tile_ref.shape[1]
    for k in range(0, whole, hd):
        block = key_ref[k : k + hd].astype(F32)
        tile_ref[:hd, k : k + hd] = block.T.astype(BF16)
        tile_ref[hd:, k : k + hd] = value_ref[k : k + hd]
    first = lax.broadcasted_iota(jnp.int32, (padded - mid, hd), 0) == 0
    last_key = jnp.where(first, key_ref[mid:keys].astype(F32), key_ref[0:1].astype(F32))
    last_value = jnp.where(first, value_ref[mid:keys].astype(F32), 0.0)
    block = jnp.concatenate([key_ref[whole:mid].astype(F32), last_key], axis=0)
    tile_ref[:hd, whole:] = block.T.astype(BF16)
    block = jnp.concatenate([value_ref[whole:mid].astype(F32), last_value], axis=0)
    tile_ref[hd:, whole:] = block.astype(BF16)


def prepare(counts, image_range, keys, values, queries, padded):
    hd = keys.shape[1]
    tokens, width = queries.shape
    apart = pl.BlockSpec(memory_space=pl.ANY)
    here = pl.BlockSpec(memory_space=pltpu.VMEM)
    return pl.pallas_call(
        prepare_kernel,
        out_shape=[
            jax.ShapeDtypeStruct((2 * hd, padded), BF16),
            jax.ShapeDtypeStruct((tokens, width + hd), BF16),
            jax.ShapeDtypeStruct((tokens, tokens), BF16),
        ],
        in_specs=[pl.BlockSpec(memory_space=pltpu.SMEM), here] + [apart] * 3,
        out_specs=[here] * 3,
        scratch_shapes=[
            pltpu.VMEM(keys.shape, BF16),
            pltpu.VMEM(values.shape, BF16),
            pltpu.VMEM(queries.shape, BF16),
            pltpu.SemaphoreType.DMA((3,)),
        ],
        compiler_params=pltpu.CompilerParams(vmem_limit_bytes=60 << 20),
        name="prepare",
    )(counts, image_range, keys, values, queries)


def work_list(wanted):
    tiles = wanted.shape[-1]
    flags = wanted.reshape(-1) > 0
    size = flags.shape[0]
    place = jnp.arange(size, dtype=jnp.int32)
    rank = jnp.sum((place[None, :] < place[:, None]) & flags[None, :], axis=1)
    count = jnp.sum(flags.astype(jnp.int32))
    code = place // tiles * 8 + place % tiles + 1
    slot = jnp.arange(size + 3, dtype=jnp.int32)
    chosen = (rank[None, :] == slot[:, None]) & flags[None, :]
    items = jnp.sum(jnp.where(chosen, code[None, :], 0), axis=1)
    items = jnp.where(items > 0, items - 1, 4)
    return items.astype(jnp.int32), count.reshape(1)


def combined(back_ref, parts, out_ref, hd, group):
    width = group * hd
    sums = []
    for ref in parts:
        pieces = ref[:, width:].astype(F32)
        sums.append(pieces[:, :group] + pieces[:, group : 2 * group] + pieces[:, 2 * group : 3 * group])
    top = jnp.maximum(jnp.maximum(sums[0], sums[1]), jnp.maximum(sums[2], sums[3]))
    shares = [jnp.exp(s - top) for s in sums]
    total = shares[0] + shares[1] + shares[2] + shares[3]
    shares = [s / total for s in shares]
    for h in range(group):
        at = slice(h * hd, (h + 1) * hd)
        mixed = parts[0][:, at].astype(F32) * shares[0][:, h : h + 1]
        for ref, share in zip(parts[1:], shares[1:]):
            mixed = mixed + ref[:, at].astype(F32) * share[:, h : h + 1]
        out_ref[:, at] = mixed.astype(BF16)
    placed = jnp.dot(back_ref[...], out_ref[...], preferred_element_type=F32)
    out_ref[...] = placed.astype(BF16)


def project_kernel(columns, *refs, hd, group, pieces, merge):
    sources = refs[: 5 if merge else 1]
    w_ref = refs[len(sources)]
    outs = refs[len(sources) + 1 : len(sources) + 1 + len(pieces)]
    if merge:
        held, sems, local, arrivals = refs[-4:]
        loads = [pltpu.make_async_copy(sources[1 + i], local.at[i], arrivals.at[i]) for i in range(4)]
        for load in loads:
            load.start()
    else:
        held, sems = refs[-2:]
    copies = []
    for count, width in pieces:
        for _ in range(count):
            i = len(copies)
            start = pl.multiple_of(columns[i] * hd, hd)
            copies.append(
                pltpu.make_async_copy(
                    w_ref.at[:, pl.ds(start, width)], held.at[i, :, pl.ds(0, width)], sems.at[i]
                )
            )
            copies[-1].start()
    if merge:
        attended = refs[len(sources) + 1 + len(pieces)]
        for load in loads:
            load.wait()
        combined(sources[0], [local.at[i] for i in range(4)], attended, hd, group)
    else:
        attended = sources[0]
    i = 0
    for out_ref, (count, width) in zip(outs, pieces):
        for c in range(count):
            copies[i].wait()
            term = jnp.dot(attended[...], held[i, :, :width], preferred_element_type=F32)
            out_ref[:, c * width : (c + 1) * width] = term.astype(BF16)
            i += 1


def project(sources, weight, columns, pieces, hd):
    merge = len(sources) > 1
    tokens = sources[-1].shape[0]
    depth = weight.shape[0]
    total = sum(count for count, _ in pieces)
    widest = max(width for _, width in pieces)
    area = sum(count * width for count, width in pieces)
    here = pl.BlockSpec(memory_space=pltpu.VMEM)
    results = [jax.ShapeDtypeStruct((tokens, width * count), BF16) for count, width in pieces]
    if merge:
        results.append(jax.ShapeDtypeStruct((tokens, depth), BF16))
    return pl.pallas_call(
        lambda *refs: project_kernel(*refs, hd=hd, group=depth // hd, pieces=pieces, merge=merge),
        out_shape=results,
        grid_spec=pltpu.PrefetchScalarGridSpec(
            num_scalar_prefetch=1,
            grid=(),
            in_specs=[here] + [pl.BlockSpec(memory_space=pl.ANY)] * len(sources),
            out_specs=[here] * len(results),
            scratch_shapes=[
                pltpu.VMEM((total, depth, widest), BF16),
                pltpu.SemaphoreType.DMA((total,)),
            ]
            + [pltpu.VMEM((4,) + sources[-1].shape, BF16), pltpu.SemaphoreType.DMA((4,))] * merge,
        ),
        cost_estimate=pl.CostEstimate(
            flops=2 * tokens * depth * area, bytes_accessed=4 * depth * area, transcendentals=0
        ),
        compiler_params=pltpu.CompilerParams(vmem_limit_bytes=50 << 20),
        name="project",
    )(jnp.stack(columns).astype(jnp.int32), *sources, weight)


def add_kernel(*refs, count):
    parts, send_ref, keep_ref = refs[:count], refs[-2], refs[-1]
    total = parts[0][...].astype(F32)
    for ref in parts[1:]:
        total = total + ref[...].astype(F32)
    cut = send_ref.shape[1]
    send_ref[...] = total[:, :cut].astype(BF16)
    keep_ref[...] = total[:, cut:]


def add_up(parts, keep):
    tokens, width = parts[0].shape
    return pl.pallas_call(
        lambda *refs: add_kernel(*refs, count=len(parts)),
        out_shape=[
            jax.ShapeDtypeStruct((tokens, width - keep), BF16),
            jax.ShapeDtypeStruct((tokens, keep), F32),
        ],
        compiler_params=pltpu.CompilerParams(vmem_limit_bytes=24 << 20),
        name="add_up",
    )(*parts)


def settle_kernel(gate_ref, layer_ref, *refs):
    parts, out_ref = refs[:-1], refs[-1]
    cut = parts[0].shape[1]
    for at, some in ((slice(0, cut), parts[:2]), (slice(cut, None), parts[2:])):
        total = some[0][...]
        for ref in some[1:]:
            total = total + ref[...].astype(F32)
        out_ref[:, at] = (layer_ref[:, at].astype(F32) + gate_ref[0] * total).astype(BF16)


def settle(gate, layer, parts):
    tokens, width = layer.shape
    cuts = 2
    rows = tokens // cuts
    wide = pl.BlockSpec((rows, width), lambda g: (g, 0))
    each = [pl.BlockSpec((rows, part.shape[1]), lambda g: (g, 0)) for part in parts]
    return pl.pallas_call(
        settle_kernel,
        out_shape=jax.ShapeDtypeStruct((tokens, width), BF16),
        grid=(cuts,),
        in_specs=[pl.BlockSpec(memory_space=pltpu.SMEM), wide] + each,
        out_specs=wide,
        compiler_params=pltpu.CompilerParams(vmem_limit_bytes=24 << 20),
        name="settle",
    )(gate, layer, *parts)


def shards(
    queries, image_keys, image_values, layer_input, out_weight, tile_counts, image_range, attn_gate
):
    tokens, width = queries.shape
    keys, hd = image_keys.shape
    y, x, core = (lax.axis_index(n) for n in SEQ)
    z, yh = (lax.axis_index(n) for n in HEAD)
    ny, nx, nc = (lax.axis_size(n) for n in SEQ)
    nz, nyh = (lax.axis_size(n) for n in HEAD)

    padded = -(-keys // 128) * 128
    own, payload, back = prepare(
        tile_counts, image_range, image_keys, image_values, queries, padded
    )
    across = shifted(own, "y", 1)
    image = jnp.arange(tile_counts.shape[0])
    ends = jnp.sum(jnp.where(image[None, :] <= image[:, None], tile_counts[None, :], 0), axis=1)
    tile = jnp.arange(ny * nx * nc, dtype=jnp.int32)
    owner = jnp.sum((ends[None, :] <= tile[:, None]).astype(jnp.int32), axis=1)
    payloads = {s: shifted(payload, "x", s) for s in (2, 1, 3)}
    payloads[0] = payload
    beside = shifted(own, "core", 1)
    diagonal = shifted(across, "core", 1)
    tiles = (own, beside, across, diagonal)

    def number(yy, cc):
        return (yy % ny * nx + x) * nc + cc % nc

    held = jnp.stack([number(y, core), number(y, core + 1), number(y + 1, core), number(y + 1, core + 1)])
    mine = (held[:, None] == tile[None, :]).astype(jnp.int32)
    images = jnp.sum(mine * owner[None, :], axis=1)

    parts = {}
    for turns in GROUPS:
        if parts:
            images = lax.optimization_barrier((images, *parts.values()))[0]
        flags = jnp.concatenate([payloads[s][::CHUNK, width + 16 : width + 32] for s in turns], axis=0)
        wanted = jnp.sum(flags.astype(jnp.int32)[:, None, :] * mine[None, :, :], axis=2)
        items, count = work_list(wanted)
        got = attend(
            [payloads[s] for s in turns],
            items,
            count,
            images,
            tiles,
            keys,
            tokens,
            hd,
        )
        parts.update(zip(turns, got))
    parts = {s: part if s == 0 else shifted(part, "x", nx - s) for s, part in parts.items()}

    some, rest = width * 3 // 8, width * 5 // 8

    def first(dz, dy):
        return ((z + dz) % nz * nyh + (yh + dy) % nyh) * (width // hd)

    def second(dz, dy):
        return first(dz, dy) + some // hd

    sources = [back] + [parts[s] for s in (2, 1, 3, 0)]
    over_y, attended = project(
        sources, out_weight, [second(dz, 1) for dz in (1, 2, 3, 0)], ((4, rest),), hd
    )
    got_y = shifted(over_y, "yh", 1)
    far = [first(dz, dy) for dz in (2, 1, 3) for dy in (1, 0)]
    over_z = project([attended], out_weight, far, ((2, some),) * 3, hd)
    got_z = [shifted(term, "z", dz) for dz, term in zip((2, 1, 3), over_z)]
    near = [first(0, 1), first(0, 0)] + [second(dz, 0) for dz in (1, 2, 3, 0)]
    own_z, own_y = project([attended], out_weight, near, ((2, some), (4, rest)), hd)
    late_z, kept_b = add_up([own_y, got_y], rest)
    ends_b = [shifted(late_z[:, i * rest : (i + 1) * rest], "z", i + 1) for i in (1, 0, 2)]
    late_y, kept_a = add_up([own_z] + got_z[::-1], some)
    end_a = shifted(late_y, "yh", 1)
    return settle(jnp.tanh(attn_gate), layer_input, [kept_a, end_a, kept_b] + ends_b)


def solution(mesh):
    split = Mesh(mesh.devices.reshape(2, 4, 2, 4, 2), ("y", "x", "core", "z", "yh"))
    return jax.shard_map(
        shards,
        mesh=split,
        in_specs=(
            P(SEQ, HEAD),
            P(SEQ, HEAD),
            P(SEQ, HEAD),
            P(SEQ, HEAD),
            P(HEAD, None),
            P(),
            P(None, SEQ),
            P(),
        ),
        out_specs=P(SEQ, HEAD),
        check_vma=False,
    )
```
